32 devices in a mesh: gx: 4 (over y, x), gy: 8 (over z, core).
Axes of the slice: x: 2, y: 2, z: 4, core: 2. Of those that a mesh axis runs over, the one named last changes fastest.
Arguments:
- forcing: float32 [3, 64, 128, 128], P(None, 'gx', 'gy'), may hold values from -6 to 6
- phase_index: int32 [64, 128, 128], P('gx', 'gy'), may hold values from 0 to 7
- visc_table: float32 [8], replicated, may hold values from 0.001 to 1000
- lower_bound: float32 [1], replicated, may hold values from 0.1 to 0.4
- upper_bound: float32 [1], replicated, may hold values from 1.9 to 2.3
Outputs:
- residual: float32 [3, 64, 128, 128], P(None, 'gx', 'gy')
The draws below stay inside these ranges and needn't reach their ends.
Inputs may be any that keep to these rules, and one draw needn't show every extreme that they name: `phase_index`: each entry names a row of visc_table.
All inputs are finite; a program needn't handle non-finite values.
Results may differ from the reference program's by a relative error of at most 0.000027.
Values sent between devices are 32-bit elements; how exact they have to be, the bound alone decides.
No kernel may reach another device: no remote copies, remote signals or barrier semaphores. Data moves between devices by JAX's collectives and lax.ppermute only.
A program may use at most 128 MiB of HBM per device.

```python
import math
import jax
import jax.numpy as jnp
from jax import lax

NZ = 128
COMP = 3
PHASES = 8
CHEB = 4
COARSE_STEPS = 4
NX = 64
NY = 128


def with_ends(values, key, smallest, top_value):
    spot = [jax.random.randint(jax.random.fold_in(key, axis), (), 0, length) for axis, length in enumerate(values.shape)]
    longest = values.shape.index(max(values.shape))
    beside = spot[:longest] + [(spot[longest] + 1) % values.shape[longest]] + spot[longest + 1:]
    return values.at[tuple(spot)].set(smallest).at[tuple(beside)].set(top_value)


def steps_of(stream_key, shape, pieces, smallest, high):
    def one(axis_at, shards_of):
        heights = jax.random.uniform(jax.random.fold_in(jax.random.fold_in(stream_key, 6), axis_at), (shards_of,), jnp.float32, smallest / len(pieces), high / len(pieces))
        return jnp.repeat(jnp.exp(heights), shape[axis_at] // shards_of).reshape((-1,) + (1,) * (len(shape) - axis_at - 1))

    factor_of = one(*pieces[0])
    for cut in pieces[1:]:
        factor_of = factor_of * one(*cut)
    return factor_of


def noise(own_key, dims, deviation, bound, pieces=(), held_as=jnp.bfloat16):
    values = deviation * jax.random.normal(own_key, dims, jnp.float32)
    if pieces:
        values = values * steps_of(own_key, dims, pieces, -0.22, 0.18)
    return jnp.clip(values, -bound, bound).astype(held_as)


def setup_inputs(seed: int = 0) -> dict:
    splits = jax.random.split(jax.random.key(seed), 6)
    return {
        "forcing": noise(splits[0], (COMP, NX, NY, NZ), 1.0, 6.0, ((1, 4), (2, 8)), jnp.float32),
        "phase_index": with_ends(jax.random.randint(splits[1], (NX, NY, NZ), 0, PHASES), jax.random.fold_in(splits[1], 1), 0, PHASES - 1).astype(jnp.int32),
        "visc_table": jnp.clip(jnp.exp(jax.random.uniform(splits[2], (PHASES,), jnp.float32, math.log(0.001), math.log(1000.0))), 0.001, 1000.0),
        "lower_bound": jnp.clip(jax.random.uniform(splits[3], (1,), jnp.float32, 0.1, 0.4), 0.1, 0.4),
        "upper_bound": jnp.clip(jax.random.uniform(splits[4], (1,), jnp.float32, 1.9, 2.3), 1.9, 2.3),
    }


def build_terms(eta_wide):
    centre = eta_wide[1:-1, 1:-1]
    depth_pad = jnp.pad(centre, ((0, 0), (0, 0), (1, 1)))
    lower_x = 0.5 * (centre + eta_wide[:-2, 1:-1])
    upper_x = 0.5 * (centre + eta_wide[2:, 1:-1])
    lower_y = 0.5 * (centre + eta_wide[1:-1, :-2])
    upper_y = 0.5 * (centre + eta_wide[1:-1, 2:])
    lower_z = 0.5 * (centre + depth_pad[:, :, :-2])
    upper_z = 0.5 * (centre + depth_pad[:, :, 2:])
    faces = (lower_x, upper_x, lower_y, upper_y, lower_z, upper_z)
    return faces + (diagonal_sum(faces),)


def diagonal_sum(faces):
    return faces[0] + faces[1] + faces[2] + faces[3] + faces[4] + faces[5]


def apply_local(padded, face_terms):
    lower_x, upper_x, lower_y, upper_y, lower_z, upper_z, diagonal = face_terms
    centre = padded[..., 1:-1, 1:-1, :]
    widths = [(0, 0)] * (centre.ndim - 1) + [(1, 1)]
    depth_pad = jnp.pad(centre, widths)
    beside = lower_x * padded[..., :-2, 1:-1, :] + upper_x * padded[..., 2:, 1:-1, :]
    beside = beside + lower_y * padded[..., 1:-1, :-2, :] + upper_y * padded[..., 1:-1, 2:, :]
    beside = beside + lower_z * depth_pad[..., :-2] + upper_z * depth_pad[..., 2:]
    return diagonal * centre - beside


def pick_child(face_term, along, which_child):
    row_count, col_count, depth_count = face_term.shape
    blocks = face_term.reshape(row_count // 2, 2, col_count // 2, 2, depth_count // 2, 2)
    selector = jnp.array([1.0 - which_child, 1.0 * which_child], jnp.float32)
    layout = [1, 1, 1, 1, 1, 1]
    layout[2 * along + 1] = 2
    return 0.0625 * jnp.sum(blocks * selector.reshape(layout), axis=(1, 3, 5))


def coarse_terms(face_terms):
    faces = (pick_child(face_terms[0], 0, 0), pick_child(face_terms[1], 0, 1),
             pick_child(face_terms[2], 1, 0), pick_child(face_terms[3], 1, 1),
             pick_child(face_terms[4], 2, 0), pick_child(face_terms[5], 2, 1))
    return faces + (diagonal_sum(faces),)


def restrict(field):
    row_count, col_count, depth_count = field.shape[-3:]
    blocks = field.reshape(field.shape[:-3] + (row_count // 2, 2, col_count // 2, 2, depth_count // 2, 2))
    return 0.125 * jnp.sum(blocks, axis=(-5, -3, -1))


def prolong(field):
    for along in (-3, -2, -1):
        field = jnp.repeat(field, 2, axis=along)
    return field


def chebyshev_constants(lower_value, upper_value, count):
    centre = 0.5 * (upper_value + lower_value)
    radius = 0.5 * (upper_value - lower_value)
    spread = centre / radius
    damping = 1.0 / spread
    carried = []
    scaled = []
    for number in range(count - 1):
        renewed = 1.0 / (2.0 * spread - damping)
        carried.append(renewed * damping)
        scaled.append(2.0 * renewed / radius)
        damping = renewed
    return 1.0 / centre, carried, scaled


def lateral(field):
    return jnp.pad(field, ((1, 1), (1, 1), (0, 0)))


def reference(forcing, phase_index, visc_table, lower_bound, upper_bound):
    viscosity = visc_table[phase_index]
    face_terms = build_terms(jnp.pad(viscosity, ((1, 1), (1, 1), (0, 0))))
    coarse_set = coarse_terms(face_terms)
    first_scale, carried, scaled = chebyshev_constants(lower_bound[0], upper_bound[0], max(CHEB, COARSE_STEPS))
    inverse = 1.0 / face_terms[6]
    coarse_inverse = 1.0 / coarse_set[6]

    def smooth(residual):
        direction = first_scale * inverse * residual
        for number in range(CHEB):
            residual = residual - apply_local(lateral(direction), face_terms)
            if number + 1 < CHEB:
                direction = carried[number] * direction + scaled[number] * inverse * residual
        return residual

    def cycle(component):
        residual = smooth(component)
        source = restrict(residual)
        direction = first_scale * coarse_inverse * source
        correction = direction
        for number in range(COARSE_STEPS - 1):
            source = source - apply_local(lateral(direction), coarse_set)
            direction = carried[number] * direction + scaled[number] * coarse_inverse * source
            correction = correction + direction
        residual = residual - apply_local(lateral(prolong(correction)), face_terms)
        return smooth(residual)

    return lax.map(cycle, forcing)
```

```python
import functools

import jax
import jax.numpy as jnp
from jax import lax
from jax.experimental import pallas as pl
from jax.experimental.pallas import tpu as pltpu
from jax.sharding import PartitionSpec as P

CHEB = 4
COARSE_STEPS = 4
HALO = CHEB
VISC_HALO = HALO + 1
COARSE_REACH = (HALO + 2) // 2
COARSE_HALO = COARSE_REACH + COARSE_STEPS - 1
ROW0 = 8
VMEM_LIMIT = 48 * 1024 * 1024


def chebyshev_constants(lower_value, upper_value, count):
    centre = 0.5 * (upper_value + lower_value)
    radius = 0.5 * (upper_value - lower_value)
    spread = centre / radius
    damping = 1.0 / spread
    carried = []
    scaled = []
    for number in range(count - 1):
        renewed = 1.0 / (2.0 * spread - damping)
        carried.append(renewed * damping)
        scaled.append(2.0 * renewed / radius)
        damping = renewed
    return (1.0 / centre, carried, scaled)


def constants_of(lower_ref, upper_ref):
    lower_value = jnp.full((1, 128), lower_ref[0], jnp.float32)
    upper_value = jnp.full((1, 128), upper_ref[0], jnp.float32)
    return chebyshev_constants(lower_value, upper_value, max(CHEB, COARSE_STEPS))


def lookup(table_ref, phases):
    viscosity = jnp.full(phases.shape, table_ref[0], jnp.float32)
    for table_row in range(1, table_ref.shape[0]):
        viscosity = jnp.where(phases == table_row, table_ref[table_row], viscosity)
    return viscosity


def lanes(rows, depth):
    return lax.broadcasted_iota(jnp.int32, (rows, depth), 1)


def below(value, by=1):
    return pltpu.roll(value, by, 1)


def above(value, by=1):
    return pltpu.roll(value, value.shape[1] - by, 1)


def is_odd(axis):
    return lax.rem(lax.axis_index(axis), 2) == 1


def pack_x_kernel(forcing_ref, phase_ref, table_ref, low_ref, high_ref):
    parts, nx = forcing_ref.shape[:2]
    for c in range(parts):
        for i in range(HALO):
            low_ref[c * HALO + i] = forcing_ref[c, i]
            high_ref[c * HALO + i] = forcing_ref[c, nx - HALO + i]
    for i in range(VISC_HALO):
        low_ref[parts * HALO + i] = lookup(table_ref, phase_ref[i])
        high_ref[parts * HALO + i] = lookup(table_ref, phase_ref[nx - VISC_HALO + i])


def pack_y_kernel(forcing_ref, phase_ref, table_ref, left_ref, right_ref, same_ref, cross_ref):
    parts, nx, ny = forcing_ref.shape[:3]
    odd = is_odd("gy")

    def put(row, low, high):
        count = low.shape[0]
        same_ref[pl.ds(row, count), :] = jnp.where(odd, low, high)
        cross_ref[pl.ds(row, count), :] = jnp.where(odd, high, low)

    row = 0
    for c in range(parts):
        for x in range(-HALO, nx + HALO):
            if x < 0:
                ref, at = left_ref, (c * HALO + x + HALO,)
            elif x < nx:
                ref, at = forcing_ref, (c, x)
            else:
                ref, at = right_ref, (c * HALO + x - nx,)
            put(row, ref[at + (slice(0, HALO),)], ref[at + (slice(ny - HALO, ny),)])
            row += HALO
    for x in range(-VISC_HALO, nx + VISC_HALO):
        first, last = slice(0, VISC_HALO), slice(ny - VISC_HALO, ny)
        if x < 0:
            at = parts * HALO + x + VISC_HALO
            put(row, left_ref[at, first], left_ref[at, last])
        elif x < nx:
            put(row, lookup(table_ref, phase_ref[x, first]), lookup(table_ref, phase_ref[x, last]))
        else:
            at = parts * HALO + x - nx
            put(row, right_ref[at, first], right_ref[at, last])
        row += VISC_HALO


def fine_steps(weight_ref, residual_ref, d_refs, constants, width):
    first_scale, carried, scaled = constants
    parts, rows = residual_ref.shape[0], residual_ref.shape[2]
    mid = pl.ds(ROW0, rows)

    def start(x, _):
        for c in range(parts):
            d_refs[0][c, x, mid, :] = first_scale * residual_ref[c, x]
        return 0

    lax.fori_loop(0, width, start, 0)
    for number in range(CHEB):
        old, new = d_refs[number % 2], d_refs[(number + 1) % 2]

        def step(x, _, number=number, old=old, new=new):
            weights = [weight_ref[f, x] for f in range(6)]
            for c in range(parts):
                own = old[c, x, mid, :]
                beside = weights[0] * old[c, x - 1, mid, :] + weights[1] * old[c, x + 1, mid, :]
                beside = beside + weights[2] * old[c, x, pl.ds(ROW0 - 1, rows), :]
                beside = beside + weights[3] * old[c, x, pl.ds(ROW0 + 1, rows), :]
                beside = beside + weights[4] * below(own) + weights[5] * above(own)
                fresh = residual_ref[c, x] - own + beside
                residual_ref[c, x] = fresh
                if number + 1 < CHEB:
                    new[c, x, mid, :] = carried[number] * own + scaled[number] * fresh
            return 0

        lax.fori_loop(number + 1, width - 1 - number, step, 0)


def clear_rims(ref, rows):
    planes = ref.shape[1]
    for c in range(ref.shape[0]):
        for x in range(planes):
            ref[c, x, pl.ds(0, ROW0), :] = jnp.zeros((ROW0, ref.shape[3]), jnp.float32)
            ref[c, x, pl.ds(ROW0 + rows, ROW0), :] = jnp.zeros((ROW0, ref.shape[3]), jnp.float32)


def pre_kernel(
    shape_x,
    shape_y,
    forcing_ref, phase_ref, table_ref, lower_ref, upper_ref, left_ref, right_ref, same_ref, cross_ref,
    weight_ref, diagonal_ref, smoothed_ref, coarse_ref, low_ref, high_ref,
    visc_ref, inverse_ref, residual_ref, d0_ref, d1_ref, pair_ref, row_ref,
):
    parts, nx, ny, depth = forcing_ref.shape
    width, rows = nx + 2 * HALO, ny + 2 * HALO
    at_x, at_y = lax.axis_index("gx"), lax.axis_index("gy")
    odd = is_odd("gy")
    has_left, has_right = at_x > 0, at_x < shape_x - 1
    has_low, has_high = at_y > 0, at_y < shape_y - 1
    visc_base = parts * width * HALO

    def low_rows(row, count):
        here = pl.ds(row, count)
        return jnp.where(odd, same_ref[here, :], cross_ref[here, :])

    def high_rows(row, count):
        here = pl.ds(row, count)
        return jnp.where(odd, cross_ref[here, :], same_ref[here, :])

    for i in range(nx + 2 * VISC_HALO):
        x = i - VISC_HALO
        if x < 0:
            own = left_ref[parts * HALO + i]
            inside = has_left
        elif x < nx:
            own = lookup(table_ref, phase_ref[x])
            inside = None
        else:
            own = right_ref[parts * HALO + x - nx]
            inside = has_right
        low = low_rows(visc_base + i * VISC_HALO, VISC_HALO)
        high = high_rows(visc_base + i * VISC_HALO, VISC_HALO)
        ok_low, ok_high = has_low, has_high
        if inside is not None:
            own = jnp.where(inside, own, 0.0)
            ok_low, ok_high = jnp.logical_and(ok_low, inside), jnp.logical_and(ok_high, inside)
        visc_ref[i, pl.ds(VISC_HALO, ny), :] = own
        visc_ref[i, pl.ds(0, VISC_HALO), :] = jnp.where(ok_low, low, 0.0)
        visc_ref[i, pl.ds(VISC_HALO + ny, VISC_HALO), :] = jnp.where(ok_high, high, 0.0)

    lane = lanes(rows, depth)

    def weigh(x, _):
        centre = visc_ref[x + 1, pl.ds(1, rows), :]
        halved = 0.5 * centre
        z_below = jnp.where(lane == 0, 0.0, below(halved))
        z_above = jnp.where(lane == depth - 1, 0.0, above(halved))
        faces = [
            halved + 0.5 * visc_ref[x, pl.ds(1, rows), :],
            halved + 0.5 * visc_ref[x + 2, pl.ds(1, rows), :],
            halved + 0.5 * visc_ref[x + 1, pl.ds(0, rows), :],
            halved + 0.5 * visc_ref[x + 1, pl.ds(2, rows), :],
            halved + z_below,
            halved + z_above,
        ]
        diagonal = faces[0] + faces[1] + faces[2] + faces[3] + faces[4] + faces[5]
        inside = centre > 0.0
        inverse = jnp.where(inside, 1.0 / jnp.where(inside, diagonal, 1.0), 0.0)
        for f in range(4):
            weight_ref[f, x] = faces[f] * inverse
        weight_ref[4, x] = jnp.where(lane == 0, 0.0, faces[4] * inverse)
        weight_ref[5, x] = jnp.where(lane == depth - 1, 0.0, faces[5] * inverse)
        inverse_ref[x] = inverse
        pair_ref[x] = diagonal
        return 0

    lax.fori_loop(0, width, weigh, 0)
    for x in range(nx):
        diagonal_ref[x] = pair_ref[x + HALO, pl.ds(HALO, ny), :]

    for c in range(parts):
        for i in range(width):
            x = i - HALO
            if x < 0:
                own = left_ref[c * HALO + i]
            elif x < nx:
                own = forcing_ref[c, x]
            else:
                own = right_ref[c * HALO + x - nx]
            at = (c * width + i) * HALO
            residual_ref[c, i, pl.ds(HALO, ny), :] = own * inverse_ref[i, pl.ds(HALO, ny), :]
            residual_ref[c, i, pl.ds(0, HALO), :] = low_rows(at, HALO) * inverse_ref[i, pl.ds(0, HALO), :]
            residual_ref[c, i, pl.ds(HALO + ny, HALO), :] = (
                high_rows(at, HALO) * inverse_ref[i, pl.ds(HALO + ny, HALO), :]
            )

    clear_rims(d0_ref, rows)
    clear_rims(d1_ref, rows)
    fine_steps(weight_ref, residual_ref, (d0_ref, d1_ref), constants_of(lower_ref, upper_ref), width)

    half = ny // 2
    even_own = lanes(ny, depth) % 2 == 0
    even_wide = lanes(ny + 2, depth) % 2 == 0
    even = lanes(half, depth) % 2 == 0
    lane_half = lanes(half, depth)

    def z_pair(value, even_mask):
        return value + jnp.where(even_mask, above(value), below(value))

    def y_sum(value, slot):
        row_ref[slot, pl.ds(0, value.shape[0]), :] = value
        return row_ref[slot, pl.ds(0, half, 2), :] + row_ref[slot, pl.ds(1, half, 2), :]

    def visc_own(x):
        return visc_ref[x + VISC_HALO, pl.ds(VISC_HALO, ny), :]

    inverses = []
    for i in range(nx // 2):
        faces_x = []
        for x in (2 * i - 1, 2 * i, 2 * i + 1, 2 * i + 2):
            faces_x.append(y_sum(z_pair(visc_own(x), even_own), 0))
        lower_x = faces_x[0] + faces_x[1]
        upper_x = faces_x[2] + faces_x[3]
        wide = pl.ds(VISC_HALO - 1, ny + 2)
        both = visc_ref[2 * i + VISC_HALO, wide, :] + visc_ref[2 * i + 1 + VISC_HALO, wide, :]
        row_ref[1, pl.ds(0, ny + 2), :] = z_pair(both, even_wide)
        picks = [row_ref[1, pl.ds(start, half, 2), :] for start in range(4)]
        lower_y = picks[0] + picks[1]
        upper_y = picks[2] + picks[3]
        column = y_sum(both[1 : ny + 1], 2)
        lower_z = column + jnp.where(lane_half == 0, 0.0, below(column))
        lower_z = jnp.where(even, lower_z, below(lower_z))
        upper_z = column + jnp.where(lane_half == depth - 1, 0.0, above(column))
        upper_z = jnp.where(even, above(upper_z), upper_z)
        inverse = 1.0 / (lower_x + upper_x + lower_y + upper_y + lower_z + upper_z)
        inverses.append(32.0 * inverse)
        sources = []
        for c in range(parts):
            total = 0.0
            for x in (2 * i, 2 * i + 1):
                total = total + residual_ref[c, x + HALO, pl.ds(HALO, ny), :] * diagonal_ref[x]
            sources.append(y_sum(z_pair(total, even_own), 3 + c) * (4.0 * inverse))
        faces = [upper_x * (1.0 / 32.0), upper_y * (1.0 / 32.0), upper_z * (1.0 / 32.0)]
        coarse_ref[0, i] = jnp.where(even, sources[0], sources[1])
        coarse_ref[1, i] = jnp.where(even, sources[2], faces[0])
        coarse_ref[2, i] = jnp.where(even, faces[1], faces[2])
        if i % 2 == 1:
            coarse_ref[3, i // 2] = jnp.where(even, inverses[i - 1], inverses[i])

    for c in range(parts):
        for x in range(nx):
            smoothed_ref[c, x] = residual_ref[c, x + HALO, pl.ds(HALO, ny), :]

    at = 0
    ncx = nx // 2
    for f in range(4):
        shared = 2 if f == 3 else 1
        count = COARSE_HALO // shared
        for i in range(count):
            low_ref[at] = coarse_ref[f, i]
            high_ref[at] = coarse_ref[f, ncx // shared - count + i]
            at += 1
    tiles = ny // half
    for c in range(parts):
        for i in range(HALO):
            for t in range(tiles):
                low_ref[at] = smoothed_ref[c, i, pl.ds(t * half, half), :]
                high_ref[at] = smoothed_ref[c, nx - HALO + i, pl.ds(t * half, half), :]
                at += 1


def coarse_spot(f, i, ncx):
    shared = 2 if f == 3 else 1
    count, own = COARSE_HALO // shared, ncx // shared
    base = f * COARSE_HALO
    if i < count:
        return "left", base + i
    if i < count + own:
        return "own", i - count
    return "right", base + i - count - own


def pack_y2_kernel(smoothed_ref, coarse_ref, left_ref, right_ref, same_ref, cross_ref):
    parts, nx, ny = smoothed_ref.shape[:3]
    ncx, half = nx // 2, ny // 2
    odd = is_odd("gy")
    sides = {"left": left_ref, "right": right_ref}

    def put(row, low, high):
        count = low.shape[0]
        same_ref[pl.ds(row, count), :] = jnp.where(odd, low, high)
        cross_ref[pl.ds(row, count), :] = jnp.where(odd, high, low)

    row = 0
    for f in range(4):
        shared = 2 if f == 3 else 1
        for i in range((ncx + 2 * COARSE_HALO) // shared):
            side, at = coarse_spot(f, i, ncx)
            if side == "own":
                ref, spot = coarse_ref, (f, at)
            else:
                ref, spot = sides[side], (at,)
            first, last = slice(0, COARSE_HALO), slice(half - COARSE_HALO, half)
            put(row, ref[spot + (first,)], ref[spot + (last,)])
            row += COARSE_HALO
    tiles = ny // half
    fine_base = 3 * COARSE_HALO + COARSE_HALO // 2
    for c in range(parts):
        for x in range(-HALO, nx + HALO):
            if 0 <= x < nx:
                put(row, smoothed_ref[c, x, pl.ds(0, HALO), :], smoothed_ref[c, x, pl.ds(ny - HALO, HALO), :])
            else:
                ref = left_ref if x < 0 else right_ref
                i = x + HALO if x < 0 else x - nx
                at = fine_base + (c * HALO + i) * tiles
                put(row, ref[at, pl.ds(0, HALO), :], ref[at + tiles - 1, pl.ds(half - HALO, HALO), :])
            row += HALO


def post_kernel(
    shape_x,
    shape_y,
    weight_ref, diagonal_ref, smoothed_ref, coarse_ref, lower_ref, upper_ref, left_ref, right_ref, same_ref, cross_ref,
    out_ref,
    field_ref, cweight_ref, source_ref, cd0_ref, cd1_ref, correction_ref, prolonged_ref, residual_ref, d0_ref, d1_ref,
):
    parts, nx, ny, depth = smoothed_ref.shape
    width, rows = nx + 2 * HALO, ny + 2 * HALO
    ncx, half = nx // 2, ny // 2
    cwidth, crows = ncx + 2 * COARSE_HALO, half + 2 * COARSE_HALO
    srows = source_ref.shape[2]
    at_x, at_y = lax.axis_index("gx"), lax.axis_index("gy")
    odd = is_odd("gy")
    has_left, has_right = at_x > 0, at_x < shape_x - 1
    has_low, has_high = at_y > 0, at_y < shape_y - 1
    sides = {"left": left_ref, "right": right_ref}
    constants = constants_of(lower_ref, upper_ref)
    first_scale, carried, scaled = constants

    def low_rows(row, count):
        here = pl.ds(row, count)
        return jnp.where(odd, same_ref[here, :], cross_ref[here, :])

    def high_rows(row, count):
        here = pl.ds(row, count)
        return jnp.where(odd, cross_ref[here, :], same_ref[here, :])

    def masked(inside, own, low, high):
        ok_low, ok_high = has_low, has_high
        if inside is not None:
            own = jnp.where(inside, own, 0.0)
            ok_low, ok_high = jnp.logical_and(ok_low, inside), jnp.logical_and(ok_high, inside)
        return own, jnp.where(ok_low, low, 0.0), jnp.where(ok_high, high, 0.0)

    insides = {"left": has_left, "own": None, "right": has_right}
    row = 0
    for f in range(4):
        shared = 2 if f == 3 else 1
        for i in range(cwidth // shared):
            side, at = coarse_spot(f, i, ncx)
            own = coarse_ref[f, at] if side == "own" else sides[side][at]
            low, high = low_rows(row, COARSE_HALO), high_rows(row, COARSE_HALO)
            own, low, high = masked(insides[side], own, low, high)
            field_ref[f, i, pl.ds(ROW0 + COARSE_HALO, half), :] = own
            field_ref[f, i, pl.ds(ROW0, COARSE_HALO), :] = low
            field_ref[f, i, pl.ds(ROW0 + COARSE_HALO + half, COARSE_HALO), :] = high
            field_ref[f, i, pl.ds(0, ROW0), :] = jnp.zeros((ROW0, depth), jnp.float32)
            tail = field_ref.shape[2] - ROW0 - crows
            field_ref[f, i, pl.ds(ROW0 + crows, tail), :] = jnp.zeros((tail, depth), jnp.float32)
            row += COARSE_HALO
    tiles = ny // half
    fine_base = 3 * COARSE_HALO + COARSE_HALO // 2
    for c in range(parts):
        for i in range(width):
            x = i - HALO
            if 0 <= x < nx:
                side = "own"
                own = smoothed_ref[c, x]
            else:
                side = "left" if x < 0 else "right"
                j = i if x < 0 else x - nx
                at = fine_base + (c * HALO + j) * tiles
                own = jnp.concatenate([sides[side][at + t] for t in range(tiles)], axis=0)
            own, low, high = masked(insides[side], own, low_rows(row, HALO), high_rows(row, HALO))
            residual_ref[c, i, pl.ds(HALO, ny), :] = own
            residual_ref[c, i, pl.ds(0, HALO), :] = low
            residual_ref[c, i, pl.ds(HALO + ny, HALO), :] = high
            row += HALO

    mid = pl.ds(ROW0, srows)
    lane = lanes(srows, depth)
    even = lane % 2 == 0

    def first_of(value):
        return jnp.where(even, value, below(value))

    def second_of(value):
        return jnp.where(even, above(value), value)

    even_low = lanes(field_ref.shape[2], depth) % 2 == 0
    for i in range(cwidth):
        packed = field_ref[3, i // 2, mid, :]
        inverse = first_of(packed) if i % 2 == 0 else second_of(packed)
        upper_x = second_of(field_ref[1, i, mid, :])
        faces_y = field_ref[2, i]
        upper_y = jnp.where(even_low, faces_y, below(faces_y))
        upper_z = second_of(field_ref[2, i, mid, :])
        source_ref[0, i] = field_ref[0, i, mid, :]
        source_ref[1, i] = first_of(field_ref[1, i, mid, :])
        if i > 0:
            cweight_ref[0, i] = second_of(field_ref[1, i - 1, mid, :]) * inverse
        cweight_ref[1, i] = upper_x * inverse
        cweight_ref[2, i] = upper_y[ROW0 - 1 : ROW0 - 1 + srows] * inverse
        cweight_ref[3, i] = upper_y[ROW0 : ROW0 + srows] * inverse
        cweight_ref[4, i] = jnp.where(lane < 2, 0.0, below(upper_z, 2) * inverse)
        cweight_ref[5, i] = jnp.where(lane >= depth - 2, 0.0, upper_z * inverse)

    clear_rims(cd0_ref, srows)
    clear_rims(cd1_ref, srows)

    def start(i, _):
        for s in range(2):
            value = first_scale * source_ref[s, i]
            cd0_ref[s, i, mid, :] = value
            correction_ref[s, i] = value
        return 0

    lax.fori_loop(0, cwidth, start, 0)
    for number in range(COARSE_STEPS - 1):
        old, new = ((cd0_ref, cd1_ref), (cd1_ref, cd0_ref))[number % 2]

        def step(i, _, number=number, old=old, new=new):
            weights = [cweight_ref[f, i] for f in range(6)]
            for s in range(2):
                own = old[s, i, mid, :]
                beside = weights[0] * old[s, i - 1, mid, :] + weights[1] * old[s, i + 1, mid, :]
                beside = beside + weights[2] * old[s, i, pl.ds(ROW0 - 1, srows), :]
                beside = beside + weights[3] * old[s, i, pl.ds(ROW0 + 1, srows), :]
                beside = beside + weights[4] * below(own, 2) + weights[5] * above(own, 2)
                fresh = source_ref[s, i] - own + beside
                source_ref[s, i] = fresh
                direction = carried[number] * own + scaled[number] * fresh
                new[s, i, mid, :] = direction
                correction_ref[s, i] = correction_ref[s, i] + direction
            return 0

        lax.fori_loop(number + 1, cwidth - 1 - number, step, 0)

    edge = COARSE_HALO - COARSE_REACH
    pwidth, prows = ncx + 2 * COARSE_REACH, half + 2 * COARSE_REACH
    prow0 = ROW0 - (2 * COARSE_REACH - HALO)
    even_p = lanes(prows, depth) % 2 == 0
    for i in range(pwidth):
        pair = correction_ref[0, i + edge, pl.ds(edge, prows), :]
        single = correction_ref[1, i + edge, pl.ds(edge, prows), :]
        values = [
            jnp.where(even_p, pair, below(pair)),
            jnp.where(even_p, above(pair), pair),
            single,
        ]
        for c in range(parts):
            prolonged_ref[c, i, pl.ds(prow0, prows, 2), :] = values[c]
            prolonged_ref[c, i, pl.ds(prow0 + 1, prows, 2), :] = values[c]

    fine = pl.ds(ROW0, rows)
    shift = 2 * COARSE_REACH - HALO
    for i in range(width):
        weights = [weight_ref[f, i] for f in range(6)]
        at, before, after = (i + shift) // 2, (i + shift - 1) // 2, (i + shift + 1) // 2
        for c in range(parts):
            own = prolonged_ref[c, at, fine, :]
            beside = weights[0] * prolonged_ref[c, before, fine, :] + weights[1] * prolonged_ref[c, after, fine, :]
            beside = beside + weights[2] * prolonged_ref[c, at, pl.ds(ROW0 - 1, rows), :]
            beside = beside + weights[3] * prolonged_ref[c, at, pl.ds(ROW0 + 1, rows), :]
            beside = beside + weights[4] * below(own) + weights[5] * above(own)
            residual_ref[c, i] = residual_ref[c, i] - own + beside

    clear_rims(d0_ref, rows)
    clear_rims(d1_ref, rows)
    fine_steps(weight_ref, residual_ref, (d0_ref, d1_ref), constants, width)
    for c in range(parts):
        for x in range(nx):
            out_ref[c, x] = residual_ref[c, x + HALO, pl.ds(HALO, ny), :] * diagonal_ref[x]


def call(kernel, outs, scratch, specs):
    return pl.pallas_call(
        kernel,
        out_shape=[jax.ShapeDtypeStruct(shape, jnp.float32) for shape in outs],
        in_specs=[pl.BlockSpec(memory_space=space) for space in specs],
        out_specs=[pl.BlockSpec(memory_space=pltpu.VMEM) for _ in outs],
        scratch_shapes=[pltpu.VMEM(shape, jnp.float32) for shape in scratch],
        compiler_params=pltpu.CompilerParams(vmem_limit_bytes=VMEM_LIMIT),
    )


def ring_x(low, high):
    devices = lax.axis_size("gx")
    up = [(i, (i + 1) % devices) for i in range(devices)]
    down = [(j, i) for i, j in up]
    return lax.ppermute(high, "gx", up), lax.ppermute(low, "gx", down)


def swap_y(same, cross):
    devices = lax.axis_size("gy")
    pairs = [(i, i ^ 1) for i in range(devices)]
    others = [(0, 0), (devices - 1, devices - 1)]
    others = others + [(i, ((i + 1) ^ 1) - 1) for i in range(1, devices - 1)]
    return lax.ppermute(same, "gy", pairs), lax.ppermute(cross, "gy", others)


def up_to(value, unit):
    return -(-value // unit) * unit


def local(forcing, phase_index, visc_table, lower_bound, upper_bound):
    vmem, smem = pltpu.VMEM, pltpu.SMEM
    parts, nx, ny, depth = forcing.shape
    shape_x, shape_y = lax.axis_size("gx"), lax.axis_size("gy")
    width, rows = nx + 2 * HALO, ny + 2 * HALO
    ncx, half = nx // 2, ny // 2
    cwidth, crows = ncx + 2 * COARSE_HALO, half + 2 * COARSE_HALO
    srows = up_to(crows, 8)

    slab = (parts * HALO + VISC_HALO, ny, depth)
    low, high = call(pack_x_kernel, [slab, slab], [], [vmem, vmem, smem])(forcing, phase_index, visc_table)
    left, right = ring_x(low, high)

    count = up_to(parts * width * HALO + (nx + 2 * VISC_HALO) * VISC_HALO, 8)
    slab = (count, depth)
    same, cross = call(pack_y_kernel, [slab, slab], [], [vmem, vmem, smem, vmem, vmem])(
        forcing, phase_index, visc_table, left, right
    )
    same, cross = swap_y(same, cross)

    tiles = 3 * COARSE_HALO + COARSE_HALO // 2 + parts * HALO * (ny // half)
    slab = (tiles, half, depth)
    fine_d = (parts, width, rows + 2 * ROW0, depth)
    weight, diagonal, smoothed, coarse, low, high = call(
        functools.partial(pre_kernel, shape_x, shape_y),
        [(6, width, rows, depth), (nx, ny, depth), (parts, nx, ny, depth), (4, ncx, half, depth), slab, slab],
        [
            (nx + 2 * VISC_HALO, up_to(ny + 2 * VISC_HALO, 8), depth),
            (width, rows, depth),
            (parts, width, rows, depth),
            fine_d,
            fine_d,
            (width, rows, depth),
            (6, up_to(ny + 2, 8), depth),
        ],
        [vmem, vmem, smem, smem, smem, vmem, vmem, vmem, vmem],
    )(forcing, phase_index, visc_table, lower_bound, upper_bound, left, right, same, cross)
    left, right = ring_x(low, high)

    count = up_to((3 * cwidth + cwidth // 2) * COARSE_HALO + parts * width * HALO, 8)
    slab = (count, depth)
    same, cross = call(pack_y2_kernel, [slab, slab], [], [vmem] * 4)(smoothed, coarse, left, right)
    same, cross = swap_y(same, cross)

    coarse_d = (2, cwidth, srows + 2 * ROW0, depth)
    (out,) = call(
        functools.partial(post_kernel, shape_x, shape_y),
        [(parts, nx, ny, depth)],
        [
            (4, cwidth, up_to(ROW0 + crows + 1, 8), depth),
            (6, cwidth, srows, depth),
            (2, cwidth, srows, depth),
            coarse_d,
            coarse_d,
            (2, cwidth, srows, depth),
            (parts, ncx + 2 * COARSE_REACH, rows + 2 * ROW0, depth),
            (parts, width, rows, depth),
            fine_d,
            fine_d,
        ],
        [vmem, vmem, vmem, vmem, smem, smem, vmem, vmem, vmem, vmem],
    )(weight, diagonal, smoothed, coarse, lower_bound, upper_bound, left, right, same, cross)
    return out


def solution(mesh):
    in_specs = (P(None, "gx", "gy", None), P("gx", "gy", None), P(), P(), P())
    out_specs = P(None, "gx", "gy", None)
    return jax.shard_map(local, mesh=mesh, in_specs=in_specs, out_specs=out_specs, check_vma=False)
```

```python
import functools

import jax
import jax.numpy as jnp
from jax import lax
from jax.experimental import pallas as pl
from jax.experimental.pallas import tpu as pltpu
from jax.sharding import PartitionSpec as P

CHEB = 4
COARSE_STEPS = 4
HALO = CHEB
VISC_HALO = HALO + 1
COARSE_REACH = (HALO + 2) // 2
COARSE_HALO = COARSE_REACH + COARSE_STEPS - 1
ROW0 = 8
VMEM_LIMIT = 48 * 1024 * 1024


def chebyshev_constants(lower_value, upper_value, count):
    centre = 0.5 * (upper_value + lower_value)
    radius = 0.5 * (upper_value - lower_value)
    spread = centre / radius
    damping = 1.0 / spread
    carried = []
    scaled = []
    for number in range(count - 1):
        renewed = 1.0 / (2.0 * spread - damping)
        carried.append(renewed * damping)
        scaled.append(2.0 * renewed / radius)
        damping = renewed
    return (1.0 / centre, carried, scaled)


def constants_of(lower_ref, upper_ref):
    lower_value = jnp.full((1, 128), lower_ref[0], jnp.float32)
    upper_value = jnp.full((1, 128), upper_ref[0], jnp.float32)
    return chebyshev_constants(lower_value, upper_value, max(CHEB, COARSE_STEPS))


def lookup(table_ref, phases):
    viscosity = jnp.full(phases.shape, table_ref[0], jnp.float32)
    for table_row in range(1, table_ref.shape[0]):
        viscosity = jnp.where(phases == table_row, table_ref[table_row], viscosity)
    return viscosity


def lanes(rows, depth):
    return lax.broadcasted_iota(jnp.int32, (rows, depth), 1)


def below(value, by=1):
    return pltpu.roll(value, by, 1)


def above(value, by=1):
    return pltpu.roll(value, value.shape[1] - by, 1)


def is_odd(axis):
    return lax.rem(lax.axis_index(axis), 2) == 1


def pack_x_kernel(forcing_ref, phase_ref, table_ref, low_ref, high_ref):
    parts, nx = forcing_ref.shape[:2]
    for c in range(parts):
        for i in range(HALO):
            low_ref[c * HALO + i] = forcing_ref[c, i]
            high_ref[c * HALO + i] = forcing_ref[c, nx - HALO + i]
    for i in range(VISC_HALO):
        low_ref[parts * HALO + i] = lookup(table_ref, phase_ref[i])
        high_ref[parts * HALO + i] = lookup(table_ref, phase_ref[nx - VISC_HALO + i])


def pack_y_kernel(forcing_ref, phase_ref, table_ref, left_ref, right_ref, same_ref, cross_ref):
    parts, nx, ny = forcing_ref.shape[:3]
    odd = is_odd("gy")

    def put(row, low, high):
        count = low.shape[0]
        same_ref[pl.ds(row, count), :] = jnp.where(odd, low, high)
        cross_ref[pl.ds(row, count), :] = jnp.where(odd, high, low)

    row = 0
    for c in range(parts):
        for x in range(-HALO, nx + HALO):
            if x < 0:
                ref, at = left_ref, (c * HALO + x + HALO,)
            elif x < nx:
                ref, at = forcing_ref, (c, x)
            else:
                ref, at = right_ref, (c * HALO + x - nx,)
            put(row, ref[at + (slice(0, HALO),)], ref[at + (slice(ny - HALO, ny),)])
            row += HALO
    for x in range(-VISC_HALO, nx + VISC_HALO):
        first, last = slice(0, VISC_HALO), slice(ny - VISC_HALO, ny)
        if x < 0:
            at = parts * HALO + x + VISC_HALO
            put(row, left_ref[at, first], left_ref[at, last])
        elif x < nx:
            put(row, lookup(table_ref, phase_ref[x, first]), lookup(table_ref, phase_ref[x, last]))
        else:
            at = parts * HALO + x - nx
            put(row, right_ref[at, first], right_ref[at, last])
        row += VISC_HALO


def fine_steps(weight_ref, base_ref, residual_ref, d_refs, constants, width, finish):
    first_scale, carried, scaled = constants
    parts, rows = residual_ref.shape[0], residual_ref.shape[2]
    for number in range(CHEB):
        old = base_ref if number == 0 else d_refs[number % 2]
        new = d_refs[(number + 1) % 2]
        last = number + 1 == CHEB
        skip, count = (HALO, rows - 2 * HALO) if last else (0, rows)
        inner = pl.ds(skip, count)
        for x in range(number + 1, width - 1 - number):
            weights = [weight_ref[f, x, inner, :] for f in range(6)]
            for c in range(parts):
                own = old[c, x, pl.ds(ROW0 + skip, count), :]
                beside = weights[0] * old[c, x - 1, pl.ds(ROW0 + skip, count), :]
                beside = beside + weights[1] * old[c, x + 1, pl.ds(ROW0 + skip, count), :]
                beside = beside + weights[2] * old[c, x, pl.ds(ROW0 + skip - 1, count), :]
                beside = beside + weights[3] * old[c, x, pl.ds(ROW0 + skip + 1, count), :]
                beside = beside + weights[4] * below(own) + weights[5] * above(own)
                if number == 0:
                    fresh = own - first_scale * (own - beside)
                    own = first_scale * own
                else:
                    fresh = residual_ref[c, x, inner, :] - own + beside
                if last:
                    finish(c, x, fresh)
                else:
                    residual_ref[c, x] = fresh
                    new[c, x, pl.ds(ROW0, rows), :] = carried[number] * own + scaled[number] * fresh


def clear_rims(ref, rows):
    planes = ref.shape[1]
    for c in range(ref.shape[0]):
        for x in range(planes):
            ref[c, x, pl.ds(0, ROW0), :] = jnp.zeros((ROW0, ref.shape[3]), jnp.float32)
            ref[c, x, pl.ds(ROW0 + rows, ROW0), :] = jnp.zeros((ROW0, ref.shape[3]), jnp.float32)


def pre_kernel(
    shape_x,
    shape_y,
    forcing_ref, phase_ref, table_ref, lower_ref, upper_ref, left_ref, right_ref, same_ref, cross_ref,
    weight_ref, diagonal_ref, smoothed_ref, coarse_ref, low_ref, high_ref,
    visc_ref, inverse_ref, residual_ref, base_ref, d0_ref, d1_ref, pair_ref, row_ref,
):
    parts, nx, ny, depth = forcing_ref.shape
    width, rows = nx + 2 * HALO, ny + 2 * HALO
    at_x, at_y = lax.axis_index("gx"), lax.axis_index("gy")
    odd = is_odd("gy")
    has_left, has_right = at_x > 0, at_x < shape_x - 1
    has_low, has_high = at_y > 0, at_y < shape_y - 1
    visc_base = parts * width * HALO

    def low_rows(row, count):
        here = pl.ds(row, count)
        return jnp.where(odd, same_ref[here, :], cross_ref[here, :])

    def high_rows(row, count):
        here = pl.ds(row, count)
        return jnp.where(odd, cross_ref[here, :], same_ref[here, :])

    for i in range(nx + 2 * VISC_HALO):
        x = i - VISC_HALO
        if x < 0:
            own = left_ref[parts * HALO + i]
            inside = has_left
        elif x < nx:
            own = lookup(table_ref, phase_ref[x])
            inside = None
        else:
            own = right_ref[parts * HALO + x - nx]
            inside = has_right
        low = low_rows(visc_base + i * VISC_HALO, VISC_HALO)
        high = high_rows(visc_base + i * VISC_HALO, VISC_HALO)
        ok_low, ok_high = has_low, has_high
        if inside is not None:
            own = jnp.where(inside, own, 0.0)
            ok_low, ok_high = jnp.logical_and(ok_low, inside), jnp.logical_and(ok_high, inside)
        visc_ref[i, pl.ds(VISC_HALO, ny), :] = own
        visc_ref[i, pl.ds(0, VISC_HALO), :] = jnp.where(ok_low, low, 0.0)
        visc_ref[i, pl.ds(VISC_HALO + ny, VISC_HALO), :] = jnp.where(ok_high, high, 0.0)

    lane = lanes(rows, depth)

    for x in range(width):
        centre = visc_ref[x + 1, pl.ds(1, rows), :]
        halved = 0.5 * centre
        z_below = jnp.where(lane == 0, 0.0, below(halved))
        z_above = jnp.where(lane == depth - 1, 0.0, above(halved))
        faces = [
            halved + 0.5 * visc_ref[x, pl.ds(1, rows), :],
            halved + 0.5 * visc_ref[x + 2, pl.ds(1, rows), :],
            halved + 0.5 * visc_ref[x + 1, pl.ds(0, rows), :],
            halved + 0.5 * visc_ref[x + 1, pl.ds(2, rows), :],
            halved + z_below,
            halved + z_above,
        ]
        diagonal = faces[0] + faces[1] + faces[2] + faces[3] + faces[4] + faces[5]
        inside = centre > 0.0
        inverse = jnp.where(inside, 1.0 / jnp.where(inside, diagonal, 1.0), 0.0)
        for f in range(4):
            weight_ref[f, x] = faces[f] * inverse
        weight_ref[4, x] = jnp.where(lane == 0, 0.0, faces[4] * inverse)
        weight_ref[5, x] = jnp.where(lane == depth - 1, 0.0, faces[5] * inverse)
        inverse_ref[x] = inverse
        if HALO <= x < HALO + nx:
            pair_ref[...] = diagonal
            diagonal_ref[x - HALO] = pair_ref[pl.ds(HALO, ny), :]

    for c in range(parts):
        for i in range(width):
            x = i - HALO
            if x < 0:
                own = left_ref[c * HALO + i]
            elif x < nx:
                own = forcing_ref[c, x]
            else:
                own = right_ref[c * HALO + x - nx]
            at = (c * width + i) * HALO
            base_ref[c, i, pl.ds(ROW0 + HALO, ny), :] = own * inverse_ref[i, pl.ds(HALO, ny), :]
            base_ref[c, i, pl.ds(ROW0, HALO), :] = low_rows(at, HALO) * inverse_ref[i, pl.ds(0, HALO), :]
            base_ref[c, i, pl.ds(ROW0 + HALO + ny, HALO), :] = (
                high_rows(at, HALO) * inverse_ref[i, pl.ds(HALO + ny, HALO), :]
            )

    for ref in (base_ref, d0_ref, d1_ref):
        clear_rims(ref, rows)

    def finish(c, x, value):
        smoothed_ref[c, x - HALO] = value

    constants = constants_of(lower_ref, upper_ref)
    fine_steps(weight_ref, base_ref, residual_ref, (d0_ref, d1_ref), constants, width, finish)

    half = ny // 2
    even_own = lanes(ny, depth) % 2 == 0
    even_wide = lanes(ny + 2, depth) % 2 == 0
    even = lanes(half, depth) % 2 == 0
    lane_half = lanes(half, depth)

    def z_pair(value, even_mask):
        return value + jnp.where(even_mask, above(value), below(value))

    def y_sum(value, slot):
        row_ref[slot, pl.ds(0, value.shape[0]), :] = value
        return row_ref[slot, pl.ds(0, half, 2), :] + row_ref[slot, pl.ds(1, half, 2), :]

    def visc_own(x):
        return visc_ref[x + VISC_HALO, pl.ds(VISC_HALO, ny), :]

    inverses = []
    for i in range(nx // 2):
        faces_x = []
        for x in (2 * i - 1, 2 * i, 2 * i + 1, 2 * i + 2):
            faces_x.append(y_sum(z_pair(visc_own(x), even_own), 0))
        lower_x = faces_x[0] + faces_x[1]
        upper_x = faces_x[2] + faces_x[3]
        wide = pl.ds(VISC_HALO - 1, ny + 2)
        both = visc_ref[2 * i + VISC_HALO, wide, :] + visc_ref[2 * i + 1 + VISC_HALO, wide, :]
        row_ref[1, pl.ds(0, ny + 2), :] = z_pair(both, even_wide)
        picks = [row_ref[1, pl.ds(start, half, 2), :] for start in range(4)]
        lower_y = picks[0] + picks[1]
        upper_y = picks[2] + picks[3]
        column = y_sum(both[1 : ny + 1], 2)
        lower_z = column + jnp.where(lane_half == 0, 0.0, below(column))
        lower_z = jnp.where(even, lower_z, below(lower_z))
        upper_z = column + jnp.where(lane_half == depth - 1, 0.0, above(column))
        upper_z = jnp.where(even, above(upper_z), upper_z)
        inverse = 1.0 / (lower_x + upper_x + lower_y + upper_y + lower_z + upper_z)
        inverses.append(32.0 * inverse)
        sources = []
        for c in range(parts):
            total = 0.0
            for x in (2 * i, 2 * i + 1):
                total = total + smoothed_ref[c, x] * diagonal_ref[x]
            sources.append(y_sum(z_pair(total, even_own), 3 + c) * (4.0 * inverse))
        faces = [upper_x * (1.0 / 32.0), upper_y * (1.0 / 32.0), upper_z * (1.0 / 32.0)]
        coarse_ref[0, i] = jnp.where(even, sources[0], sources[1])
        coarse_ref[1, i] = jnp.where(even, sources[2], faces[0])
        coarse_ref[2, i] = jnp.where(even, faces[1], faces[2])
        if i % 2 == 1:
            coarse_ref[3, i // 2] = jnp.where(even, inverses[i - 1], inverses[i])

    at = 0
    ncx = nx // 2
    for f in range(4):
        shared = 2 if f == 3 else 1
        count = COARSE_HALO // shared
        for i in range(count):
            low_ref[at] = coarse_ref[f, i]
            high_ref[at] = coarse_ref[f, ncx // shared - count + i]
            at += 1
    tiles = ny // half
    for c in range(parts):
        for i in range(HALO):
            for t in range(tiles):
                low_ref[at] = smoothed_ref[c, i, pl.ds(t * half, half), :]
                high_ref[at] = smoothed_ref[c, nx - HALO + i, pl.ds(t * half, half), :]
                at += 1


def coarse_spot(f, i, ncx):
    shared = 2 if f == 3 else 1
    count, own = COARSE_HALO // shared, ncx // shared
    base = f * COARSE_HALO
    if i < count:
        return "left", base + i
    if i < count + own:
        return "own", i - count
    return "right", base + i - count - own


def pack_y2_kernel(smoothed_ref, coarse_ref, left_ref, right_ref, same_ref, cross_ref):
    parts, nx, ny = smoothed_ref.shape[:3]
    ncx, half = nx // 2, ny // 2
    odd = is_odd("gy")
    sides = {"left": left_ref, "right": right_ref}

    def put(row, low, high):
        count = low.shape[0]
        same_ref[pl.ds(row, count), :] = jnp.where(odd, low, high)
        cross_ref[pl.ds(row, count), :] = jnp.where(odd, high, low)

    row = 0
    for f in range(4):
        shared = 2 if f == 3 else 1
        for i in range((ncx + 2 * COARSE_HALO) // shared):
            side, at = coarse_spot(f, i, ncx)
            if side == "own":
                ref, spot = coarse_ref, (f, at)
            else:
                ref, spot = sides[side], (at,)
            first, last = slice(0, COARSE_HALO), slice(half - COARSE_HALO, half)
            put(row, ref[spot + (first,)], ref[spot + (last,)])
            row += COARSE_HALO
    tiles = ny // half
    fine_base = 3 * COARSE_HALO + COARSE_HALO // 2
    for c in range(parts):
        for x in range(-HALO, nx + HALO):
            if 0 <= x < nx:
                put(row, smoothed_ref[c, x, pl.ds(0, HALO), :], smoothed_ref[c, x, pl.ds(ny - HALO, HALO), :])
            else:
                ref = left_ref if x < 0 else right_ref
                i = x + HALO if x < 0 else x - nx
                at = fine_base + (c * HALO + i) * tiles
                put(row, ref[at, pl.ds(0, HALO), :], ref[at + tiles - 1, pl.ds(half - HALO, HALO), :])
            row += HALO


def post_kernel(
    shape_x,
    shape_y,
    weight_ref, diagonal_ref, smoothed_ref, coarse_ref, lower_ref, upper_ref, left_ref, right_ref, same_ref, cross_ref,
    out_ref,
    field_ref, cweight_ref, source_ref, cd0_ref, cd1_ref, correction_ref, prolonged_ref, residual_ref, base_ref, d0_ref, d1_ref,
):
    parts, nx, ny, depth = smoothed_ref.shape
    width, rows = nx + 2 * HALO, ny + 2 * HALO
    ncx, half = nx // 2, ny // 2
    cwidth, crows = ncx + 2 * COARSE_HALO, half + 2 * COARSE_HALO
    srows = source_ref.shape[2]
    at_x, at_y = lax.axis_index("gx"), lax.axis_index("gy")
    odd = is_odd("gy")
    has_left, has_right = at_x > 0, at_x < shape_x - 1
    has_low, has_high = at_y > 0, at_y < shape_y - 1
    sides = {"left": left_ref, "right": right_ref}
    constants = constants_of(lower_ref, upper_ref)
    first_scale, carried, scaled = constants

    def low_rows(row, count):
        here = pl.ds(row, count)
        return jnp.where(odd, same_ref[here, :], cross_ref[here, :])

    def high_rows(row, count):
        here = pl.ds(row, count)
        return jnp.where(odd, cross_ref[here, :], same_ref[here, :])

    def masked(inside, own, low, high):
        ok_low, ok_high = has_low, has_high
        if inside is not None:
            own = jnp.where(inside, own, 0.0)
            ok_low, ok_high = jnp.logical_and(ok_low, inside), jnp.logical_and(ok_high, inside)
        return own, jnp.where(ok_low, low, 0.0), jnp.where(ok_high, high, 0.0)

    insides = {"left": has_left, "own": None, "right": has_right}
    row = 0
    for f in range(4):
        shared = 2 if f == 3 else 1
        for i in range(cwidth // shared):
            side, at = coarse_spot(f, i, ncx)
            own = coarse_ref[f, at] if side == "own" else sides[side][at]
            low, high = low_rows(row, COARSE_HALO), high_rows(row, COARSE_HALO)
            own, low, high = masked(insides[side], own, low, high)
            field_ref[f, i, pl.ds(ROW0 + COARSE_HALO, half), :] = own
            field_ref[f, i, pl.ds(ROW0, COARSE_HALO), :] = low
            field_ref[f, i, pl.ds(ROW0 + COARSE_HALO + half, COARSE_HALO), :] = high
            field_ref[f, i, pl.ds(0, ROW0), :] = jnp.zeros((ROW0, depth), jnp.float32)
            tail = field_ref.shape[2] - ROW0 - crows
            field_ref[f, i, pl.ds(ROW0 + crows, tail), :] = jnp.zeros((tail, depth), jnp.float32)
            row += COARSE_HALO
    tiles = ny // half
    fine_base = 3 * COARSE_HALO + COARSE_HALO // 2
    for c in range(parts):
        for i in range(width):
            x = i - HALO
            if 0 <= x < nx:
                side = "own"
                own = smoothed_ref[c, x]
            else:
                side = "left" if x < 0 else "right"
                j = i if x < 0 else x - nx
                at = fine_base + (c * HALO + j) * tiles
                own = jnp.concatenate([sides[side][at + t] for t in range(tiles)], axis=0)
            own, low, high = masked(insides[side], own, low_rows(row, HALO), high_rows(row, HALO))
            residual_ref[c, i, pl.ds(HALO, ny), :] = own
            residual_ref[c, i, pl.ds(0, HALO), :] = low
            residual_ref[c, i, pl.ds(HALO + ny, HALO), :] = high
            row += HALO

    mid = pl.ds(ROW0, srows)
    lane = lanes(srows, depth)
    even = lane % 2 == 0

    def first_of(value):
        return jnp.where(even, value, below(value))

    def second_of(value):
        return jnp.where(even, above(value), value)

    even_low = lanes(field_ref.shape[2], depth) % 2 == 0
    for i in range(cwidth):
        packed = field_ref[3, i // 2, mid, :]
        inverse = first_of(packed) if i % 2 == 0 else second_of(packed)
        upper_x = second_of(field_ref[1, i, mid, :])
        faces_y = field_ref[2, i]
        upper_y = jnp.where(even_low, faces_y, below(faces_y))
        upper_z = second_of(field_ref[2, i, mid, :])
        source_ref[0, i] = field_ref[0, i, mid, :]
        source_ref[1, i] = first_of(field_ref[1, i, mid, :])
        if i > 0:
            cweight_ref[0, i] = second_of(field_ref[1, i - 1, mid, :]) * inverse
        cweight_ref[1, i] = upper_x * inverse
        cweight_ref[2, i] = upper_y[ROW0 - 1 : ROW0 - 1 + srows] * inverse
        cweight_ref[3, i] = upper_y[ROW0 : ROW0 + srows] * inverse
        cweight_ref[4, i] = jnp.where(lane < 2, 0.0, below(upper_z, 2) * inverse)
        cweight_ref[5, i] = jnp.where(lane >= depth - 2, 0.0, upper_z * inverse)

    clear_rims(cd0_ref, srows)
    clear_rims(cd1_ref, srows)

    for i in range(cwidth):
        for s in range(2):
            value = first_scale * source_ref[s, i]
            cd0_ref[s, i, mid, :] = value
            correction_ref[s, i] = value
    for number in range(COARSE_STEPS - 1):
        old, new = ((cd0_ref, cd1_ref), (cd1_ref, cd0_ref))[number % 2]
        last = number + 2 == COARSE_STEPS
        for i in range(number + 1, cwidth - 1 - number):
            weights = [cweight_ref[f, i] for f in range(6)]
            for s in range(2):
                own = old[s, i, mid, :]
                beside = weights[0] * old[s, i - 1, mid, :] + weights[1] * old[s, i + 1, mid, :]
                beside = beside + weights[2] * old[s, i, pl.ds(ROW0 - 1, srows), :]
                beside = beside + weights[3] * old[s, i, pl.ds(ROW0 + 1, srows), :]
                beside = beside + weights[4] * below(own, 2) + weights[5] * above(own, 2)
                fresh = source_ref[s, i] - own + beside
                direction = carried[number] * own + scaled[number] * fresh
                if not last:
                    source_ref[s, i] = fresh
                    new[s, i, mid, :] = direction
                correction_ref[s, i] = correction_ref[s, i] + direction

    edge = COARSE_HALO - COARSE_REACH
    pwidth, prows = ncx + 2 * COARSE_REACH, half + 2 * COARSE_REACH
    prow0 = ROW0 - (2 * COARSE_REACH - HALO)
    even_p = lanes(prows, depth) % 2 == 0
    for i in range(pwidth):
        pair = correction_ref[0, i + edge, pl.ds(edge, prows), :]
        single = correction_ref[1, i + edge, pl.ds(edge, prows), :]
        values = [
            jnp.where(even_p, pair, below(pair)),
            jnp.where(even_p, above(pair), pair),
            single,
        ]
        for c in range(parts):
            prolonged_ref[c, i, pl.ds(prow0, prows, 2), :] = values[c]
            prolonged_ref[c, i, pl.ds(prow0 + 1, prows, 2), :] = values[c]

    fine = pl.ds(ROW0, rows)
    shift = 2 * COARSE_REACH - HALO
    for i in range(width):
        weights = [weight_ref[f, i] for f in range(6)]
        at, before, after = (i + shift) // 2, (i + shift - 1) // 2, (i + shift + 1) // 2
        for c in range(parts):
            own = prolonged_ref[c, at, fine, :]
            beside = weights[0] * prolonged_ref[c, before, fine, :] + weights[1] * prolonged_ref[c, after, fine, :]
            beside = beside + weights[2] * prolonged_ref[c, at, pl.ds(ROW0 - 1, rows), :]
            beside = beside + weights[3] * prolonged_ref[c, at, pl.ds(ROW0 + 1, rows), :]
            beside = beside + weights[4] * below(own) + weights[5] * above(own)
            base_ref[c, i, fine, :] = residual_ref[c, i] - own + beside

    for ref in (base_ref, d0_ref, d1_ref):
        clear_rims(ref, rows)

    def finish(c, x, value):
        out_ref[c, x - HALO] = value * diagonal_ref[x - HALO]

    fine_steps(weight_ref, base_ref, residual_ref, (d0_ref, d1_ref), constants, width, finish)


def call(kernel, outs, scratch, specs):
    return pl.pallas_call(
        kernel,
        out_shape=[jax.ShapeDtypeStruct(shape, jnp.float32) for shape in outs],
        in_specs=[pl.BlockSpec(memory_space=space) for space in specs],
        out_specs=[pl.BlockSpec(memory_space=pltpu.VMEM) for _ in outs],
        scratch_shapes=[pltpu.VMEM(shape, jnp.float32) for shape in scratch],
        compiler_params=pltpu.CompilerParams(vmem_limit_bytes=VMEM_LIMIT),
    )


def ring_x(low, high):
    devices = lax.axis_size("gx")
    up = [(i, (i + 1) % devices) for i in range(devices)]
    down = [(j, i) for i, j in up]
    return lax.ppermute(high, "gx", up), lax.ppermute(low, "gx", down)


def swap_y(same, cross):
    devices = lax.axis_size("gy")
    pairs = [(i, i ^ 1) for i in range(devices)]
    others = [(0, 0), (devices - 1, devices - 1)]
    others = others + [(i, ((i + 1) ^ 1) - 1) for i in range(1, devices - 1)]
    return lax.ppermute(same, "gy", pairs), lax.ppermute(cross, "gy", others)


def up_to(value, unit):
    return -(-value // unit) * unit


def local(forcing, phase_index, visc_table, lower_bound, upper_bound):
    vmem, smem = pltpu.VMEM, pltpu.SMEM
    parts, nx, ny, depth = forcing.shape
    shape_x, shape_y = lax.axis_size("gx"), lax.axis_size("gy")
    width, rows = nx + 2 * HALO, ny + 2 * HALO
    ncx, half = nx // 2, ny // 2
    cwidth, crows = ncx + 2 * COARSE_HALO, half + 2 * COARSE_HALO
    srows = up_to(crows, 8)

    slab = (parts * HALO + VISC_HALO, ny, depth)
    low, high = call(pack_x_kernel, [slab, slab], [], [vmem, vmem, smem])(forcing, phase_index, visc_table)
    left, right = ring_x(low, high)

    count = up_to(parts * width * HALO + (nx + 2 * VISC_HALO) * VISC_HALO, 8)
    slab = (count, depth)
    same, cross = call(pack_y_kernel, [slab, slab], [], [vmem, vmem, smem, vmem, vmem])(
        forcing, phase_index, visc_table, left, right
    )
    same, cross = swap_y(same, cross)

    tiles = 3 * COARSE_HALO + COARSE_HALO // 2 + parts * HALO * (ny // half)
    slab = (tiles, half, depth)
    fine_d = (parts, width, rows + 2 * ROW0, depth)
    weight, diagonal, smoothed, coarse, low, high = call(
        functools.partial(pre_kernel, shape_x, shape_y),
        [(6, width, rows, depth), (nx, ny, depth), (parts, nx, ny, depth), (4, ncx, half, depth), slab, slab],
        [
            (nx + 2 * VISC_HALO, up_to(ny + 2 * VISC_HALO, 8), depth),
            (width, rows, depth),
            (parts, width, rows, depth),
            fine_d,
            fine_d,
            fine_d,
            (rows, depth),
            (6, up_to(ny + 2, 8), depth),
        ],
        [vmem, vmem, smem, smem, smem, vmem, vmem, vmem, vmem],
    )(forcing, phase_index, visc_table, lower_bound, upper_bound, left, right, same, cross)
    left, right = ring_x(low, high)

    count = up_to((3 * cwidth + cwidth // 2) * COARSE_HALO + parts * width * HALO, 8)
    slab = (count, depth)
    same, cross = call(pack_y2_kernel, [slab, slab], [], [vmem] * 4)(smoothed, coarse, left, right)
    same, cross = swap_y(same, cross)

    coarse_d = (2, cwidth, srows + 2 * ROW0, depth)
    (out,) = call(
        functools.partial(post_kernel, shape_x, shape_y),
        [(parts, nx, ny, depth)],
        [
            (4, cwidth, up_to(ROW0 + crows + 1, 8), depth),
            (6, cwidth, srows, depth),
            (2, cwidth, srows, depth),
            coarse_d,
            coarse_d,
            (2, cwidth, srows, depth),
            (parts, ncx + 2 * COARSE_REACH, rows + 2 * ROW0, depth),
            (parts, width, rows, depth),
            fine_d,
            fine_d,
            fine_d,
        ],
        [vmem, vmem, vmem, vmem, smem, smem, vmem, vmem, vmem, vmem],
    )(weight, diagonal, smoothed, coarse, lower_bound, upper_bound, left, right, same, cross)
    return out


def solution(mesh):
    in_specs = (P(None, "gx", "gy", None), P("gx", "gy", None), P(), P(), P())
    out_specs = P(None, "gx", "gy", None)
    return jax.shard_map(local, mesh=mesh, in_specs=in_specs, out_specs=out_specs, check_vma=False)
```

```python
import functools

import jax
import jax.numpy as jnp
from jax import lax
from jax.experimental import pallas as pl
from jax.experimental.pallas import tpu as pltpu
from jax.sharding import PartitionSpec as P

CHEB = 4
COARSE_STEPS = 4
HALO = CHEB
VISC_HALO = HALO + 1
COARSE_REACH = (HALO + 2) // 2
COARSE_HALO = COARSE_REACH + COARSE_STEPS - 1
ROW0 = 8
VMEM_LIMIT = 48 * 1024 * 1024


def chebyshev_constants(lower_value, upper_value, count):
    centre = 0.5 * (upper_value + lower_value)
    radius = 0.5 * (upper_value - lower_value)
    spread = centre / radius
    damping = 1.0 / spread
    carried = []
    scaled = []
    for number in range(count - 1):
        renewed = 1.0 / (2.0 * spread - damping)
        carried.append(renewed * damping)
        scaled.append(2.0 * renewed / radius)
        damping = renewed
    return (1.0 / centre, carried, scaled)


def constants_of(lower_ref, upper_ref):
    lower_value = jnp.full((1, 128), lower_ref[0], jnp.float32)
    upper_value = jnp.full((1, 128), upper_ref[0], jnp.float32)
    return chebyshev_constants(lower_value, upper_value, max(CHEB, COARSE_STEPS))


def lookup(table_ref, phases):
    viscosity = jnp.full(phases.shape, table_ref[0], jnp.float32)
    for table_row in range(1, table_ref.shape[0]):
        viscosity = jnp.where(phases == table_row, table_ref[table_row], viscosity)
    return viscosity


def lanes(rows, depth):
    return lax.broadcasted_iota(jnp.int32, (rows, depth), 1)


def below(value, by=1):
    return pltpu.roll(value, by, 1)


def above(value, by=1):
    return pltpu.roll(value, value.shape[1] - by, 1)


def is_odd(axis):
    return lax.rem(lax.axis_index(axis), 2) == 1


def pack_x_kernel(forcing_ref, phase_ref, table_ref, low_ref, high_ref, phases_ref, rows_ref, sems):
    parts, nx = forcing_ref.shape[:2]
    base = parts * HALO
    sides = ((low_ref, 0, 0), (high_ref, nx - HALO, nx - VISC_HALO))
    first_copies, copies = [pltpu.make_async_copy(table_ref, rows_ref, sems.at[2, 0])], []
    for s, (ref, x, visc_x) in enumerate(sides):
        source = phase_ref.at[pl.ds(visc_x, VISC_HALO)]
        first_copies.append(pltpu.make_async_copy(source, phases_ref.at[s], sems.at[s, parts]))
        for c in range(parts):
            source, target = forcing_ref.at[c, pl.ds(x, HALO)], ref.at[pl.ds(c * HALO, HALO)]
            copies.append(pltpu.make_async_copy(source, target, sems.at[s, c]))
    for copy in first_copies + copies:
        copy.start()
    for copy in first_copies:
        copy.wait()
    for s, (ref, _, _) in enumerate(sides):
        for i in range(VISC_HALO):
            ref[base + i] = lookup(rows_ref, phases_ref[s, i])
    for copy in copies:
        copy.wait()


def stage_kernel(forcing_ref, phase_ref, table_ref, here_ref, visc_ref, phases_ref, rows_ref, sems):
    first_copies = [
        pltpu.make_async_copy(table_ref, rows_ref, sems.at[0]),
        pltpu.make_async_copy(phase_ref, phases_ref, sems.at[1]),
    ]
    copy = pltpu.make_async_copy(forcing_ref, here_ref, sems.at[2])
    for each in first_copies + [copy]:
        each.start()
    for each in first_copies:
        each.wait()
    for x in range(phase_ref.shape[0]):
        visc_ref[x] = lookup(rows_ref, phases_ref[x])
    copy.wait()


def row_plan(length, halo, shared=1):
    plan, row = [], 0
    for start in range(-halo, length + halo, shared):
        away = min(max(-x, x - length + 1, 0) for x in range(start, start + shared))
        plan.append((start, row, halo - away))
        row += halo - away
    return plan, row


def place(plane, first, inner, halo, own, low, high):
    count = low.shape[0] if low is not None else 0
    plane(first + halo, own)
    if count:
        plane(first + halo - count, low)
        plane(first + halo + inner, high)
    if count < halo:
        empty = jnp.zeros((halo - count, own.shape[1]), jnp.float32)
        plane(first, empty)
        plane(first + halo + inner + count, empty)


def writer(ref, *at):
    def store(row, value):
        ref[at + (pl.ds(row, value.shape[0]), slice(None))] = value

    return store


def message_reader(same_ref, cross_ref):
    odd = is_odd("gy")

    def low_and_high(row, count):
        if count == 0:
            return None, None
        same, cross = same_ref[pl.ds(row, count), :], cross_ref[pl.ds(row, count), :]
        return jnp.where(odd, same, cross), jnp.where(odd, cross, same)

    return low_and_high


def message_writer(same_ref, cross_ref):
    odd = is_odd("gy")

    def put(row, count, ref, at, ref_high=None, at_high=None):
        if count == 0:
            return
        ref_high, at_high = (ref, at) if ref_high is None else (ref_high, at_high)
        length = ref_high.shape[-2]
        low = ref[at + (pl.ds(0, count), slice(None))]
        high = ref_high[at_high + (pl.ds(length - count, count), slice(None))]
        same_ref[pl.ds(row, count), :] = jnp.where(odd, low, high)
        cross_ref[pl.ds(row, count), :] = jnp.where(odd, high, low)

    return put


def pack_y_kernel(forcing_ref, visc_ref, left_ref, right_ref, same_ref, cross_ref):
    parts, nx = forcing_ref.shape[:2]
    put = message_writer(same_ref, cross_ref)
    plan, total = row_plan(nx, HALO)
    for c in range(parts):
        for x, row, count in plan:
            if x < 0:
                put(c * total + row, count, left_ref, (c * HALO + x + HALO,))
            elif x < nx:
                put(c * total + row, count, forcing_ref, (c, x))
            else:
                put(c * total + row, count, right_ref, (c * HALO + x - nx,))
    for x, row, count in row_plan(nx, VISC_HALO)[0]:
        if x < 0:
            put(parts * total + row, count, left_ref, (parts * HALO + x + VISC_HALO,))
        elif x < nx:
            put(parts * total + row, count, visc_ref, (x,))
        else:
            put(parts * total + row, count, right_ref, (parts * HALO + x - nx,))


def fine_steps(weight_ref, base_ref, residual_ref, d_refs, constants, width, finish):
    first_scale, carried, scaled = constants
    parts, rows = residual_ref.shape[0], residual_ref.shape[2]
    for number in range(CHEB):
        old = base_ref if number == 0 else d_refs[number % 2]
        new = d_refs[(number + 1) % 2]
        last = number + 1 == CHEB
        skip, count = (HALO, rows - 2 * HALO) if last else (0, rows)
        inner = pl.ds(skip, count)
        for x in range(number + 1, width - 1 - number):
            weights = [weight_ref[f, x, inner, :] for f in range(6)]
            for c in range(parts):
                own = old[c, x, pl.ds(ROW0 + skip, count), :]
                beside = weights[0] * old[c, x - 1, pl.ds(ROW0 + skip, count), :]
                beside = beside + weights[1] * old[c, x + 1, pl.ds(ROW0 + skip, count), :]
                beside = beside + weights[2] * old[c, x, pl.ds(ROW0 + skip - 1, count), :]
                beside = beside + weights[3] * old[c, x, pl.ds(ROW0 + skip + 1, count), :]
                beside = beside + weights[4] * below(own) + weights[5] * above(own)
                if number == 0:
                    fresh = own - first_scale * (own - beside)
                    own = first_scale * own
                else:
                    fresh = residual_ref[c, x, inner, :] - own + beside
                if last:
                    finish(c, x, fresh)
                else:
                    residual_ref[c, x] = fresh
                    new[c, x, pl.ds(ROW0, rows), :] = carried[number] * own + scaled[number] * fresh


def masked(inside, has_low, has_high, own, low, high):
    if inside is not None:
        own = jnp.where(inside, own, 0.0)
        has_low, has_high = jnp.logical_and(has_low, inside), jnp.logical_and(has_high, inside)
    if low is not None:
        low, high = jnp.where(has_low, low, 0.0), jnp.where(has_high, high, 0.0)
    return own, low, high


def pre_kernel(
    shape_x,
    shape_y,
    forcing_ref, own_visc_ref, lower_ref, upper_ref, left_ref, right_ref, same_ref, cross_ref,
    weight_ref, diagonal_ref, smoothed_ref, coarse_ref, low_ref, high_ref,
    visc_ref, inverse_ref, residual_ref, base_ref, d0_ref, d1_ref, pair_ref, row_ref,
):
    parts, nx, ny, depth = forcing_ref.shape
    width, rows = nx + 2 * HALO, ny + 2 * HALO
    at_x, at_y = lax.axis_index("gx"), lax.axis_index("gy")
    has_left, has_right = at_x > 0, at_x < shape_x - 1
    has_low, has_high = at_y > 0, at_y < shape_y - 1
    low_and_high = message_reader(same_ref, cross_ref)
    fine_plan, fine_total = row_plan(nx, HALO)

    for x, row, count in row_plan(nx, VISC_HALO)[0]:
        if x < 0:
            own = left_ref[parts * HALO + x + VISC_HALO]
            inside = has_left
        elif x < nx:
            own = own_visc_ref[x]
            inside = None
        else:
            own = right_ref[parts * HALO + x - nx]
            inside = has_right
        low, high = low_and_high(parts * fine_total + row, count)
        own, low, high = masked(inside, has_low, has_high, own, low, high)
        place(writer(visc_ref, x + VISC_HALO), 0, ny, VISC_HALO, own, low, high)

    lane = lanes(rows, depth)

    for x in range(width):
        centre = visc_ref[x + 1, pl.ds(1, rows), :]
        halved = 0.5 * centre
        z_below = jnp.where(lane == 0, 0.0, below(halved))
        z_above = jnp.where(lane == depth - 1, 0.0, above(halved))
        faces = [
            halved + 0.5 * visc_ref[x, pl.ds(1, rows), :],
            halved + 0.5 * visc_ref[x + 2, pl.ds(1, rows), :],
            halved + 0.5 * visc_ref[x + 1, pl.ds(0, rows), :],
            halved + 0.5 * visc_ref[x + 1, pl.ds(2, rows), :],
            halved + z_below,
            halved + z_above,
        ]
        diagonal = faces[0] + faces[1] + faces[2] + faces[3] + faces[4] + faces[5]
        inside = centre > 0.0
        inverse = jnp.where(inside, 1.0 / jnp.where(inside, diagonal, 1.0), 0.0)
        for f in range(4):
            weight_ref[f, x] = faces[f] * inverse
        weight_ref[4, x] = jnp.where(lane == 0, 0.0, faces[4] * inverse)
        weight_ref[5, x] = jnp.where(lane == depth - 1, 0.0, faces[5] * inverse)
        inverse_ref[x] = inverse
        if HALO <= x < HALO + nx:
            pair_ref[...] = diagonal
            diagonal_ref[x - HALO] = pair_ref[pl.ds(HALO, ny), :]

    for c in range(parts):
        for x, row, count in fine_plan:
            i = x + HALO
            if x < 0:
                own = left_ref[c * HALO + i]
            elif x < nx:
                own = forcing_ref[c, x]
            else:
                own = right_ref[c * HALO + x - nx]
            low, high = low_and_high(c * fine_total + row, count)
            own = own * inverse_ref[i, pl.ds(HALO, ny), :]
            if count:
                low = low * inverse_ref[i, pl.ds(HALO - count, count), :]
                high = high * inverse_ref[i, pl.ds(HALO + ny, count), :]
            place(writer(base_ref, c, i), ROW0, ny, HALO, own, low, high)

    def finish(c, x, value):
        smoothed_ref[c, x - HALO] = value

    constants = constants_of(lower_ref, upper_ref)
    fine_steps(weight_ref, base_ref, residual_ref, (d0_ref, d1_ref), constants, width, finish)

    half = ny // 2
    even_own = lanes(ny, depth) % 2 == 0
    even_wide = lanes(ny + 2, depth) % 2 == 0
    even = lanes(half, depth) % 2 == 0
    lane_half = lanes(half, depth)

    def z_pair(value, even_mask):
        return value + jnp.where(even_mask, above(value), below(value))

    def y_sum(value, slot):
        row_ref[slot, pl.ds(0, value.shape[0]), :] = value
        return row_ref[slot, pl.ds(0, half, 2), :] + row_ref[slot, pl.ds(1, half, 2), :]

    def visc_own(x):
        return visc_ref[x + VISC_HALO, pl.ds(VISC_HALO, ny), :]

    inverses = []
    for i in range(nx // 2):
        faces_x = []
        for x in (2 * i - 1, 2 * i, 2 * i + 1, 2 * i + 2):
            faces_x.append(y_sum(z_pair(visc_own(x), even_own), 0))
        lower_x = faces_x[0] + faces_x[1]
        upper_x = faces_x[2] + faces_x[3]
        wide = pl.ds(VISC_HALO - 1, ny + 2)
        both = visc_ref[2 * i + VISC_HALO, wide, :] + visc_ref[2 * i + 1 + VISC_HALO, wide, :]
        row_ref[1, pl.ds(0, ny + 2), :] = z_pair(both, even_wide)
        picks = [row_ref[1, pl.ds(start, half, 2), :] for start in range(4)]
        lower_y = picks[0] + picks[1]
        upper_y = picks[2] + picks[3]
        column = y_sum(both[1 : ny + 1], 2)
        lower_z = column + jnp.where(lane_half == 0, 0.0, below(column))
        lower_z = jnp.where(even, lower_z, below(lower_z))
        upper_z = column + jnp.where(lane_half == depth - 1, 0.0, above(column))
        upper_z = jnp.where(even, above(upper_z), upper_z)
        inverse = 1.0 / (lower_x + upper_x + lower_y + upper_y + lower_z + upper_z)
        inverses.append(32.0 * inverse)
        sources = []
        for c in range(parts):
            total = 0.0
            for x in (2 * i, 2 * i + 1):
                total = total + smoothed_ref[c, x] * diagonal_ref[x]
            sources.append(y_sum(z_pair(total, even_own), 3 + c) * (4.0 * inverse))
        faces = [upper_x * (1.0 / 32.0), upper_y * (1.0 / 32.0), upper_z * (1.0 / 32.0)]
        coarse_ref[0, i] = jnp.where(even, sources[0], sources[1])
        coarse_ref[1, i] = jnp.where(even, sources[2], faces[0])
        coarse_ref[2, i] = jnp.where(even, faces[1], faces[2])
        if i % 2 == 1:
            coarse_ref[3, i // 2] = jnp.where(even, inverses[i - 1], inverses[i])

    at = 0
    ncx = nx // 2
    for f in range(4):
        shared = 2 if f == 3 else 1
        count = COARSE_HALO // shared
        for i in range(count):
            low_ref[at] = coarse_ref[f, i]
            high_ref[at] = coarse_ref[f, ncx // shared - count + i]
            at += 1
    tiles = ny // half
    for c in range(parts):
        for i in range(HALO):
            for t in range(tiles):
                low_ref[at] = smoothed_ref[c, i, pl.ds(t * half, half), :]
                high_ref[at] = smoothed_ref[c, nx - HALO + i, pl.ds(t * half, half), :]
                at += 1


def coarse_spot(f, i, ncx):
    shared = 2 if f == 3 else 1
    count, own = COARSE_HALO // shared, ncx // shared
    base = f * COARSE_HALO
    if i < count:
        return "left", base + i
    if i < count + own:
        return "own", i - count
    return "right", base + i - count - own


def pack_y2_kernel(smoothed_ref, coarse_ref, left_ref, right_ref, same_ref, cross_ref):
    parts, nx, ny = smoothed_ref.shape[:3]
    ncx, half = nx // 2, ny // 2
    sides = {"left": left_ref, "right": right_ref}
    put = message_writer(same_ref, cross_ref)
    base = 0
    for f in range(4):
        shared = 2 if f == 3 else 1
        plan, total = row_plan(ncx, COARSE_HALO, shared)
        for i, (_, row, count) in enumerate(plan):
            side, at = coarse_spot(f, i, ncx)
            if side == "own":
                put(base + row, count, coarse_ref, (f, at))
            else:
                put(base + row, count, sides[side], (at,))
        base += total
    tiles = ny // half
    fine_base = 3 * COARSE_HALO + COARSE_HALO // 2
    plan, total = row_plan(nx, HALO)
    for c in range(parts):
        for x, row, count in plan:
            if 0 <= x < nx:
                put(base + row, count, smoothed_ref, (c, x))
            else:
                ref = left_ref if x < 0 else right_ref
                i = x + HALO if x < 0 else x - nx
                at = fine_base + (c * HALO + i) * tiles
                put(base + row, count, ref, (at,), ref, (at + tiles - 1,))
        base += total


def post_kernel(
    shape_x,
    shape_y,
    weight_ref, diagonal_ref, smoothed_ref, coarse_ref, lower_ref, upper_ref, left_ref, right_ref, same_ref, cross_ref,
    out_ref,
    field_ref, cweight_ref, source_ref, cd0_ref, cd1_ref, correction_ref, prolonged_ref, residual_ref, base_ref, d0_ref, d1_ref,
):
    parts, nx, ny, depth = smoothed_ref.shape
    width, rows = nx + 2 * HALO, ny + 2 * HALO
    ncx, half = nx // 2, ny // 2
    cwidth, crows = ncx + 2 * COARSE_HALO, half + 2 * COARSE_HALO
    srows = source_ref.shape[2]
    at_x, at_y = lax.axis_index("gx"), lax.axis_index("gy")
    has_left, has_right = at_x > 0, at_x < shape_x - 1
    has_low, has_high = at_y > 0, at_y < shape_y - 1
    sides = {"left": left_ref, "right": right_ref}
    insides = {"left": has_left, "own": None, "right": has_right}
    low_and_high = message_reader(same_ref, cross_ref)
    constants = constants_of(lower_ref, upper_ref)
    first_scale, carried, scaled = constants

    base = 0
    tail = field_ref.shape[2] - ROW0 - crows
    for f in range(4):
        shared = 2 if f == 3 else 1
        plan, total = row_plan(ncx, COARSE_HALO, shared)
        for i, (_, row, count) in enumerate(plan):
            side, at = coarse_spot(f, i, ncx)
            own = coarse_ref[f, at] if side == "own" else sides[side][at]
            low, high = low_and_high(base + row, count)
            own, low, high = masked(insides[side], has_low, has_high, own, low, high)
            place(writer(field_ref, f, i), ROW0, half, COARSE_HALO, own, low, high)
            field_ref[f, i, pl.ds(0, ROW0), :] = jnp.zeros((ROW0, depth), jnp.float32)
            field_ref[f, i, pl.ds(ROW0 + crows, tail), :] = jnp.zeros((tail, depth), jnp.float32)
        base += total
    tiles = ny // half
    fine_base = 3 * COARSE_HALO + COARSE_HALO // 2
    plan, total = row_plan(nx, HALO)
    for c in range(parts):
        for i, (x, row, count) in enumerate(plan):
            if 0 <= x < nx:
                side = "own"
                own = smoothed_ref[c, x]
            else:
                side = "left" if x < 0 else "right"
                j = i if x < 0 else x - nx
                at = fine_base + (c * HALO + j) * tiles
                own = jnp.concatenate([sides[side][at + t] for t in range(tiles)], axis=0)
            low, high = low_and_high(base + row, count)
            own, low, high = masked(insides[side], has_low, has_high, own, low, high)
            place(writer(residual_ref, c, i), 0, ny, HALO, own, low, high)
        base += total

    mid = pl.ds(ROW0, srows)
    lane = lanes(srows, depth)
    even = lane % 2 == 0

    def first_of(value):
        return jnp.where(even, value, below(value))

    def second_of(value):
        return jnp.where(even, above(value), value)

    even_low = lanes(field_ref.shape[2], depth) % 2 == 0
    for i in range(cwidth):
        packed = field_ref[3, i // 2, mid, :]
        inverse = first_of(packed) if i % 2 == 0 else second_of(packed)
        upper_x = second_of(field_ref[1, i, mid, :])
        faces_y = field_ref[2, i]
        upper_y = jnp.where(even_low, faces_y, below(faces_y))
        upper_z = second_of(field_ref[2, i, mid, :])
        source_ref[0, i] = field_ref[0, i, mid, :]
        source_ref[1, i] = first_of(field_ref[1, i, mid, :])
        if i > 0:
            cweight_ref[0, i] = second_of(field_ref[1, i - 1, mid, :]) * inverse
        cweight_ref[1, i] = upper_x * inverse
        cweight_ref[2, i] = upper_y[ROW0 - 1 : ROW0 - 1 + srows] * inverse
        cweight_ref[3, i] = upper_y[ROW0 : ROW0 + srows] * inverse
        cweight_ref[4, i] = jnp.where(lane < 2, 0.0, below(upper_z, 2) * inverse)
        cweight_ref[5, i] = jnp.where(lane >= depth - 2, 0.0, upper_z * inverse)

    for i in range(cwidth):
        for s in range(2):
            value = first_scale * source_ref[s, i]
            cd0_ref[s, i, mid, :] = value
            correction_ref[s, i] = value
    for number in range(COARSE_STEPS - 1):
        old, new = ((cd0_ref, cd1_ref), (cd1_ref, cd0_ref))[number % 2]
        last = number + 2 == COARSE_STEPS
        for i in range(number + 1, cwidth - 1 - number):
            weights = [cweight_ref[f, i] for f in range(6)]
            for s in range(2):
                own = old[s, i, mid, :]
                beside = weights[0] * old[s, i - 1, mid, :] + weights[1] * old[s, i + 1, mid, :]
                beside = beside + weights[2] * old[s, i, pl.ds(ROW0 - 1, srows), :]
                beside = beside + weights[3] * old[s, i, pl.ds(ROW0 + 1, srows), :]
                beside = beside + weights[4] * below(own, 2) + weights[5] * above(own, 2)
                fresh = source_ref[s, i] - own + beside
                direction = carried[number] * own + scaled[number] * fresh
                if not last:
                    source_ref[s, i] = fresh
                    new[s, i, mid, :] = direction
                correction_ref[s, i] = correction_ref[s, i] + direction

    edge = COARSE_HALO - COARSE_REACH
    pwidth, prows = ncx + 2 * COARSE_REACH, half + 2 * COARSE_REACH
    prow0 = ROW0 - (2 * COARSE_REACH - HALO)
    even_p = lanes(prows, depth) % 2 == 0
    for i in range(pwidth):
        pair = correction_ref[0, i + edge, pl.ds(edge, prows), :]
        single = correction_ref[1, i + edge, pl.ds(edge, prows), :]
        values = [
            jnp.where(even_p, pair, below(pair)),
            jnp.where(even_p, above(pair), pair),
            single,
        ]
        for c in range(parts):
            prolonged_ref[c, i, pl.ds(prow0, prows, 2), :] = values[c]
            prolonged_ref[c, i, pl.ds(prow0 + 1, prows, 2), :] = values[c]

    fine = pl.ds(ROW0, rows)
    shift = 2 * COARSE_REACH - HALO
    for i in range(width):
        weights = [weight_ref[f, i] for f in range(6)]
        at, before, after = (i + shift) // 2, (i + shift - 1) // 2, (i + shift + 1) // 2
        for c in range(parts):
            own = prolonged_ref[c, at, fine, :]
            beside = weights[0] * prolonged_ref[c, before, fine, :] + weights[1] * prolonged_ref[c, after, fine, :]
            beside = beside + weights[2] * prolonged_ref[c, at, pl.ds(ROW0 - 1, rows), :]
            beside = beside + weights[3] * prolonged_ref[c, at, pl.ds(ROW0 + 1, rows), :]
            beside = beside + weights[4] * below(own) + weights[5] * above(own)
            base_ref[c, i, fine, :] = residual_ref[c, i] - own + beside

    def finish(c, x, value):
        out_ref[c, x - HALO] = value * diagonal_ref[x - HALO]

    fine_steps(weight_ref, base_ref, residual_ref, (d0_ref, d1_ref), constants, width, finish)


def call(kernel, outs, scratch, specs):
    return pl.pallas_call(
        kernel,
        out_shape=[jax.ShapeDtypeStruct(shape, jnp.float32) for shape in outs],
        in_specs=[pl.BlockSpec(memory_space=space) for space in specs],
        out_specs=[pl.BlockSpec(memory_space=pltpu.VMEM) for _ in outs],
        scratch_shapes=[pltpu.VMEM(shape, jnp.float32) if isinstance(shape, tuple) else shape for shape in scratch],
        compiler_params=pltpu.CompilerParams(vmem_limit_bytes=VMEM_LIMIT),
    )


def ring_x(low, high):
    devices = lax.axis_size("gx")
    up = [(i, (i + 1) % devices) for i in range(devices)]
    down = [(j, i) for i, j in up]
    return lax.ppermute(high, "gx", up), lax.ppermute(low, "gx", down)


def swap_y(same, cross):
    devices = lax.axis_size("gy")
    pairs = [(i, i ^ 1) for i in range(devices)]
    others = [(0, 0), (devices - 1, devices - 1)]
    others = others + [(i, ((i + 1) ^ 1) - 1) for i in range(1, devices - 1)]
    return lax.ppermute(same, "gy", pairs), lax.ppermute(cross, "gy", others)


def in_hbm(value):
    return pltpu.with_memory_space_constraint(value, pltpu.HBM)


def up_to(value, unit):
    return -(-value // unit) * unit


def local(forcing, phase_index, visc_table, lower_bound, upper_bound):
    vmem, smem = pltpu.VMEM, pltpu.SMEM
    parts, nx, ny, depth = forcing.shape
    shape_x, shape_y = lax.axis_size("gx"), lax.axis_size("gy")
    width, rows = nx + 2 * HALO, ny + 2 * HALO
    ncx, half = nx // 2, ny // 2
    cwidth, crows = ncx + 2 * COARSE_HALO, half + 2 * COARSE_HALO
    srows = up_to(crows, 8)

    slab = (parts * HALO + VISC_HALO, ny, depth)
    semaphores = pltpu.SemaphoreType.DMA
    table_rows = pltpu.SMEM(visc_table.shape, jnp.float32)
    scratch = [pltpu.VMEM((2, VISC_HALO, ny, depth), jnp.int32), table_rows, semaphores((3, parts + 1))]
    low, high = call(pack_x_kernel, [slab, slab], scratch, [pltpu.HBM] * 3)(
        in_hbm(forcing), in_hbm(phase_index), in_hbm(visc_table)
    )
    left, right = ring_x(low, high)
    scratch = [pltpu.VMEM((nx, ny, depth), jnp.int32), table_rows, semaphores((3,))]
    forcing, viscosity = call(stage_kernel, [forcing.shape, (nx, ny, depth)], scratch, [pltpu.HBM] * 3)(
        in_hbm(forcing), in_hbm(phase_index), in_hbm(visc_table)
    )

    slab = (up_to(parts * row_plan(nx, HALO)[1] + row_plan(nx, VISC_HALO)[1], 8), depth)
    same, cross = call(pack_y_kernel, [slab, slab], [], [vmem] * 4)(forcing, viscosity, left, right)
    same, cross = swap_y(same, cross)

    tiles = 3 * COARSE_HALO + COARSE_HALO // 2 + parts * HALO * (ny // half)
    slab = (tiles, half, depth)
    fine_d = (parts, width, rows + 2 * ROW0, depth)
    weight, diagonal, smoothed, coarse, low, high = call(
        functools.partial(pre_kernel, shape_x, shape_y),
        [(6, width, rows, depth), (nx, ny, depth), (parts, nx, ny, depth), (4, ncx, half, depth), slab, slab],
        [
            (nx + 2 * VISC_HALO, up_to(ny + 2 * VISC_HALO, 8), depth),
            (width, rows, depth),
            (parts, width, rows, depth),
            fine_d,
            fine_d,
            fine_d,
            (rows, depth),
            (6, up_to(ny + 2, 8), depth),
        ],
        [vmem, vmem, smem, smem, vmem, vmem, vmem, vmem],
    )(forcing, viscosity, lower_bound, upper_bound, left, right, same, cross)
    left, right = ring_x(low, high)

    count = 3 * row_plan(ncx, COARSE_HALO)[1] + row_plan(ncx, COARSE_HALO, 2)[1] + parts * row_plan(nx, HALO)[1]
    slab = (up_to(count, 8), depth)
    same, cross = call(pack_y2_kernel, [slab, slab], [], [vmem] * 4)(smoothed, coarse, left, right)
    same, cross = swap_y(same, cross)

    coarse_d = (2, cwidth, srows + 2 * ROW0, depth)
    (out,) = call(
        functools.partial(post_kernel, shape_x, shape_y),
        [(parts, nx, ny, depth)],
        [
            (4, cwidth, up_to(ROW0 + crows + 1, 8), depth),
            (6, cwidth, srows, depth),
            (2, cwidth, srows, depth),
            coarse_d,
            coarse_d,
            (2, cwidth, srows, depth),
            (parts, ncx + 2 * COARSE_REACH, rows + 2 * ROW0, depth),
            (parts, width, rows, depth),
            fine_d,
            fine_d,
            fine_d,
        ],
        [vmem, vmem, vmem, vmem, smem, smem, vmem, vmem, vmem, vmem],
    )(weight, diagonal, smoothed, coarse, lower_bound, upper_bound, left, right, same, cross)
    return out


def solution(mesh):
    in_specs = (P(None, "gx", "gy", None), P("gx", "gy", None), P(), P(), P())
    out_specs = P(None, "gx", "gy", None)
    return jax.shard_map(local, mesh=mesh, in_specs=in_specs, out_specs=out_specs, check_vma=False)
```

```python
import functools

import jax
import jax.numpy as jnp
from jax import lax
from jax.experimental import pallas as pl
from jax.experimental.pallas import tpu as pltpu
from jax.sharding import PartitionSpec as P

CHEB = 4
COARSE_STEPS = 4
HALO = CHEB
VISC_HALO = HALO + 1
COARSE_REACH = (HALO + 2) // 2
COARSE_HALO = COARSE_REACH + COARSE_STEPS - 1
ROW0 = 8
VMEM_LIMIT = 48 * 1024 * 1024


def chebyshev_constants(lower_value, upper_value, count):
    centre = 0.5 * (upper_value + lower_value)
    radius = 0.5 * (upper_value - lower_value)
    spread = centre / radius
    damping = 1.0 / spread
    carried = []
    scaled = []
    for number in range(count - 1):
        renewed = 1.0 / (2.0 * spread - damping)
        carried.append(renewed * damping)
        scaled.append(2.0 * renewed / radius)
        damping = renewed
    return (1.0 / centre, carried, scaled)


def constants_of(lower_ref, upper_ref):
    lower_value = jnp.full((1, 128), lower_ref[0], jnp.float32)
    upper_value = jnp.full((1, 128), upper_ref[0], jnp.float32)
    return chebyshev_constants(lower_value, upper_value, max(CHEB, COARSE_STEPS))


def lookup(table_ref, phases):
    viscosity = jnp.full(phases.shape, table_ref[0], jnp.float32)
    for table_row in range(1, table_ref.shape[0]):
        viscosity = jnp.where(phases == table_row, table_ref[table_row], viscosity)
    return viscosity


def lanes(rows, depth):
    return lax.broadcasted_iota(jnp.int32, (rows, depth), 1)


def below(value, by=1):
    return pltpu.roll(value, by, 1)


def above(value, by=1):
    return pltpu.roll(value, value.shape[1] - by, 1)


def is_odd(axis):
    return lax.rem(lax.axis_index(axis), 2) == 1


def pack_x_kernel(forcing_ref, phase_ref, table_ref, low_ref, high_ref, phases_ref, rows_ref, sems):
    parts, nx = forcing_ref.shape[:2]
    base = parts * HALO
    sides = ((low_ref, 0, 0), (high_ref, nx - HALO, nx - VISC_HALO))
    first_copies, copies = [pltpu.make_async_copy(table_ref, rows_ref, sems.at[2, 0])], []
    for s, (ref, x, visc_x) in enumerate(sides):
        source = phase_ref.at[pl.ds(visc_x, VISC_HALO)]
        first_copies.append(pltpu.make_async_copy(source, phases_ref.at[s], sems.at[s, parts]))
        for c in range(parts):
            source, target = forcing_ref.at[c, pl.ds(x, HALO)], ref.at[pl.ds(c * HALO, HALO)]
            copies.append(pltpu.make_async_copy(source, target, sems.at[s, c]))
    for copy in first_copies + copies:
        copy.start()
    for copy in first_copies:
        copy.wait()
    for s, (ref, _, _) in enumerate(sides):
        for i in range(VISC_HALO):
            ref[base + i] = lookup(rows_ref, phases_ref[s, i])
    for copy in copies:
        copy.wait()


def stage_kernel(forcing_ref, phase_ref, table_ref, here_ref, visc_ref, phases_ref, rows_ref, sems):
    first_copies = [
        pltpu.make_async_copy(table_ref, rows_ref, sems.at[0]),
        pltpu.make_async_copy(phase_ref, phases_ref, sems.at[1]),
    ]
    copy = pltpu.make_async_copy(forcing_ref, here_ref, sems.at[2])
    for each in first_copies + [copy]:
        each.start()
    for each in first_copies:
        each.wait()
    for x in range(phase_ref.shape[0]):
        visc_ref[x] = lookup(rows_ref, phases_ref[x])
    copy.wait()


def row_plan(length, halo, shared=1):
    plan, row = [], 0
    for start in range(-halo, length + halo, shared):
        away = min(max(-x, x - length + 1, 0) for x in range(start, start + shared))
        plan.append((start, row, halo - away))
        row += halo - away
    return plan, row


def place(plane, first, inner, halo, own, low, high):
    count = low.shape[0] if low is not None else 0
    plane(first + halo, own)
    if count:
        plane(first + halo - count, low)
        plane(first + halo + inner, high)
    if count < halo:
        empty = jnp.zeros((halo - count, own.shape[1]), jnp.float32)
        plane(first, empty)
        plane(first + halo + inner + count, empty)


def writer(ref, *at):
    def store(row, value):
        ref[at + (pl.ds(row, value.shape[0]), slice(None))] = value

    return store


def message_reader(same_ref, cross_ref):
    odd = is_odd("gy")

    def low_and_high(row, count):
        if count == 0:
            return None, None
        same, cross = same_ref[pl.ds(row, count), :], cross_ref[pl.ds(row, count), :]
        return jnp.where(odd, same, cross), jnp.where(odd, cross, same)

    return low_and_high


def message_writer(same_ref, cross_ref):
    odd = is_odd("gy")

    def put(row, count, ref, at, ref_high=None, at_high=None):
        if count == 0:
            return
        ref_high, at_high = (ref, at) if ref_high is None else (ref_high, at_high)
        length = ref_high.shape[-2]
        low = ref[at + (pl.ds(0, count), slice(None))]
        high = ref_high[at_high + (pl.ds(length - count, count), slice(None))]
        same_ref[pl.ds(row, count), :] = jnp.where(odd, low, high)
        cross_ref[pl.ds(row, count), :] = jnp.where(odd, high, low)

    return put


def pack_y_kernel(forcing_ref, visc_ref, left_ref, right_ref, same_ref, cross_ref):
    parts, nx = forcing_ref.shape[:2]
    put = message_writer(same_ref, cross_ref)
    plan, total = row_plan(nx, HALO)
    for c in range(parts):
        for x, row, count in plan:
            if x < 0:
                put(c * total + row, count, left_ref, (c * HALO + x + HALO,))
            elif x < nx:
                put(c * total + row, count, forcing_ref, (c, x))
            else:
                put(c * total + row, count, right_ref, (c * HALO + x - nx,))
    for x, row, count in row_plan(nx, VISC_HALO)[0]:
        if x < 0:
            put(parts * total + row, count, left_ref, (parts * HALO + x + VISC_HALO,))
        elif x < nx:
            put(parts * total + row, count, visc_ref, (x,))
        else:
            put(parts * total + row, count, right_ref, (parts * HALO + x - nx,))


def fine_steps(weight_ref, base_ref, residual_ref, d_refs, constants, width, finish):
    first_scale, carried, scaled = constants
    parts, rows = residual_ref.shape[0], residual_ref.shape[2]
    for number in range(CHEB):
        old = base_ref if number == 0 else d_refs[number % 2]
        new = d_refs[(number + 1) % 2]
        last = number + 1 == CHEB
        skip, count = (HALO, rows - 2 * HALO) if last else (0, rows)
        inner = pl.ds(skip, count)
        for x in range(number + 1, width - 1 - number):
            weights = [weight_ref[f, x, inner, :] for f in range(6)]
            for c in range(parts):
                own = old[c, x, pl.ds(ROW0 + skip, count), :]
                beside = weights[0] * old[c, x - 1, pl.ds(ROW0 + skip, count), :]
                beside = beside + weights[1] * old[c, x + 1, pl.ds(ROW0 + skip, count), :]
                beside = beside + weights[2] * old[c, x, pl.ds(ROW0 + skip - 1, count), :]
                beside = beside + weights[3] * old[c, x, pl.ds(ROW0 + skip + 1, count), :]
                beside = beside + weights[4] * below(own) + weights[5] * above(own)
                if number == 0:
                    fresh = own - first_scale * (own - beside)
                    own = first_scale * own
                else:
                    fresh = residual_ref[c, x, inner, :] - own + beside
                if last:
                    finish(c, x, fresh)
                else:
                    residual_ref[c, x] = fresh
                    new[c, x, pl.ds(ROW0, rows), :] = carried[number] * own + scaled[number] * fresh


def masked(inside, has_low, has_high, own, low, high):
    if inside is not None:
        own = jnp.where(inside, own, 0.0)
        has_low, has_high = jnp.logical_and(has_low, inside), jnp.logical_and(has_high, inside)
    if low is not None:
        low, high = jnp.where(has_low, low, 0.0), jnp.where(has_high, high, 0.0)
    return own, low, high


def pre_kernel(
    shape_x,
    shape_y,
    forcing_ref, own_visc_ref, lower_ref, upper_ref, left_ref, right_ref, same_ref, cross_ref,
    weight_ref, diagonal_ref, smoothed_ref, coarse_ref, low_ref, high_ref, fine_low_ref, fine_high_ref,
    visc_ref, inverse_ref, residual_ref, base_ref, d0_ref, d1_ref, pair_ref, row_ref,
):
    parts, nx, ny, depth = forcing_ref.shape
    width, rows = nx + 2 * HALO, ny + 2 * HALO
    at_x, at_y = lax.axis_index("gx"), lax.axis_index("gy")
    has_left, has_right = at_x > 0, at_x < shape_x - 1
    has_low, has_high = at_y > 0, at_y < shape_y - 1
    low_and_high = message_reader(same_ref, cross_ref)
    fine_plan, fine_total = row_plan(nx, HALO)

    for x, row, count in row_plan(nx, VISC_HALO)[0]:
        if x < 0:
            own = left_ref[parts * HALO + x + VISC_HALO]
            inside = has_left
        elif x < nx:
            own = own_visc_ref[x]
            inside = None
        else:
            own = right_ref[parts * HALO + x - nx]
            inside = has_right
        low, high = low_and_high(parts * fine_total + row, count)
        own, low, high = masked(inside, has_low, has_high, own, low, high)
        place(writer(visc_ref, x + VISC_HALO), 0, ny, VISC_HALO, own, low, high)

    lane = lanes(rows, depth)

    for x in range(width):
        centre = visc_ref[x + 1, pl.ds(1, rows), :]
        halved = 0.5 * centre
        z_below = jnp.where(lane == 0, 0.0, below(halved))
        z_above = jnp.where(lane == depth - 1, 0.0, above(halved))
        faces = [
            halved + 0.5 * visc_ref[x, pl.ds(1, rows), :],
            halved + 0.5 * visc_ref[x + 2, pl.ds(1, rows), :],
            halved + 0.5 * visc_ref[x + 1, pl.ds(0, rows), :],
            halved + 0.5 * visc_ref[x + 1, pl.ds(2, rows), :],
            halved + z_below,
            halved + z_above,
        ]
        diagonal = faces[0] + faces[1] + faces[2] + faces[3] + faces[4] + faces[5]
        inside = centre > 0.0
        inverse = jnp.where(inside, 1.0 / jnp.where(inside, diagonal, 1.0), 0.0)
        for f in range(4):
            weight_ref[f, x] = faces[f] * inverse
        weight_ref[4, x] = jnp.where(lane == 0, 0.0, faces[4] * inverse)
        weight_ref[5, x] = jnp.where(lane == depth - 1, 0.0, faces[5] * inverse)
        inverse_ref[x] = inverse
        if HALO <= x < HALO + nx:
            pair_ref[...] = diagonal
            diagonal_ref[x - HALO] = pair_ref[pl.ds(HALO, ny), :]

    for c in range(parts):
        for x, row, count in fine_plan:
            i = x + HALO
            if x < 0:
                own = left_ref[c * HALO + i]
            elif x < nx:
                own = forcing_ref[c, x]
            else:
                own = right_ref[c * HALO + x - nx]
            low, high = low_and_high(c * fine_total + row, count)
            own = own * inverse_ref[i, pl.ds(HALO, ny), :]
            if count:
                low = low * inverse_ref[i, pl.ds(HALO - count, count), :]
                high = high * inverse_ref[i, pl.ds(HALO + ny, count), :]
            place(writer(base_ref, c, i), ROW0, ny, HALO, own, low, high)

    def finish(c, x, value):
        smoothed_ref[c, x - HALO] = value

    constants = constants_of(lower_ref, upper_ref)
    fine_steps(weight_ref, base_ref, residual_ref, (d0_ref, d1_ref), constants, width, finish)

    half = ny // 2
    even_own = lanes(ny, depth) % 2 == 0
    even_wide = lanes(ny + 2, depth) % 2 == 0
    even = lanes(half, depth) % 2 == 0
    lane_half = lanes(half, depth)

    def z_pair(value, even_mask):
        return value + jnp.where(even_mask, above(value), below(value))

    def y_sum(value, slot):
        row_ref[slot, pl.ds(0, value.shape[0]), :] = value
        return row_ref[slot, pl.ds(0, half, 2), :] + row_ref[slot, pl.ds(1, half, 2), :]

    def visc_own(x):
        return visc_ref[x + VISC_HALO, pl.ds(VISC_HALO, ny), :]

    inverses = []
    for i in range(nx // 2):
        faces_x = []
        for x in (2 * i - 1, 2 * i, 2 * i + 1, 2 * i + 2):
            faces_x.append(y_sum(z_pair(visc_own(x), even_own), 0))
        lower_x = faces_x[0] + faces_x[1]
        upper_x = faces_x[2] + faces_x[3]
        wide = pl.ds(VISC_HALO - 1, ny + 2)
        both = visc_ref[2 * i + VISC_HALO, wide, :] + visc_ref[2 * i + 1 + VISC_HALO, wide, :]
        row_ref[1, pl.ds(0, ny + 2), :] = z_pair(both, even_wide)
        picks = [row_ref[1, pl.ds(start, half, 2), :] for start in range(4)]
        lower_y = picks[0] + picks[1]
        upper_y = picks[2] + picks[3]
        column = y_sum(both[1 : ny + 1], 2)
        lower_z = column + jnp.where(lane_half == 0, 0.0, below(column))
        lower_z = jnp.where(even, lower_z, below(lower_z))
        upper_z = column + jnp.where(lane_half == depth - 1, 0.0, above(column))
        upper_z = jnp.where(even, above(upper_z), upper_z)
        inverse = 1.0 / (lower_x + upper_x + lower_y + upper_y + lower_z + upper_z)
        inverses.append(32.0 * inverse)
        sources = []
        for c in range(parts):
            total = 0.0
            for x in (2 * i, 2 * i + 1):
                total = total + smoothed_ref[c, x] * diagonal_ref[x]
            sources.append(y_sum(z_pair(total, even_own), 3 + c) * (4.0 * inverse))
        faces = [upper_x * (1.0 / 32.0), upper_y * (1.0 / 32.0), upper_z * (1.0 / 32.0)]
        coarse_ref[0, i] = jnp.where(even, sources[0], sources[1])
        coarse_ref[1, i] = jnp.where(even, sources[2], faces[0])
        coarse_ref[2, i] = jnp.where(even, faces[1], faces[2])
        if i % 2 == 1:
            coarse_ref[3, i // 2] = jnp.where(even, inverses[i - 1], inverses[i])

    at = 0
    ncx = nx // 2
    for f in range(4):
        shared = 2 if f == 3 else 1
        count = COARSE_HALO // shared
        for i in range(count):
            low_ref[at] = coarse_ref[f, i]
            high_ref[at] = coarse_ref[f, ncx // shared - count + i]
            at += 1
    for c in range(parts):
        for i in range(HALO):
            fine_low_ref[c * HALO + i] = smoothed_ref[c, i]
            fine_high_ref[c * HALO + i] = smoothed_ref[c, nx - HALO + i]


def coarse_spot(f, i, ncx):
    shared = 2 if f == 3 else 1
    count, own = COARSE_HALO // shared, ncx // shared
    base = f * COARSE_HALO
    if i < count:
        return "left", base + i
    if i < count + own:
        return "own", i - count
    return "right", base + i - count - own


def pack_coarse_kernel(coarse_ref, left_ref, right_ref, same_ref, cross_ref):
    ncx = coarse_ref.shape[1]
    sides = {"left": left_ref, "right": right_ref}
    put = message_writer(same_ref, cross_ref)
    base = 0
    for f in range(4):
        plan, total = row_plan(ncx, COARSE_HALO, 2 if f == 3 else 1)
        for i, (_, row, count) in enumerate(plan):
            side, at = coarse_spot(f, i, ncx)
            if side == "own":
                put(base + row, count, coarse_ref, (f, at))
            else:
                put(base + row, count, sides[side], (at,))
        base += total


def pack_fine_kernel(smoothed_ref, left_ref, right_ref, after_ref, same_ref, cross_ref):
    parts, nx = smoothed_ref.shape[:2]
    put = message_writer(same_ref, cross_ref)
    plan, total = row_plan(nx, HALO)
    for c in range(parts):
        for x, row, count in plan:
            if x < 0:
                put(c * total + row, count, left_ref, (c * HALO + x + HALO,))
            elif x < nx:
                put(c * total + row, count, smoothed_ref, (c, x))
            else:
                put(c * total + row, count, right_ref, (c * HALO + x - nx,))


def coarse_kernel(
    shape_x,
    shape_y,
    weight_ref, coarse_ref, lower_ref, upper_ref, left_ref, right_ref, same_ref, cross_ref,
    change_ref,
    field_ref, cweight_ref, source_ref, cd0_ref, cd1_ref, correction_ref, prolonged_ref,
):
    parts = change_ref.shape[0]
    width, rows = weight_ref.shape[1:3]
    ncx, half, depth = coarse_ref.shape[1:]
    cwidth, crows = ncx + 2 * COARSE_HALO, half + 2 * COARSE_HALO
    srows = source_ref.shape[2]
    at_x, at_y = lax.axis_index("gx"), lax.axis_index("gy")
    has_left, has_right = at_x > 0, at_x < shape_x - 1
    has_low, has_high = at_y > 0, at_y < shape_y - 1
    sides = {"left": left_ref, "right": right_ref}
    insides = {"left": has_left, "own": None, "right": has_right}
    low_and_high = message_reader(same_ref, cross_ref)
    constants = constants_of(lower_ref, upper_ref)
    first_scale, carried, scaled = constants

    base = 0
    tail = field_ref.shape[2] - ROW0 - crows
    for f in range(4):
        shared = 2 if f == 3 else 1
        plan, total = row_plan(ncx, COARSE_HALO, shared)
        for i, (_, row, count) in enumerate(plan):
            side, at = coarse_spot(f, i, ncx)
            own = coarse_ref[f, at] if side == "own" else sides[side][at]
            low, high = low_and_high(base + row, count)
            own, low, high = masked(insides[side], has_low, has_high, own, low, high)
            place(writer(field_ref, f, i), ROW0, half, COARSE_HALO, own, low, high)
            field_ref[f, i, pl.ds(0, ROW0), :] = jnp.zeros((ROW0, depth), jnp.float32)
            field_ref[f, i, pl.ds(ROW0 + crows, tail), :] = jnp.zeros((tail, depth), jnp.float32)
        base += total
    mid = pl.ds(ROW0, srows)
    lane = lanes(srows, depth)
    even = lane % 2 == 0

    def first_of(value):
        return jnp.where(even, value, below(value))

    def second_of(value):
        return jnp.where(even, above(value), value)

    even_low = lanes(field_ref.shape[2], depth) % 2 == 0
    for i in range(cwidth):
        packed = field_ref[3, i // 2, mid, :]
        inverse = first_of(packed) if i % 2 == 0 else second_of(packed)
        upper_x = second_of(field_ref[1, i, mid, :])
        faces_y = field_ref[2, i]
        upper_y = jnp.where(even_low, faces_y, below(faces_y))
        upper_z = second_of(field_ref[2, i, mid, :])
        source_ref[0, i] = field_ref[0, i, mid, :]
        source_ref[1, i] = first_of(field_ref[1, i, mid, :])
        if i > 0:
            cweight_ref[0, i] = second_of(field_ref[1, i - 1, mid, :]) * inverse
        cweight_ref[1, i] = upper_x * inverse
        cweight_ref[2, i] = upper_y[ROW0 - 1 : ROW0 - 1 + srows] * inverse
        cweight_ref[3, i] = upper_y[ROW0 : ROW0 + srows] * inverse
        cweight_ref[4, i] = jnp.where(lane < 2, 0.0, below(upper_z, 2) * inverse)
        cweight_ref[5, i] = jnp.where(lane >= depth - 2, 0.0, upper_z * inverse)

    for i in range(cwidth):
        for s in range(2):
            value = first_scale * source_ref[s, i]
            cd0_ref[s, i, mid, :] = value
            correction_ref[s, i] = value
    for number in range(COARSE_STEPS - 1):
        old, new = ((cd0_ref, cd1_ref), (cd1_ref, cd0_ref))[number % 2]
        last = number + 2 == COARSE_STEPS
        for i in range(number + 1, cwidth - 1 - number):
            weights = [cweight_ref[f, i] for f in range(6)]
            for s in range(2):
                own = old[s, i, mid, :]
                beside = weights[0] * old[s, i - 1, mid, :] + weights[1] * old[s, i + 1, mid, :]
                beside = beside + weights[2] * old[s, i, pl.ds(ROW0 - 1, srows), :]
                beside = beside + weights[3] * old[s, i, pl.ds(ROW0 + 1, srows), :]
                beside = beside + weights[4] * below(own, 2) + weights[5] * above(own, 2)
                fresh = source_ref[s, i] - own + beside
                direction = carried[number] * own + scaled[number] * fresh
                if not last:
                    source_ref[s, i] = fresh
                    new[s, i, mid, :] = direction
                correction_ref[s, i] = correction_ref[s, i] + direction

    edge = COARSE_HALO - COARSE_REACH
    pwidth, prows = ncx + 2 * COARSE_REACH, half + 2 * COARSE_REACH
    prow0 = ROW0 - (2 * COARSE_REACH - HALO)
    even_p = lanes(prows, depth) % 2 == 0
    for i in range(pwidth):
        pair = correction_ref[0, i + edge, pl.ds(edge, prows), :]
        single = correction_ref[1, i + edge, pl.ds(edge, prows), :]
        values = [
            jnp.where(even_p, pair, below(pair)),
            jnp.where(even_p, above(pair), pair),
            single,
        ]
        for c in range(parts):
            prolonged_ref[c, i, pl.ds(prow0, prows, 2), :] = values[c]
            prolonged_ref[c, i, pl.ds(prow0 + 1, prows, 2), :] = values[c]

    fine = pl.ds(ROW0, rows)
    shift = 2 * COARSE_REACH - HALO
    for i in range(width):
        weights = [weight_ref[f, i] for f in range(6)]
        at, before, after = (i + shift) // 2, (i + shift - 1) // 2, (i + shift + 1) // 2
        for c in range(parts):
            own = prolonged_ref[c, at, fine, :]
            beside = weights[0] * prolonged_ref[c, before, fine, :] + weights[1] * prolonged_ref[c, after, fine, :]
            beside = beside + weights[2] * prolonged_ref[c, at, pl.ds(ROW0 - 1, rows), :]
            beside = beside + weights[3] * prolonged_ref[c, at, pl.ds(ROW0 + 1, rows), :]
            beside = beside + weights[4] * below(own) + weights[5] * above(own)
            change_ref[c, i] = beside - own


def post_kernel(
    shape_x,
    shape_y,
    weight_ref, diagonal_ref, smoothed_ref, change_ref, lower_ref, upper_ref, left_ref, right_ref, same_ref, cross_ref,
    out_ref,
    residual_ref, base_ref, d0_ref, d1_ref,
):
    parts, nx, ny = smoothed_ref.shape[:3]
    width = nx + 2 * HALO
    at_x, at_y = lax.axis_index("gx"), lax.axis_index("gy")
    has_left, has_right = at_x > 0, at_x < shape_x - 1
    has_low, has_high = at_y > 0, at_y < shape_y - 1
    low_and_high = message_reader(same_ref, cross_ref)
    plan, total = row_plan(nx, HALO)
    for c in range(parts):
        for i, (x, row, count) in enumerate(plan):
            inside = None
            if x < 0:
                own, inside = left_ref[c * HALO + i], has_left
            elif x < nx:
                own = smoothed_ref[c, x]
            else:
                own, inside = right_ref[c * HALO + x - nx], has_right
            low, high = low_and_high(c * total + row, count)
            own, low, high = masked(inside, has_low, has_high, own, low, high)
            own = own + change_ref[c, i, pl.ds(HALO, ny), :]
            if count:
                low = low + change_ref[c, i, pl.ds(HALO - count, count), :]
                high = high + change_ref[c, i, pl.ds(HALO + ny, count), :]
            place(writer(base_ref, c, i), ROW0, ny, HALO, own, low, high)

    def finish(c, x, value):
        out_ref[c, x - HALO] = value * diagonal_ref[x - HALO]

    constants = constants_of(lower_ref, upper_ref)
    fine_steps(weight_ref, base_ref, residual_ref, (d0_ref, d1_ref), constants, width, finish)


def call(kernel, outs, scratch, specs):
    return pl.pallas_call(
        kernel,
        out_shape=[jax.ShapeDtypeStruct(shape, jnp.float32) for shape in outs],
        in_specs=[pl.BlockSpec(memory_space=space) for space in specs],
        out_specs=[pl.BlockSpec(memory_space=pltpu.VMEM) for _ in outs],
        scratch_shapes=[pltpu.VMEM(shape, jnp.float32) if isinstance(shape, tuple) else shape for shape in scratch],
        compiler_params=pltpu.CompilerParams(vmem_limit_bytes=VMEM_LIMIT),
    )


def ring_x(low, high):
    devices = lax.axis_size("gx")
    up = [(i, (i + 1) % devices) for i in range(devices)]
    down = [(j, i) for i, j in up]
    return lax.ppermute(high, "gx", up), lax.ppermute(low, "gx", down)


def swap_y(same, cross):
    devices = lax.axis_size("gy")
    pairs = [(i, i ^ 1) for i in range(devices)]
    others = [(0, 0), (devices - 1, devices - 1)]
    others = others + [(i, ((i + 1) ^ 1) - 1) for i in range(1, devices - 1)]
    return lax.ppermute(same, "gy", pairs), lax.ppermute(cross, "gy", others)


def in_hbm(value):
    return pltpu.with_memory_space_constraint(value, pltpu.HBM)


def up_to(value, unit):
    return -(-value // unit) * unit


def local(forcing, phase_index, visc_table, lower_bound, upper_bound):
    vmem, smem = pltpu.VMEM, pltpu.SMEM
    parts, nx, ny, depth = forcing.shape
    shape_x, shape_y = lax.axis_size("gx"), lax.axis_size("gy")
    width, rows = nx + 2 * HALO, ny + 2 * HALO
    ncx, half = nx // 2, ny // 2
    cwidth, crows = ncx + 2 * COARSE_HALO, half + 2 * COARSE_HALO
    srows = up_to(crows, 8)

    slab = (parts * HALO + VISC_HALO, ny, depth)
    semaphores = pltpu.SemaphoreType.DMA
    table_rows = pltpu.SMEM(visc_table.shape, jnp.float32)
    scratch = [pltpu.VMEM((2, VISC_HALO, ny, depth), jnp.int32), table_rows, semaphores((3, parts + 1))]
    low, high = call(pack_x_kernel, [slab, slab], scratch, [pltpu.HBM] * 3)(
        in_hbm(forcing), in_hbm(phase_index), in_hbm(visc_table)
    )
    left, right = ring_x(low, high)
    scratch = [pltpu.VMEM((nx, ny, depth), jnp.int32), table_rows, semaphores((3,))]
    forcing, viscosity = call(stage_kernel, [forcing.shape, (nx, ny, depth)], scratch, [pltpu.HBM] * 3)(
        in_hbm(forcing), in_hbm(phase_index), in_hbm(visc_table)
    )

    slab = (up_to(parts * row_plan(nx, HALO)[1] + row_plan(nx, VISC_HALO)[1], 8), depth)
    same, cross = call(pack_y_kernel, [slab, slab], [], [vmem] * 4)(forcing, viscosity, left, right)
    same, cross = swap_y(same, cross)

    slab = (3 * COARSE_HALO + COARSE_HALO // 2, half, depth)
    fine_slab = (parts * HALO, ny, depth)
    fine_d = (parts, width, rows + 2 * ROW0, depth)
    weight, diagonal, smoothed, coarse, low, high, fine_low, fine_high = call(
        functools.partial(pre_kernel, shape_x, shape_y),
        [(6, width, rows, depth), (nx, ny, depth), (parts, nx, ny, depth), (4, ncx, half, depth)]
        + [slab, slab, fine_slab, fine_slab],
        [
            (nx + 2 * VISC_HALO, up_to(ny + 2 * VISC_HALO, 8), depth),
            (width, rows, depth),
            (parts, width, rows, depth),
            fine_d,
            fine_d,
            fine_d,
            (rows, depth),
            (6, up_to(ny + 2, 8), depth),
        ],
        [vmem, vmem, smem, smem, vmem, vmem, vmem, vmem],
    )(forcing, viscosity, lower_bound, upper_bound, left, right, same, cross)
    left, right = ring_x(low, high)
    fine_left, fine_right = ring_x(fine_low, fine_high)

    count = 3 * row_plan(ncx, COARSE_HALO)[1] + row_plan(ncx, COARSE_HALO, 2)[1]
    slab = (up_to(count, 8), depth)
    packed, cross = call(pack_coarse_kernel, [slab, slab], [], [vmem] * 3)(coarse, left, right)
    same, cross = swap_y(packed, cross)
    slab = (up_to(parts * row_plan(nx, HALO)[1], 8), depth)
    fine_same, fine_cross = call(pack_fine_kernel, [slab, slab], [], [vmem] * 4)(
        smoothed, fine_left, fine_right, packed
    )
    fine_same, fine_cross = swap_y(fine_same, fine_cross)

    coarse_d = (2, cwidth, srows + 2 * ROW0, depth)
    (change,) = call(
        functools.partial(coarse_kernel, shape_x, shape_y),
        [(parts, width, rows, depth)],
        [
            (4, cwidth, up_to(ROW0 + crows + 1, 8), depth),
            (6, cwidth, srows, depth),
            (2, cwidth, srows, depth),
            coarse_d,
            coarse_d,
            (2, cwidth, srows, depth),
            (parts, ncx + 2 * COARSE_REACH, rows + 2 * ROW0, depth),
        ],
        [vmem, vmem, smem, smem, vmem, vmem, vmem, vmem],
    )(weight, coarse, lower_bound, upper_bound, left, right, same, cross)

    (out,) = call(
        functools.partial(post_kernel, shape_x, shape_y),
        [(parts, nx, ny, depth)],
        [(parts, width, rows, depth), fine_d, fine_d, fine_d],
        [vmem, vmem, vmem, vmem, smem, smem, vmem, vmem, vmem, vmem],
    )(weight, diagonal, smoothed, change, lower_bound, upper_bound, fine_left, fine_right, fine_same, fine_cross)
    return out


def solution(mesh):
    in_specs = (P(None, "gx", "gy", None), P("gx", "gy", None), P(), P(), P())
    out_specs = P(None, "gx", "gy", None)
    return jax.shard_map(local, mesh=mesh, in_specs=in_specs, out_specs=out_specs, check_vma=False)
```

```python
import functools

import jax
import jax.numpy as jnp
from jax import lax
from jax.experimental import pallas as pl
from jax.experimental.pallas import tpu as pltpu
from jax.sharding import PartitionSpec as P

CHEB = 4
COARSE_STEPS = 4
OUT_PIECES = 4
HALO = CHEB
VISC_HALO = HALO + 1
COARSE_REACH = (HALO + 2) // 2
COARSE_HALO = COARSE_REACH + COARSE_STEPS - 1
ROW0 = 8
VMEM_LIMIT = 48 * 1024 * 1024


def chebyshev_constants(lower_value, upper_value, count):
    centre = 0.5 * (upper_value + lower_value)
    radius = 0.5 * (upper_value - lower_value)
    spread = centre / radius
    damping = 1.0 / spread
    carried = []
    scaled = []
    for number in range(count - 1):
        renewed = 1.0 / (2.0 * spread - damping)
        carried.append(renewed * damping)
        scaled.append(2.0 * renewed / radius)
        damping = renewed
    return (1.0 / centre, carried, scaled)


def constants_of(lower_ref, upper_ref):
    lower_value = jnp.full((1, 128), lower_ref[0], jnp.float32)
    upper_value = jnp.full((1, 128), upper_ref[0], jnp.float32)
    return chebyshev_constants(lower_value, upper_value, max(CHEB, COARSE_STEPS))


def lookup(table_ref, phases):
    viscosity = jnp.full(phases.shape, table_ref[0], jnp.float32)
    for table_row in range(1, table_ref.shape[0]):
        viscosity = jnp.where(phases == table_row, table_ref[table_row], viscosity)
    return viscosity


def lanes(rows, depth):
    return lax.broadcasted_iota(jnp.int32, (rows, depth), 1)


def below(value, by=1):
    return pltpu.roll(value, by, 1)


def above(value, by=1):
    return pltpu.roll(value, value.shape[1] - by, 1)


def is_odd(axis):
    return lax.rem(lax.axis_index(axis), 2) == 1


def pack_x_kernel(forcing_ref, phase_ref, table_ref, low_ref, high_ref, phases_ref, rows_ref, sems):
    parts, nx = forcing_ref.shape[:2]
    base = parts * HALO
    sides = ((low_ref, 0, 0), (high_ref, nx - HALO, nx - VISC_HALO))
    first_copies, copies = [pltpu.make_async_copy(table_ref, rows_ref, sems.at[2, 0])], []
    for s, (ref, x, visc_x) in enumerate(sides):
        source = phase_ref.at[pl.ds(visc_x, VISC_HALO)]
        first_copies.append(pltpu.make_async_copy(source, phases_ref.at[s], sems.at[s, parts]))
        for c in range(parts):
            source, target = forcing_ref.at[c, pl.ds(x, HALO)], ref.at[pl.ds(c * HALO, HALO)]
            copies.append(pltpu.make_async_copy(source, target, sems.at[s, c]))
    for copy in first_copies + copies:
        copy.start()
    for copy in first_copies:
        copy.wait()
    for s, (ref, _, _) in enumerate(sides):
        for i in range(VISC_HALO):
            ref[base + i] = lookup(rows_ref, phases_ref[s, i])
    for copy in copies:
        copy.wait()


def stage_kernel(forcing_ref, phase_ref, table_ref, here_ref, visc_ref, phases_ref, rows_ref, sems):
    first_copies = [
        pltpu.make_async_copy(table_ref, rows_ref, sems.at[0]),
        pltpu.make_async_copy(phase_ref, phases_ref, sems.at[1]),
    ]
    copy = pltpu.make_async_copy(forcing_ref, here_ref, sems.at[2])
    for each in first_copies + [copy]:
        each.start()
    for each in first_copies:
        each.wait()
    for x in range(phase_ref.shape[0]):
        visc_ref[x] = lookup(rows_ref, phases_ref[x])
    copy.wait()


def row_plan(length, halo, shared=1):
    plan, row = [], 0
    for start in range(-halo, length + halo, shared):
        away = min(max(-x, x - length + 1, 0) for x in range(start, start + shared))
        plan.append((start, row, halo - away))
        row += halo - away
    return plan, row


def place(plane, first, inner, halo, own, low, high):
    count = low.shape[0] if low is not None else 0
    plane(first + halo, own)
    if count:
        plane(first + halo - count, low)
        plane(first + halo + inner, high)
    if count < halo:
        empty = jnp.zeros((halo - count, own.shape[1]), jnp.float32)
        plane(first, empty)
        plane(first + halo + inner + count, empty)


def writer(ref, *at):
    def store(row, value):
        ref[at + (pl.ds(row, value.shape[0]), slice(None))] = value

    return store


def message_reader(cross_ref, same_ref):
    odd = is_odd("gy")

    def low_and_high(row, count):
        if count == 0:
            return None, None
        same, cross = same_ref[pl.ds(row, count), :], cross_ref[pl.ds(row, count), :]
        return jnp.where(odd, same, cross), jnp.where(odd, cross, same)

    return low_and_high


def message_writer(cross_ref, same_ref):
    odd = is_odd("gy")

    def put(row, count, ref, at, ref_high=None, at_high=None):
        if count == 0:
            return
        ref_high, at_high = (ref, at) if ref_high is None else (ref_high, at_high)
        length = ref_high.shape[-2]
        low = ref[at + (pl.ds(0, count), slice(None))]
        high = ref_high[at_high + (pl.ds(length - count, count), slice(None))]
        same_ref[pl.ds(row, count), :] = jnp.where(odd, low, high)
        cross_ref[pl.ds(row, count), :] = jnp.where(odd, high, low)

    return put


def pack_y_kernel(forcing_ref, visc_ref, left_ref, right_ref, cross_ref, same_ref):
    parts, nx = forcing_ref.shape[:2]
    put = message_writer(cross_ref, same_ref)
    plan, total = row_plan(nx, HALO)
    for c in range(parts):
        for x, row, count in plan:
            if x < 0:
                put(c * total + row, count, left_ref, (c * HALO + x + HALO,))
            elif x < nx:
                put(c * total + row, count, forcing_ref, (c, x))
            else:
                put(c * total + row, count, right_ref, (c * HALO + x - nx,))
    for x, row, count in row_plan(nx, VISC_HALO)[0]:
        if x < 0:
            put(parts * total + row, count, left_ref, (parts * HALO + x + VISC_HALO,))
        elif x < nx:
            put(parts * total + row, count, visc_ref, (x,))
        else:
            put(parts * total + row, count, right_ref, (parts * HALO + x - nx,))


def fine_steps(weight_ref, base_ref, residual_ref, d_refs, constants, width, finish):
    first_scale, carried, scaled = constants
    parts, rows = residual_ref.shape[0], residual_ref.shape[2]
    for number in range(CHEB):
        old = base_ref if number == 0 else d_refs[number % 2]
        new = d_refs[(number + 1) % 2]
        last = number + 1 == CHEB
        skip, count = (HALO, rows - 2 * HALO) if last else (0, rows)
        inner = pl.ds(skip, count)
        for x in range(number + 1, width - 1 - number):
            weights = [weight_ref[f, x, inner, :] for f in range(6)]
            for c in range(parts):
                own = old[c, x, pl.ds(ROW0 + skip, count), :]
                beside = weights[0] * old[c, x - 1, pl.ds(ROW0 + skip, count), :]
                beside = beside + weights[1] * old[c, x + 1, pl.ds(ROW0 + skip, count), :]
                beside = beside + weights[2] * old[c, x, pl.ds(ROW0 + skip - 1, count), :]
                beside = beside + weights[3] * old[c, x, pl.ds(ROW0 + skip + 1, count), :]
                beside = beside + weights[4] * below(own) + weights[5] * above(own)
                if number == 0:
                    fresh = own - first_scale * (own - beside)
                    own = first_scale * own
                else:
                    fresh = residual_ref[c, x, inner, :] - own + beside
                if last:
                    finish(c, x, fresh)
                else:
                    residual_ref[c, x] = fresh
                    new[c, x, pl.ds(ROW0, rows), :] = carried[number] * own + scaled[number] * fresh


def masked(inside, has_low, has_high, own, low, high):
    if inside is not None:
        own = jnp.where(inside, own, 0.0)
        has_low, has_high = jnp.logical_and(has_low, inside), jnp.logical_and(has_high, inside)
    if low is not None:
        low, high = jnp.where(has_low, low, 0.0), jnp.where(has_high, high, 0.0)
    return own, low, high


def pre_kernel(
    shape_x,
    shape_y,
    forcing_ref, own_visc_ref, lower_ref, upper_ref, left_ref, right_ref, cross_ref, same_ref,
    weight_ref, diagonal_ref, smoothed_ref, coarse_ref, low_ref, high_ref, fine_low_ref, fine_high_ref,
    visc_ref, inverse_ref, residual_ref, base_ref, d0_ref, d1_ref, pair_ref, row_ref,
):
    parts, nx, ny, depth = forcing_ref.shape
    width, rows = nx + 2 * HALO, ny + 2 * HALO
    at_x, at_y = lax.axis_index("gx"), lax.axis_index("gy")
    has_left, has_right = at_x > 0, at_x < shape_x - 1
    has_low, has_high = at_y > 0, at_y < shape_y - 1
    low_and_high = message_reader(cross_ref, same_ref)
    fine_plan, fine_total = row_plan(nx, HALO)

    for x, row, count in row_plan(nx, VISC_HALO)[0]:
        if x < 0:
            own = left_ref[parts * HALO + x + VISC_HALO]
            inside = has_left
        elif x < nx:
            own = own_visc_ref[x]
            inside = None
        else:
            own = right_ref[parts * HALO + x - nx]
            inside = has_right
        low, high = low_and_high(parts * fine_total + row, count)
        own, low, high = masked(inside, has_low, has_high, own, low, high)
        place(writer(visc_ref, x + VISC_HALO), 0, ny, VISC_HALO, own, low, high)

    lane = lanes(rows, depth)

    for x in range(width):
        centre = visc_ref[x + 1, pl.ds(1, rows), :]
        halved = 0.5 * centre
        z_below = jnp.where(lane == 0, 0.0, below(halved))
        z_above = jnp.where(lane == depth - 1, 0.0, above(halved))
        faces = [
            halved + 0.5 * visc_ref[x, pl.ds(1, rows), :],
            halved + 0.5 * visc_ref[x + 2, pl.ds(1, rows), :],
            halved + 0.5 * visc_ref[x + 1, pl.ds(0, rows), :],
            halved + 0.5 * visc_ref[x + 1, pl.ds(2, rows), :],
            halved + z_below,
            halved + z_above,
        ]
        diagonal = faces[0] + faces[1] + faces[2] + faces[3] + faces[4] + faces[5]
        inside = centre > 0.0
        inverse = jnp.where(inside, 1.0 / jnp.where(inside, diagonal, 1.0), 0.0)
        for f in range(4):
            weight_ref[f, x] = faces[f] * inverse
        weight_ref[4, x] = jnp.where(lane == 0, 0.0, faces[4] * inverse)
        weight_ref[5, x] = jnp.where(lane == depth - 1, 0.0, faces[5] * inverse)
        inverse_ref[x] = inverse
        if HALO <= x < HALO + nx:
            pair_ref[...] = diagonal
            diagonal_ref[x - HALO] = pair_ref[pl.ds(HALO, ny), :]

    for c in range(parts):
        for x, row, count in fine_plan:
            i = x + HALO
            if x < 0:
                own = left_ref[c * HALO + i]
            elif x < nx:
                own = forcing_ref[c, x]
            else:
                own = right_ref[c * HALO + x - nx]
            low, high = low_and_high(c * fine_total + row, count)
            own = own * inverse_ref[i, pl.ds(HALO, ny), :]
            if count:
                low = low * inverse_ref[i, pl.ds(HALO - count, count), :]
                high = high * inverse_ref[i, pl.ds(HALO + ny, count), :]
            place(writer(base_ref, c, i), ROW0, ny, HALO, own, low, high)

    def finish(c, x, value):
        smoothed_ref[c, x - HALO] = value

    constants = constants_of(lower_ref, upper_ref)
    fine_steps(weight_ref, base_ref, residual_ref, (d0_ref, d1_ref), constants, width, finish)

    half = ny // 2
    even_own = lanes(ny, depth) % 2 == 0
    even_wide = lanes(ny + 2, depth) % 2 == 0
    even = lanes(half, depth) % 2 == 0
    lane_half = lanes(half, depth)

    def z_pair(value, even_mask):
        return value + jnp.where(even_mask, above(value), below(value))

    def y_sum(value, slot):
        row_ref[slot, pl.ds(0, value.shape[0]), :] = value
        return row_ref[slot, pl.ds(0, half, 2), :] + row_ref[slot, pl.ds(1, half, 2), :]

    def visc_own(x):
        return visc_ref[x + VISC_HALO, pl.ds(VISC_HALO, ny), :]

    inverses = []
    for i in range(nx // 2):
        faces_x = []
        for x in (2 * i - 1, 2 * i, 2 * i + 1, 2 * i + 2):
            faces_x.append(y_sum(z_pair(visc_own(x), even_own), 0))
        lower_x = faces_x[0] + faces_x[1]
        upper_x = faces_x[2] + faces_x[3]
        wide = pl.ds(VISC_HALO - 1, ny + 2)
        both = visc_ref[2 * i + VISC_HALO, wide, :] + visc_ref[2 * i + 1 + VISC_HALO, wide, :]
        row_ref[1, pl.ds(0, ny + 2), :] = z_pair(both, even_wide)
        picks = [row_ref[1, pl.ds(start, half, 2), :] for start in range(4)]
        lower_y = picks[0] + picks[1]
        upper_y = picks[2] + picks[3]
        column = y_sum(both[1 : ny + 1], 2)
        lower_z = column + jnp.where(lane_half == 0, 0.0, below(column))
        lower_z = jnp.where(even, lower_z, below(lower_z))
        upper_z = column + jnp.where(lane_half == depth - 1, 0.0, above(column))
        upper_z = jnp.where(even, above(upper_z), upper_z)
        inverse = 1.0 / (lower_x + upper_x + lower_y + upper_y + lower_z + upper_z)
        inverses.append(32.0 * inverse)
        sources = []
        for c in range(parts):
            total = 0.0
            for x in (2 * i, 2 * i + 1):
                total = total + smoothed_ref[c, x] * diagonal_ref[x]
            sources.append(y_sum(z_pair(total, even_own), 3 + c) * (4.0 * inverse))
        faces = [upper_x * (1.0 / 32.0), upper_y * (1.0 / 32.0), upper_z * (1.0 / 32.0)]
        coarse_ref[0, i] = jnp.where(even, sources[0], sources[1])
        coarse_ref[1, i] = jnp.where(even, sources[2], faces[0])
        coarse_ref[2, i] = jnp.where(even, faces[1], faces[2])
        if i % 2 == 1:
            coarse_ref[3, i // 2] = jnp.where(even, inverses[i - 1], inverses[i])

    at = 0
    ncx = nx // 2
    for f in range(4):
        shared = 2 if f == 3 else 1
        count = COARSE_HALO // shared
        for i in range(count):
            low_ref[at] = coarse_ref[f, i]
            high_ref[at] = coarse_ref[f, ncx // shared - count + i]
            at += 1
    for c in range(parts):
        for i in range(HALO):
            fine_low_ref[c * HALO + i] = smoothed_ref[c, i]
            fine_high_ref[c * HALO + i] = smoothed_ref[c, nx - HALO + i]


def coarse_spot(f, i, ncx):
    shared = 2 if f == 3 else 1
    count, own = COARSE_HALO // shared, ncx // shared
    base = f * COARSE_HALO
    if i < count:
        return "left", base + i
    if i < count + own:
        return "own", i - count
    return "right", base + i - count - own


def pack_coarse_kernel(coarse_ref, left_ref, right_ref, cross_ref, same_ref):
    ncx = coarse_ref.shape[1]
    sides = {"left": left_ref, "right": right_ref}
    put = message_writer(cross_ref, same_ref)
    base = 0
    for f in range(4):
        plan, total = row_plan(ncx, COARSE_HALO, 2 if f == 3 else 1)
        for i, (_, row, count) in enumerate(plan):
            side, at = coarse_spot(f, i, ncx)
            if side == "own":
                put(base + row, count, coarse_ref, (f, at))
            else:
                put(base + row, count, sides[side], (at,))
        base += total


def pack_fine_kernel(smoothed_ref, left_ref, right_ref, after_ref, cross_ref, same_ref):
    parts, nx = smoothed_ref.shape[:2]
    put = message_writer(cross_ref, same_ref)
    plan, total = row_plan(nx, HALO)
    for c in range(parts):
        for x, row, count in plan:
            if x < 0:
                put(c * total + row, count, left_ref, (c * HALO + x + HALO,))
            elif x < nx:
                put(c * total + row, count, smoothed_ref, (c, x))
            else:
                put(c * total + row, count, right_ref, (c * HALO + x - nx,))


def coarse_kernel(
    shape_x,
    shape_y,
    weight_ref, coarse_ref, lower_ref, upper_ref, left_ref, right_ref, cross_ref, same_ref,
    change_ref,
    field_ref, cweight_ref, source_ref, cd0_ref, cd1_ref, correction_ref, prolonged_ref,
):
    parts = change_ref.shape[0]
    width, rows = weight_ref.shape[1:3]
    ncx, half, depth = coarse_ref.shape[1:]
    cwidth, crows = ncx + 2 * COARSE_HALO, half + 2 * COARSE_HALO
    srows = source_ref.shape[2]
    at_x, at_y = lax.axis_index("gx"), lax.axis_index("gy")
    has_left, has_right = at_x > 0, at_x < shape_x - 1
    has_low, has_high = at_y > 0, at_y < shape_y - 1
    sides = {"left": left_ref, "right": right_ref}
    insides = {"left": has_left, "own": None, "right": has_right}
    low_and_high = message_reader(cross_ref, same_ref)
    constants = constants_of(lower_ref, upper_ref)
    first_scale, carried, scaled = constants

    base = 0
    tail = field_ref.shape[2] - ROW0 - crows
    for f in range(4):
        shared = 2 if f == 3 else 1
        plan, total = row_plan(ncx, COARSE_HALO, shared)
        for i, (_, row, count) in enumerate(plan):
            side, at = coarse_spot(f, i, ncx)
            own = coarse_ref[f, at] if side == "own" else sides[side][at]
            low, high = low_and_high(base + row, count)
            own, low, high = masked(insides[side], has_low, has_high, own, low, high)
            place(writer(field_ref, f, i), ROW0, half, COARSE_HALO, own, low, high)
            field_ref[f, i, pl.ds(0, ROW0), :] = jnp.zeros((ROW0, depth), jnp.float32)
            field_ref[f, i, pl.ds(ROW0 + crows, tail), :] = jnp.zeros((tail, depth), jnp.float32)
        base += total
    mid = pl.ds(ROW0, srows)
    lane = lanes(srows, depth)
    even = lane % 2 == 0

    def first_of(value):
        return jnp.where(even, value, below(value))

    def second_of(value):
        return jnp.where(even, above(value), value)

    before_x = None
    for i in range(cwidth):
        pair, faces_x = field_ref[0, i, mid, :], field_ref[1, i, mid, :]
        single, upper_x = first_of(faces_x), second_of(faces_x)
        source_ref[0, i] = pair
        source_ref[1, i] = single
        cd0_ref[0, i, mid, :] = first_scale * pair
        cd0_ref[1, i, mid, :] = first_scale * single
        if 0 < i < cwidth - 1:
            packed = field_ref[3, i // 2, mid, :]
            inverse = first_of(packed) if i % 2 == 0 else second_of(packed)
            faces_y = field_ref[2, i, mid, :]
            upper_z = second_of(faces_y)
            cweight_ref[0, i] = before_x * inverse
            cweight_ref[1, i] = upper_x * inverse
            cweight_ref[2, i] = first_of(field_ref[2, i, pl.ds(ROW0 - 1, srows), :]) * inverse
            cweight_ref[3, i] = first_of(faces_y) * inverse
            cweight_ref[4, i] = jnp.where(lane < 2, 0.0, below(upper_z, 2) * inverse)
            cweight_ref[5, i] = jnp.where(lane >= depth - 2, 0.0, upper_z * inverse)
        before_x = upper_x

    for number in range(COARSE_STEPS - 1):
        old, new = ((cd0_ref, cd1_ref), (cd1_ref, cd0_ref))[number % 2]
        last = number + 2 == COARSE_STEPS
        for i in range(number + 1, cwidth - 1 - number):
            weights = [cweight_ref[f, i] for f in range(6)]
            for s in range(2):
                own = old[s, i, mid, :]
                beside = weights[0] * old[s, i - 1, mid, :] + weights[1] * old[s, i + 1, mid, :]
                beside = beside + weights[2] * old[s, i, pl.ds(ROW0 - 1, srows), :]
                beside = beside + weights[3] * old[s, i, pl.ds(ROW0 + 1, srows), :]
                beside = beside + weights[4] * below(own, 2) + weights[5] * above(own, 2)
                fresh = source_ref[s, i] - own + beside
                direction = carried[number] * own + scaled[number] * fresh
                if not last:
                    source_ref[s, i] = fresh
                    new[s, i, mid, :] = direction
                correction_ref[s, i] = (own if number == 0 else correction_ref[s, i]) + direction

    edge = COARSE_HALO - COARSE_REACH
    pwidth, prows = ncx + 2 * COARSE_REACH, half + 2 * COARSE_REACH
    prow0 = ROW0 - (2 * COARSE_REACH - HALO)
    even_p = lanes(prows, depth) % 2 == 0
    for i in range(pwidth):
        pair = correction_ref[0, i + edge, pl.ds(edge, prows), :]
        single = correction_ref[1, i + edge, pl.ds(edge, prows), :]
        values = [
            jnp.where(even_p, pair, below(pair)),
            jnp.where(even_p, above(pair), pair),
            single,
        ]
        for c in range(parts):
            prolonged_ref[c, i, pl.ds(prow0, prows, 2), :] = values[c]
            prolonged_ref[c, i, pl.ds(prow0 + 1, prows, 2), :] = values[c]

    fine = pl.ds(ROW0, rows)
    shift = 2 * COARSE_REACH - HALO
    for i in range(width):
        weights = [weight_ref[f, i] for f in range(6)]
        at, before, after = (i + shift) // 2, (i + shift - 1) // 2, (i + shift + 1) // 2
        for c in range(parts):
            own = prolonged_ref[c, at, fine, :]
            beside = weights[0] * prolonged_ref[c, before, fine, :] + weights[1] * prolonged_ref[c, after, fine, :]
            beside = beside + weights[2] * prolonged_ref[c, at, pl.ds(ROW0 - 1, rows), :]
            beside = beside + weights[3] * prolonged_ref[c, at, pl.ds(ROW0 + 1, rows), :]
            beside = beside + weights[4] * below(own) + weights[5] * above(own)
            change_ref[c, i] = beside - own


def post_kernel(
    shape_x,
    shape_y,
    weight_ref, diagonal_ref, smoothed_ref, change_ref, lower_ref, upper_ref, left_ref, right_ref, cross_ref, same_ref,
    out_ref,
    done_ref, sems, residual_ref, base_ref, d0_ref, d1_ref,
):
    parts, nx, ny = smoothed_ref.shape[:3]
    width = nx + 2 * HALO
    at_x, at_y = lax.axis_index("gx"), lax.axis_index("gy")
    has_left, has_right = at_x > 0, at_x < shape_x - 1
    has_low, has_high = at_y > 0, at_y < shape_y - 1
    low_and_high = message_reader(cross_ref, same_ref)
    plan, total = row_plan(nx, HALO)
    for c in range(parts):
        for i, (x, row, count) in enumerate(plan):
            inside = None
            if x < 0:
                own, inside = left_ref[c * HALO + i], has_left
            elif x < nx:
                own = smoothed_ref[c, x]
            else:
                own, inside = right_ref[c * HALO + x - nx], has_right
            low, high = low_and_high(c * total + row, count)
            own, low, high = masked(inside, has_low, has_high, own, low, high)
            own = own + change_ref[c, i, pl.ds(HALO, ny), :]
            if count:
                low = low + change_ref[c, i, pl.ds(HALO - count, count), :]
                high = high + change_ref[c, i, pl.ds(HALO + ny, count), :]
            place(writer(base_ref, c, i), ROW0, ny, HALO, own, low, high)

    piece = nx // OUT_PIECES
    copies = []

    def finish(c, x, value):
        at = x - HALO
        done_ref[c, at] = value * diagonal_ref[at]
        if c == parts - 1 and at % piece == piece - 1:
            here = pl.ds(at + 1 - piece, piece)
            copies.append(pltpu.make_async_copy(done_ref.at[:, here], out_ref.at[:, here], sems.at[len(copies)]))
            copies[-1].start()

    constants = constants_of(lower_ref, upper_ref)
    fine_steps(weight_ref, base_ref, residual_ref, (d0_ref, d1_ref), constants, width, finish)
    for copy in copies:
        copy.wait()


def call(kernel, outs, scratch, specs, out_space=pltpu.VMEM):
    return pl.pallas_call(
        kernel,
        out_shape=[jax.ShapeDtypeStruct(shape, jnp.float32) for shape in outs],
        in_specs=[pl.BlockSpec(memory_space=space) for space in specs],
        out_specs=[pl.BlockSpec(memory_space=out_space) for _ in outs],
        scratch_shapes=[pltpu.VMEM(shape, jnp.float32) if isinstance(shape, tuple) else shape for shape in scratch],
        compiler_params=pltpu.CompilerParams(vmem_limit_bytes=VMEM_LIMIT),
    )


def ring_x(low, high):
    devices = lax.axis_size("gx")
    up = [(i, (i + 1) % devices) for i in range(devices)]
    down = [(j, i) for i, j in up]
    return lax.ppermute(high, "gx", up), lax.ppermute(low, "gx", down)


def swap_y(cross, same):
    devices = lax.axis_size("gy")
    pairs = [(i, i ^ 1) for i in range(devices)]
    others = [(0, 0), (devices - 1, devices - 1)]
    others = others + [(i, ((i + 1) ^ 1) - 1) for i in range(1, devices - 1)]
    return lax.ppermute(cross, "gy", others), lax.ppermute(same, "gy", pairs)


def in_hbm(value):
    return pltpu.with_memory_space_constraint(value, pltpu.HBM)


def up_to(value, unit):
    return -(-value // unit) * unit


def local(forcing, phase_index, visc_table, lower_bound, upper_bound):
    vmem, smem = pltpu.VMEM, pltpu.SMEM
    parts, nx, ny, depth = forcing.shape
    shape_x, shape_y = lax.axis_size("gx"), lax.axis_size("gy")
    width, rows = nx + 2 * HALO, ny + 2 * HALO
    ncx, half = nx // 2, ny // 2
    cwidth, crows = ncx + 2 * COARSE_HALO, half + 2 * COARSE_HALO
    srows = up_to(crows, 8)

    slab = (parts * HALO + VISC_HALO, ny, depth)
    semaphores = pltpu.SemaphoreType.DMA
    table_rows = pltpu.SMEM(visc_table.shape, jnp.float32)
    scratch = [pltpu.VMEM((2, VISC_HALO, ny, depth), jnp.int32), table_rows, semaphores((3, parts + 1))]
    low, high = call(pack_x_kernel, [slab, slab], scratch, [pltpu.HBM] * 3)(
        in_hbm(forcing), in_hbm(phase_index), in_hbm(visc_table)
    )
    left, right = ring_x(low, high)
    scratch = [pltpu.VMEM((nx, ny, depth), jnp.int32), table_rows, semaphores((3,))]
    forcing, viscosity = call(stage_kernel, [forcing.shape, (nx, ny, depth)], scratch, [pltpu.HBM] * 3)(
        in_hbm(forcing), in_hbm(phase_index), in_hbm(visc_table)
    )

    slab = (up_to(parts * row_plan(nx, HALO)[1] + row_plan(nx, VISC_HALO)[1], 8), depth)
    cross, same = call(pack_y_kernel, [slab, slab], [], [vmem] * 4)(forcing, viscosity, left, right)
    cross, same = swap_y(cross, same)

    slab = (3 * COARSE_HALO + COARSE_HALO // 2, half, depth)
    fine_slab = (parts * HALO, ny, depth)
    fine_d = (parts, width, rows + 2 * ROW0, depth)
    weight, diagonal, smoothed, coarse, low, high, fine_low, fine_high = call(
        functools.partial(pre_kernel, shape_x, shape_y),
        [(6, width, rows, depth), (nx, ny, depth), (parts, nx, ny, depth), (4, ncx, half, depth)]
        + [slab, slab, fine_slab, fine_slab],
        [
            (nx + 2 * VISC_HALO, up_to(ny + 2 * VISC_HALO, 8), depth),
            (width, rows, depth),
            (parts, width, rows, depth),
            fine_d,
            fine_d,
            fine_d,
            (rows, depth),
            (6, up_to(ny + 2, 8), depth),
        ],
        [vmem, vmem, smem, smem, vmem, vmem, vmem, vmem],
    )(forcing, viscosity, lower_bound, upper_bound, left, right, cross, same)
    left, right = ring_x(low, high)
    fine_left, fine_right = ring_x(fine_low, fine_high)

    count = 3 * row_plan(ncx, COARSE_HALO)[1] + row_plan(ncx, COARSE_HALO, 2)[1]
    slab = (up_to(count, 8), depth)
    packed, same = call(pack_coarse_kernel, [slab, slab], [], [vmem] * 3)(coarse, left, right)
    cross, same = swap_y(packed, same)
    slab = (up_to(parts * row_plan(nx, HALO)[1], 8), depth)
    fine_cross, fine_same = call(pack_fine_kernel, [slab, slab], [], [vmem] * 4)(
        smoothed, fine_left, fine_right, packed
    )
    fine_cross, fine_same = swap_y(fine_cross, fine_same)

    coarse_d = (2, cwidth, srows + 2 * ROW0, depth)
    (change,) = call(
        functools.partial(coarse_kernel, shape_x, shape_y),
        [(parts, width, rows, depth)],
        [
            (4, cwidth, up_to(ROW0 + crows + 1, 8), depth),
            (6, cwidth, srows, depth),
            (2, cwidth, srows, depth),
            coarse_d,
            coarse_d,
            (2, cwidth, srows, depth),
            (parts, ncx + 2 * COARSE_REACH, rows + 2 * ROW0, depth),
        ],
        [vmem, vmem, smem, smem, vmem, vmem, vmem, vmem],
    )(weight, coarse, lower_bound, upper_bound, left, right, cross, same)

    (out,) = call(
        functools.partial(post_kernel, shape_x, shape_y),
        [(parts, nx, ny, depth)],
        [(parts, nx, ny, depth), pltpu.SemaphoreType.DMA((OUT_PIECES,)), (parts, width, rows, depth), fine_d, fine_d, fine_d],
        [vmem, vmem, vmem, vmem, smem, smem, vmem, vmem, vmem, vmem],
        pltpu.HBM,
    )(weight, diagonal, smoothed, change, lower_bound, upper_bound, fine_left, fine_right, fine_cross, fine_same)
    return out


def solution(mesh):
    in_specs = (P(None, "gx", "gy", None), P("gx", "gy", None), P(), P(), P())
    out_specs = P(None, "gx", "gy", None)
    return jax.shard_map(local, mesh=mesh, in_specs=in_specs, out_specs=out_specs, check_vma=False)
```

```python
import functools

import jax
import jax.numpy as jnp
from jax import lax
from jax.experimental import pallas as pl
from jax.experimental.pallas import tpu as pltpu
from jax.sharding import PartitionSpec as P

CHEB = 4
COARSE_STEPS = 4
OUT_PIECES = 4
HALO = CHEB
VISC_HALO = HALO + 1
COARSE_REACH = (HALO + 2) // 2
COARSE_HALO = COARSE_REACH + COARSE_STEPS - 1
ROW0 = 8
VMEM_LIMIT = 48 * 1024 * 1024


def chebyshev_constants(lower_value, upper_value, count):
    centre = 0.5 * (upper_value + lower_value)
    radius = 0.5 * (upper_value - lower_value)
    spread = centre / radius
    damping = 1.0 / spread
    carried = []
    scaled = []
    for number in range(count - 1):
        renewed = 1.0 / (2.0 * spread - damping)
        carried.append(renewed * damping)
        scaled.append(2.0 * renewed / radius)
        damping = renewed
    return (1.0 / centre, carried, scaled)


def constants_of(lower_ref, upper_ref):
    lower_value = jnp.full((1, 128), lower_ref[0], jnp.float32)
    upper_value = jnp.full((1, 128), upper_ref[0], jnp.float32)
    return chebyshev_constants(lower_value, upper_value, max(CHEB, COARSE_STEPS))


def lookup(table_ref, phases):
    viscosity = jnp.full(phases.shape, table_ref[0], jnp.float32)
    for table_row in range(1, table_ref.shape[0]):
        viscosity = jnp.where(phases == table_row, table_ref[table_row], viscosity)
    return viscosity


def lanes(rows, depth):
    return lax.broadcasted_iota(jnp.int32, (rows, depth), 1)


def below(value, by=1):
    return pltpu.roll(value, by, 1)


def above(value, by=1):
    return pltpu.roll(value, value.shape[1] - by, 1)


def is_odd(axis):
    return lax.rem(lax.axis_index(axis), 2) == 1


def pack_x_kernel(forcing_ref, phase_ref, table_ref, low_ref, high_ref, phases_ref, rows_ref, sems):
    parts, nx = forcing_ref.shape[:2]
    base = parts * HALO
    sides = ((low_ref, 0, 0), (high_ref, nx - HALO, nx - VISC_HALO))
    first_copies, copies = [pltpu.make_async_copy(table_ref, rows_ref, sems.at[2, 0])], []
    for s, (ref, x, visc_x) in enumerate(sides):
        source = phase_ref.at[pl.ds(visc_x, VISC_HALO)]
        first_copies.append(pltpu.make_async_copy(source, phases_ref.at[s], sems.at[s, parts]))
        for c in range(parts):
            source, target = forcing_ref.at[c, pl.ds(x, HALO)], ref.at[pl.ds(c * HALO, HALO)]
            copies.append(pltpu.make_async_copy(source, target, sems.at[s, c]))
    for copy in first_copies + copies:
        copy.start()
    for copy in first_copies:
        copy.wait()
    for s, (ref, _, _) in enumerate(sides):
        for i in range(VISC_HALO):
            ref[base + i] = lookup(rows_ref, phases_ref[s, i])
    for copy in copies:
        copy.wait()


def stage_kernel(forcing_ref, phase_ref, table_ref, here_ref, visc_ref, phases_ref, rows_ref, sems):
    first_copies = [
        pltpu.make_async_copy(table_ref, rows_ref, sems.at[0]),
        pltpu.make_async_copy(phase_ref, phases_ref, sems.at[1]),
    ]
    copy = pltpu.make_async_copy(forcing_ref, here_ref, sems.at[2])
    for each in first_copies + [copy]:
        each.start()
    for each in first_copies:
        each.wait()
    for x in range(phase_ref.shape[0]):
        visc_ref[x] = lookup(rows_ref, phases_ref[x])
    copy.wait()


def row_plan(length, halo, shared=1):
    plan, row = [], 0
    for start in range(-halo, length + halo, shared):
        away = min(max(-x, x - length + 1, 0) for x in range(start, start + shared))
        plan.append((start, row, halo - away))
        row += halo - away
    return plan, row


def place(plane, first, inner, halo, own, low, high):
    count = low.shape[0] if low is not None else 0
    plane(first + halo, own)
    if count:
        plane(first + halo - count, low)
        plane(first + halo + inner, high)
    if count < halo:
        empty = jnp.zeros((halo - count, own.shape[1]), jnp.float32)
        plane(first, empty)
        plane(first + halo + inner + count, empty)


def writer(ref, *at):
    def store(row, value):
        ref[at + (pl.ds(row, value.shape[0]), slice(None))] = value

    return store


def message_reader(cross_ref, same_ref):
    odd = is_odd("gy")

    def low_and_high(row, count):
        if count == 0:
            return None, None
        same, cross = same_ref[pl.ds(row, count), :], cross_ref[pl.ds(row, count), :]
        return jnp.where(odd, same, cross), jnp.where(odd, cross, same)

    return low_and_high


def message_writer(cross_ref, same_ref):
    odd = is_odd("gy")

    def put(row, count, ref, at, ref_high=None, at_high=None):
        if count == 0:
            return
        ref_high, at_high = (ref, at) if ref_high is None else (ref_high, at_high)
        length = ref_high.shape[-2]
        low = ref[at + (pl.ds(0, count), slice(None))]
        high = ref_high[at_high + (pl.ds(length - count, count), slice(None))]
        same_ref[pl.ds(row, count), :] = jnp.where(odd, low, high)
        cross_ref[pl.ds(row, count), :] = jnp.where(odd, high, low)

    return put


def pack_y_kernel(forcing_ref, visc_ref, left_ref, right_ref, cross_ref, same_ref):
    parts, nx = forcing_ref.shape[:2]
    put = message_writer(cross_ref, same_ref)
    plan, total = row_plan(nx, HALO)
    for c in range(parts):
        for x, row, count in plan:
            if x < 0:
                put(c * total + row, count, left_ref, (c * HALO + x + HALO,))
            elif x < nx:
                put(c * total + row, count, forcing_ref, (c, x))
            else:
                put(c * total + row, count, right_ref, (c * HALO + x - nx,))
    for x, row, count in row_plan(nx, VISC_HALO)[0]:
        if x < 0:
            put(parts * total + row, count, left_ref, (parts * HALO + x + VISC_HALO,))
        elif x < nx:
            put(parts * total + row, count, visc_ref, (x,))
        else:
            put(parts * total + row, count, right_ref, (parts * HALO + x - nx,))


def fine_steps(weight_ref, base_ref, residual_ref, d_refs, constants, width, finish):
    first_scale, carried, scaled = constants
    parts, rows = residual_ref.shape[0], residual_ref.shape[2]
    for number in range(CHEB):
        old = base_ref if number == 0 else d_refs[number % 2]
        new = d_refs[(number + 1) % 2]
        last = number + 1 == CHEB
        skip, count = (HALO, rows - 2 * HALO) if last else (0, rows)
        inner = pl.ds(skip, count)
        for x in range(number + 1, width - 1 - number):
            weights = [weight_ref[f, x, inner, :] for f in range(6)]
            for c in range(parts):
                own = old[c, x, pl.ds(ROW0 + skip, count), :]
                beside = weights[0] * old[c, x - 1, pl.ds(ROW0 + skip, count), :]
                beside = beside + weights[1] * old[c, x + 1, pl.ds(ROW0 + skip, count), :]
                beside = beside + weights[2] * old[c, x, pl.ds(ROW0 + skip - 1, count), :]
                beside = beside + weights[3] * old[c, x, pl.ds(ROW0 + skip + 1, count), :]
                beside = beside + weights[4] * below(own) + weights[5] * above(own)
                if number == 0:
                    fresh = own - first_scale * (own - beside)
                    own = first_scale * own
                else:
                    fresh = residual_ref[c, x, inner, :] - own + beside
                if last:
                    finish(c, x, fresh)
                else:
                    residual_ref[c, x] = fresh
                    new[c, x, pl.ds(ROW0, rows), :] = carried[number] * own + scaled[number] * fresh


def masked(inside, has_low, has_high, own, low, high):
    if inside is not None:
        own = jnp.where(inside, own, 0.0)
        has_low, has_high = jnp.logical_and(has_low, inside), jnp.logical_and(has_high, inside)
    if low is not None:
        low, high = jnp.where(has_low, low, 0.0), jnp.where(has_high, high, 0.0)
    return own, low, high


def pre_kernel(
    shape_x,
    shape_y,
    forcing_ref, own_visc_ref, lower_ref, upper_ref, left_ref, right_ref, cross_ref, same_ref,
    weight_ref, diagonal_ref, smoothed_ref, coarse_ref, low_ref, high_ref, fine_low_ref, fine_high_ref,
    visc_ref, inverse_ref, residual_ref, base_ref, d0_ref, d1_ref, pair_ref, row_ref,
):
    parts, nx, ny, depth = forcing_ref.shape
    width, rows = nx + 2 * HALO, ny + 2 * HALO
    at_x, at_y = lax.axis_index("gx"), lax.axis_index("gy")
    has_left, has_right = at_x > 0, at_x < shape_x - 1
    has_low, has_high = at_y > 0, at_y < shape_y - 1
    low_and_high = message_reader(cross_ref, same_ref)
    fine_plan, fine_total = row_plan(nx, HALO)

    for x, row, count in row_plan(nx, VISC_HALO)[0]:
        if x < 0:
            own = left_ref[parts * HALO + x + VISC_HALO]
            inside = has_left
        elif x < nx:
            own = own_visc_ref[x]
            inside = None
        else:
            own = right_ref[parts * HALO + x - nx]
            inside = has_right
        low, high = low_and_high(parts * fine_total + row, count)
        own, low, high = masked(inside, has_low, has_high, own, low, high)
        place(writer(visc_ref, x + VISC_HALO), 0, ny, VISC_HALO, own, low, high)

    lane = lanes(rows, depth)

    for x in range(width):
        centre = visc_ref[x + 1, pl.ds(1, rows), :]
        halved = 0.5 * centre
        z_below = jnp.where(lane == 0, 0.0, below(halved))
        z_above = jnp.where(lane == depth - 1, 0.0, above(halved))
        faces = [
            halved + 0.5 * visc_ref[x, pl.ds(1, rows), :],
            halved + 0.5 * visc_ref[x + 2, pl.ds(1, rows), :],
            halved + 0.5 * visc_ref[x + 1, pl.ds(0, rows), :],
            halved + 0.5 * visc_ref[x + 1, pl.ds(2, rows), :],
            halved + z_below,
            halved + z_above,
        ]
        diagonal = faces[0] + faces[1] + faces[2] + faces[3] + faces[4] + faces[5]
        inside = centre > 0.0
        inverse = jnp.where(inside, 1.0 / jnp.where(inside, diagonal, 1.0), 0.0)
        for f in range(4):
            weight_ref[f, x] = faces[f] * inverse
        weight_ref[4, x] = jnp.where(lane == 0, 0.0, faces[4] * inverse)
        weight_ref[5, x] = jnp.where(lane == depth - 1, 0.0, faces[5] * inverse)
        inverse_ref[x] = inverse
        if HALO <= x < HALO + nx:
            pair_ref[...] = diagonal
            diagonal_ref[x - HALO] = pair_ref[pl.ds(HALO, ny), :]

    for c in range(parts):
        for x, row, count in fine_plan:
            i = x + HALO
            if x < 0:
                own = left_ref[c * HALO + i]
            elif x < nx:
                own = forcing_ref[c, x]
            else:
                own = right_ref[c * HALO + x - nx]
            low, high = low_and_high(c * fine_total + row, count)
            own = own * inverse_ref[i, pl.ds(HALO, ny), :]
            if count:
                low = low * inverse_ref[i, pl.ds(HALO - count, count), :]
                high = high * inverse_ref[i, pl.ds(HALO + ny, count), :]
            place(writer(base_ref, c, i), ROW0, ny, HALO, own, low, high)

    def finish(c, x, value):
        smoothed_ref[c, x - HALO] = value

    constants = constants_of(lower_ref, upper_ref)
    fine_steps(weight_ref, base_ref, residual_ref, (d0_ref, d1_ref), constants, width, finish)

    half = ny // 2
    even_own = lanes(ny, depth) % 2 == 0
    even_wide = lanes(ny + 2, depth) % 2 == 0
    even = lanes(half, depth) % 2 == 0
    lane_half = lanes(half, depth)

    def z_pair(value, even_mask):
        return value + jnp.where(even_mask, above(value), below(value))

    def y_sum(value, slot):
        row_ref[slot, pl.ds(0, value.shape[0]), :] = value
        return row_ref[slot, pl.ds(0, half, 2), :] + row_ref[slot, pl.ds(1, half, 2), :]

    def visc_own(x):
        return visc_ref[x + VISC_HALO, pl.ds(VISC_HALO, ny), :]

    inverses = []
    for i in range(nx // 2):
        faces_x = []
        for x in (2 * i - 1, 2 * i, 2 * i + 1, 2 * i + 2):
            faces_x.append(y_sum(z_pair(visc_own(x), even_own), 0))
        lower_x = faces_x[0] + faces_x[1]
        upper_x = faces_x[2] + faces_x[3]
        wide = pl.ds(VISC_HALO - 1, ny + 2)
        both = visc_ref[2 * i + VISC_HALO, wide, :] + visc_ref[2 * i + 1 + VISC_HALO, wide, :]
        row_ref[1, pl.ds(0, ny + 2), :] = z_pair(both, even_wide)
        picks = [row_ref[1, pl.ds(start, half, 2), :] for start in range(4)]
        lower_y = picks[0] + picks[1]
        upper_y = picks[2] + picks[3]
        column = y_sum(both[1 : ny + 1], 2)
        lower_z = column + jnp.where(lane_half == 0, 0.0, below(column))
        lower_z = jnp.where(even, lower_z, below(lower_z))
        upper_z = column + jnp.where(lane_half == depth - 1, 0.0, above(column))
        upper_z = jnp.where(even, above(upper_z), upper_z)
        inverse = 1.0 / (lower_x + upper_x + lower_y + upper_y + lower_z + upper_z)
        inverses.append(32.0 * inverse)
        sources = []
        for c in range(parts):
            total = 0.0
            for x in (2 * i, 2 * i + 1):
                total = total + smoothed_ref[c, x] * diagonal_ref[x]
            sources.append(y_sum(z_pair(total, even_own), 3 + c) * (4.0 * inverse))
        faces = [upper_x * (1.0 / 32.0), upper_y * (1.0 / 32.0), upper_z * (1.0 / 32.0)]
        coarse_ref[0, i] = jnp.where(even, sources[0], sources[1])
        coarse_ref[1, i] = jnp.where(even, sources[2], faces[0])
        coarse_ref[2, i] = jnp.where(even, faces[1], faces[2])
        if i % 2 == 1:
            coarse_ref[3, i // 2] = jnp.where(even, inverses[i - 1], inverses[i])

    at = 0
    ncx = nx // 2
    for f in range(4):
        shared = 2 if f == 3 else 1
        count = COARSE_HALO // shared
        for i in range(count):
            low_ref[at] = coarse_ref[f, i]
            high_ref[at] = coarse_ref[f, ncx // shared - count + i]
            at += 1
    for c in range(parts):
        for i in range(HALO):
            fine_low_ref[c * HALO + i] = smoothed_ref[c, i]
            fine_high_ref[c * HALO + i] = smoothed_ref[c, nx - HALO + i]


def coarse_spot(f, i, ncx):
    shared = 2 if f == 3 else 1
    count, own = COARSE_HALO // shared, ncx // shared
    base = f * COARSE_HALO
    if i < count:
        return "left", base + i
    if i < count + own:
        return "own", i - count
    return "right", base + i - count - own


def pack_coarse_kernel(coarse_ref, left_ref, right_ref, cross_ref, same_ref):
    ncx = coarse_ref.shape[1]
    sides = {"left": left_ref, "right": right_ref}
    put = message_writer(cross_ref, same_ref)
    base = 0
    for f in range(4):
        plan, total = row_plan(ncx, COARSE_HALO, 2 if f == 3 else 1)
        for i, (_, row, count) in enumerate(plan):
            side, at = coarse_spot(f, i, ncx)
            if side == "own":
                put(base + row, count, coarse_ref, (f, at))
            else:
                put(base + row, count, sides[side], (at,))
        base += total


def pack_fine_kernel(smoothed_ref, left_ref, right_ref, after_ref, cross_ref, same_ref):
    parts, nx = smoothed_ref.shape[:2]
    put = message_writer(cross_ref, same_ref)
    plan, total = row_plan(nx, HALO)
    for c in range(parts):
        for x, row, count in plan:
            if x < 0:
                put(c * total + row, count, left_ref, (c * HALO + x + HALO,))
            elif x < nx:
                put(c * total + row, count, smoothed_ref, (c, x))
            else:
                put(c * total + row, count, right_ref, (c * HALO + x - nx,))


def coarse_kernel(
    shape_x,
    shape_y,
    weight_ref, coarse_ref, lower_ref, upper_ref, left_ref, right_ref, cross_ref, same_ref,
    change_ref,
    field_ref, cweight_ref, source_ref, cd0_ref, cd1_ref, correction_ref, prolonged_ref,
):
    parts = change_ref.shape[0]
    width, rows = weight_ref.shape[1:3]
    ncx, half, depth = coarse_ref.shape[1:]
    cwidth, crows = ncx + 2 * COARSE_HALO, half + 2 * COARSE_HALO
    srows = source_ref.shape[2]
    at_x, at_y = lax.axis_index("gx"), lax.axis_index("gy")
    has_left, has_right = at_x > 0, at_x < shape_x - 1
    has_low, has_high = at_y > 0, at_y < shape_y - 1
    sides = {"left": left_ref, "right": right_ref}
    insides = {"left": has_left, "own": None, "right": has_right}
    low_and_high = message_reader(cross_ref, same_ref)
    constants = constants_of(lower_ref, upper_ref)
    first_scale, carried, scaled = constants

    base = 0
    tail = field_ref.shape[2] - ROW0 - crows
    for f in range(4):
        shared = 2 if f == 3 else 1
        plan, total = row_plan(ncx, COARSE_HALO, shared)
        for i, (_, row, count) in enumerate(plan):
            side, at = coarse_spot(f, i, ncx)
            own = coarse_ref[f, at] if side == "own" else sides[side][at]
            low, high = low_and_high(base + row, count)
            own, low, high = masked(insides[side], has_low, has_high, own, low, high)
            place(writer(field_ref, f, i), ROW0, half, COARSE_HALO, own, low, high)
            field_ref[f, i, pl.ds(0, ROW0), :] = jnp.zeros((ROW0, depth), jnp.float32)
            field_ref[f, i, pl.ds(ROW0 + crows, tail), :] = jnp.zeros((tail, depth), jnp.float32)
        base += total
    mid = pl.ds(ROW0, srows)
    lane = lanes(srows, depth)
    even = lane % 2 == 0

    def first_of(value):
        return jnp.where(even, value, below(value))

    def second_of(value):
        return jnp.where(even, above(value), value)

    before_x = None
    for i in range(cwidth):
        pair, faces_x = field_ref[0, i, mid, :], field_ref[1, i, mid, :]
        single, upper_x = first_of(faces_x), second_of(faces_x)
        source_ref[0, i] = pair
        source_ref[1, i] = single
        cd0_ref[0, i, mid, :] = first_scale * pair
        cd0_ref[1, i, mid, :] = first_scale * single
        if 0 < i < cwidth - 1:
            packed = field_ref[3, i // 2, mid, :]
            inverse = first_of(packed) if i % 2 == 0 else second_of(packed)
            faces_y = field_ref[2, i, mid, :]
            upper_z = second_of(faces_y)
            cweight_ref[0, i] = before_x * inverse
            cweight_ref[1, i] = upper_x * inverse
            cweight_ref[2, i] = first_of(field_ref[2, i, pl.ds(ROW0 - 1, srows), :]) * inverse
            cweight_ref[3, i] = first_of(faces_y) * inverse
            cweight_ref[4, i] = jnp.where(lane < 2, 0.0, below(upper_z, 2) * inverse)
            cweight_ref[5, i] = jnp.where(lane >= depth - 2, 0.0, upper_z * inverse)
        before_x = upper_x

    for number in range(COARSE_STEPS - 1):
        old, new = ((cd0_ref, cd1_ref), (cd1_ref, cd0_ref))[number % 2]
        last = number + 2 == COARSE_STEPS
        skip = 0 if number == 0 else 2
        count = srows if number == 0 else crows - 2 * skip
        inner, here = pl.ds(skip, count), pl.ds(ROW0 + skip, count)
        for i in range(number + 1, cwidth - 1 - number):
            weights = [cweight_ref[f, i, inner, :] for f in range(6)]
            for s in range(2):
                own = old[s, i, here, :]
                beside = weights[0] * old[s, i - 1, here, :] + weights[1] * old[s, i + 1, here, :]
                beside = beside + weights[2] * old[s, i, pl.ds(ROW0 + skip - 1, count), :]
                beside = beside + weights[3] * old[s, i, pl.ds(ROW0 + skip + 1, count), :]
                beside = beside + weights[4] * below(own, 2) + weights[5] * above(own, 2)
                fresh = source_ref[s, i, inner, :] - own + beside
                direction = carried[number] * own + scaled[number] * fresh
                if not last:
                    source_ref[s, i, inner, :] = fresh
                    new[s, i, here, :] = direction
                before = own if number == 0 else correction_ref[s, i, inner, :]
                correction_ref[s, i, inner, :] = before + direction

    edge = COARSE_HALO - COARSE_REACH
    pwidth, prows = ncx + 2 * COARSE_REACH, half + 2 * COARSE_REACH
    prow0 = ROW0 - (2 * COARSE_REACH - HALO)
    even_p = lanes(prows, depth) % 2 == 0
    for i in range(pwidth):
        pair = correction_ref[0, i + edge, pl.ds(edge, prows), :]
        single = correction_ref[1, i + edge, pl.ds(edge, prows), :]
        values = [
            jnp.where(even_p, pair, below(pair)),
            jnp.where(even_p, above(pair), pair),
            single,
        ]
        for c in range(parts):
            prolonged_ref[c, i, pl.ds(prow0, prows, 2), :] = values[c]
            prolonged_ref[c, i, pl.ds(prow0 + 1, prows, 2), :] = values[c]

    fine = pl.ds(ROW0, rows)
    shift = 2 * COARSE_REACH - HALO
    for i in range(width):
        weights = [weight_ref[f, i] for f in range(6)]
        at, before, after = (i + shift) // 2, (i + shift - 1) // 2, (i + shift + 1) // 2
        for c in range(parts):
            own = prolonged_ref[c, at, fine, :]
            beside = weights[0] * prolonged_ref[c, before, fine, :] + weights[1] * prolonged_ref[c, after, fine, :]
            beside = beside + weights[2] * prolonged_ref[c, at, pl.ds(ROW0 - 1, rows), :]
            beside = beside + weights[3] * prolonged_ref[c, at, pl.ds(ROW0 + 1, rows), :]
            beside = beside + weights[4] * below(own) + weights[5] * above(own)
            change_ref[c, i] = beside - own


def post_kernel(
    shape_x,
    shape_y,
    weight_ref, diagonal_ref, smoothed_ref, change_ref, lower_ref, upper_ref, left_ref, right_ref, cross_ref, same_ref,
    out_ref,
    done_ref, sems, residual_ref, base_ref, d0_ref, d1_ref,
):
    parts, nx, ny = smoothed_ref.shape[:3]
    width = nx + 2 * HALO
    at_x, at_y = lax.axis_index("gx"), lax.axis_index("gy")
    has_left, has_right = at_x > 0, at_x < shape_x - 1
    has_low, has_high = at_y > 0, at_y < shape_y - 1
    low_and_high = message_reader(cross_ref, same_ref)
    plan, total = row_plan(nx, HALO)
    for c in range(parts):
        for i, (x, row, count) in enumerate(plan):
            inside = None
            if x < 0:
                own, inside = left_ref[c * HALO + i], has_left
            elif x < nx:
                own = smoothed_ref[c, x]
            else:
                own, inside = right_ref[c * HALO + x - nx], has_right
            low, high = low_and_high(c * total + row, count)
            own, low, high = masked(inside, has_low, has_high, own, low, high)
            own = own + change_ref[c, i, pl.ds(HALO, ny), :]
            if count:
                low = low + change_ref[c, i, pl.ds(HALO - count, count), :]
                high = high + change_ref[c, i, pl.ds(HALO + ny, count), :]
            place(writer(base_ref, c, i), ROW0, ny, HALO, own, low, high)

    piece = nx // OUT_PIECES
    copies = []

    def finish(c, x, value):
        at = x - HALO
        done_ref[c, at] = value * diagonal_ref[at]
        if c == parts - 1 and at % piece == piece - 1:
            here = pl.ds(at + 1 - piece, piece)
            copies.append(pltpu.make_async_copy(done_ref.at[:, here], out_ref.at[:, here], sems.at[len(copies)]))
            copies[-1].start()

    constants = constants_of(lower_ref, upper_ref)
    fine_steps(weight_ref, base_ref, residual_ref, (d0_ref, d1_ref), constants, width, finish)
    for copy in copies:
        copy.wait()


def call(kernel, outs, scratch, specs, out_space=pltpu.VMEM):
    return pl.pallas_call(
        kernel,
        out_shape=[jax.ShapeDtypeStruct(shape, jnp.float32) for shape in outs],
        in_specs=[pl.BlockSpec(memory_space=space) for space in specs],
        out_specs=[pl.BlockSpec(memory_space=out_space) for _ in outs],
        scratch_shapes=[pltpu.VMEM(shape, jnp.float32) if isinstance(shape, tuple) else shape for shape in scratch],
        compiler_params=pltpu.CompilerParams(vmem_limit_bytes=VMEM_LIMIT),
    )


def ring_x(low, high):
    devices = lax.axis_size("gx")
    up = [(i, (i + 1) % devices) for i in range(devices)]
    down = [(j, i) for i, j in up]
    return lax.ppermute(high, "gx", up), lax.ppermute(low, "gx", down)


def swap_y(cross, same):
    devices = lax.axis_size("gy")
    pairs = [(i, i ^ 1) for i in range(devices)]
    others = [(0, 0), (devices - 1, devices - 1)]
    others = others + [(i, ((i + 1) ^ 1) - 1) for i in range(1, devices - 1)]
    return lax.ppermute(cross, "gy", others), lax.ppermute(same, "gy", pairs)


def in_hbm(value):
    return pltpu.with_memory_space_constraint(value, pltpu.HBM)


def up_to(value, unit):
    return -(-value // unit) * unit


def local(forcing, phase_index, visc_table, lower_bound, upper_bound):
    vmem, smem = pltpu.VMEM, pltpu.SMEM
    parts, nx, ny, depth = forcing.shape
    shape_x, shape_y = lax.axis_size("gx"), lax.axis_size("gy")
    width, rows = nx + 2 * HALO, ny + 2 * HALO
    ncx, half = nx // 2, ny // 2
    cwidth, crows = ncx + 2 * COARSE_HALO, half + 2 * COARSE_HALO
    srows = up_to(crows, 8)

    slab = (parts * HALO + VISC_HALO, ny, depth)
    semaphores = pltpu.SemaphoreType.DMA
    table_rows = pltpu.SMEM(visc_table.shape, jnp.float32)
    scratch = [pltpu.VMEM((2, VISC_HALO, ny, depth), jnp.int32), table_rows, semaphores((3, parts + 1))]
    low, high = call(pack_x_kernel, [slab, slab], scratch, [pltpu.HBM] * 3)(
        in_hbm(forcing), in_hbm(phase_index), in_hbm(visc_table)
    )
    left, right = ring_x(low, high)
    scratch = [pltpu.VMEM((nx, ny, depth), jnp.int32), table_rows, semaphores((3,))]
    forcing, viscosity = call(stage_kernel, [forcing.shape, (nx, ny, depth)], scratch, [pltpu.HBM] * 3)(
        in_hbm(forcing), in_hbm(phase_index), in_hbm(visc_table)
    )

    slab = (up_to(parts * row_plan(nx, HALO)[1] + row_plan(nx, VISC_HALO)[1], 8), depth)
    cross, same = call(pack_y_kernel, [slab, slab], [], [vmem] * 4)(forcing, viscosity, left, right)
    cross, same = swap_y(cross, same)

    slab = (3 * COARSE_HALO + COARSE_HALO // 2, half, depth)
    fine_slab = (parts * HALO, ny, depth)
    fine_d = (parts, width, rows + 2 * ROW0, depth)
    weight, diagonal, smoothed, coarse, low, high, fine_low, fine_high = call(
        functools.partial(pre_kernel, shape_x, shape_y),
        [(6, width, rows, depth), (nx, ny, depth), (parts, nx, ny, depth), (4, ncx, half, depth)]
        + [slab, slab, fine_slab, fine_slab],
        [
            (nx + 2 * VISC_HALO, up_to(ny + 2 * VISC_HALO, 8), depth),
            (width, rows, depth),
            (parts, width, rows, depth),
            fine_d,
            fine_d,
            fine_d,
            (rows, depth),
            (6, up_to(ny + 2, 8), depth),
        ],
        [vmem, vmem, smem, smem, vmem, vmem, vmem, vmem],
    )(forcing, viscosity, lower_bound, upper_bound, left, right, cross, same)
    left, right = ring_x(low, high)
    fine_left, fine_right = ring_x(fine_low, fine_high)

    count = 3 * row_plan(ncx, COARSE_HALO)[1] + row_plan(ncx, COARSE_HALO, 2)[1]
    slab = (up_to(count, 8), depth)
    packed, same = call(pack_coarse_kernel, [slab, slab], [], [vmem] * 3)(coarse, left, right)
    cross, same = swap_y(packed, same)
    slab = (up_to(parts * row_plan(nx, HALO)[1], 8), depth)
    fine_cross, fine_same = call(pack_fine_kernel, [slab, slab], [], [vmem] * 4)(
        smoothed, fine_left, fine_right, packed
    )
    fine_cross, fine_same = swap_y(fine_cross, fine_same)

    coarse_d = (2, cwidth, srows + 2 * ROW0, depth)
    (change,) = call(
        functools.partial(coarse_kernel, shape_x, shape_y),
        [(parts, width, rows, depth)],
        [
            (4, cwidth, up_to(ROW0 + crows + 1, 8), depth),
            (6, cwidth, srows, depth),
            (2, cwidth, srows, depth),
            coarse_d,
            coarse_d,
            (2, cwidth, srows, depth),
            (parts, ncx + 2 * COARSE_REACH, rows + 2 * ROW0, depth),
        ],
        [vmem, vmem, smem, smem, vmem, vmem, vmem, vmem],
    )(weight, coarse, lower_bound, upper_bound, left, right, cross, same)

    (out,) = call(
        functools.partial(post_kernel, shape_x, shape_y),
        [(parts, nx, ny, depth)],
        [(parts, nx, ny, depth), pltpu.SemaphoreType.DMA((OUT_PIECES,)), (parts, width, rows, depth), fine_d, fine_d, fine_d],
        [vmem, vmem, vmem, vmem, smem, smem, vmem, vmem, vmem, vmem],
        pltpu.HBM,
    )(weight, diagonal, smoothed, change, lower_bound, upper_bound, fine_left, fine_right, fine_cross, fine_same)
    return out


def solution(mesh):
    in_specs = (P(None, "gx", "gy", None), P("gx", "gy", None), P(), P(), P())
    out_specs = P(None, "gx", "gy", None)
    return jax.shard_map(local, mesh=mesh, in_specs=in_specs, out_specs=out_specs, check_vma=False)
```

```python
import functools

import jax
import jax.numpy as jnp
from jax import lax
from jax.experimental import pallas as pl
from jax.experimental.pallas import tpu as pltpu
from jax.sharding import PartitionSpec as P

CHEB = 4
COARSE_STEPS = 4
OUT_PIECES = 4
HALO = CHEB
VISC_HALO = HALO + 1
COARSE_REACH = (HALO + 2) // 2
COARSE_HALO = COARSE_REACH + COARSE_STEPS - 1
ROW0 = 8
VMEM_LIMIT = 48 * 1024 * 1024


def chebyshev_constants(lower_value, upper_value, count):
    centre = 0.5 * (upper_value + lower_value)
    radius = 0.5 * (upper_value - lower_value)
    spread = centre / radius
    damping = 1.0 / spread
    carried = []
    scaled = []
    for number in range(count - 1):
        renewed = 1.0 / (2.0 * spread - damping)
        carried.append(renewed * damping)
        scaled.append(2.0 * renewed / radius)
        damping = renewed
    return (1.0 / centre, carried, scaled)


def constants_of(lower_ref, upper_ref):
    lower_value = jnp.full((1, 128), lower_ref[0], jnp.float32)
    upper_value = jnp.full((1, 128), upper_ref[0], jnp.float32)
    return chebyshev_constants(lower_value, upper_value, max(CHEB, COARSE_STEPS))


def lookup(table_ref, phases):
    viscosity = jnp.full(phases.shape, table_ref[0], jnp.float32)
    for table_row in range(1, table_ref.shape[0]):
        viscosity = jnp.where(phases == table_row, table_ref[table_row], viscosity)
    return viscosity


def lanes(rows, depth):
    return lax.broadcasted_iota(jnp.int32, (rows, depth), 1)


def below(value, by=1):
    return pltpu.roll(value, by, 1)


def above(value, by=1):
    return pltpu.roll(value, value.shape[1] - by, 1)


def is_odd(axis):
    return lax.rem(lax.axis_index(axis), 2) == 1


def pack_x_kernel(forcing_ref, phase_ref, table_ref, low_ref, high_ref, phases_ref, rows_ref, sems):
    parts, nx = forcing_ref.shape[:2]
    base = parts * HALO
    sides = ((low_ref, 0, 0), (high_ref, nx - HALO, nx - VISC_HALO))
    first_copies, copies = [pltpu.make_async_copy(table_ref, rows_ref, sems.at[2, 0])], []
    for s, (ref, x, visc_x) in enumerate(sides):
        source = phase_ref.at[pl.ds(visc_x, VISC_HALO)]
        first_copies.append(pltpu.make_async_copy(source, phases_ref.at[s], sems.at[s, parts]))
        for c in range(parts):
            source, target = forcing_ref.at[c, pl.ds(x, HALO)], ref.at[pl.ds(c * HALO, HALO)]
            copies.append(pltpu.make_async_copy(source, target, sems.at[s, c]))
    for copy in first_copies + copies:
        copy.start()
    for copy in first_copies:
        copy.wait()
    for s, (ref, _, _) in enumerate(sides):
        for i in range(VISC_HALO):
            ref[base + i] = lookup(rows_ref, phases_ref[s, i])
    for copy in copies:
        copy.wait()


def stage_kernel(forcing_ref, phase_ref, table_ref, here_ref, visc_ref, phases_ref, rows_ref, sems):
    first_copies = [
        pltpu.make_async_copy(table_ref, rows_ref, sems.at[0]),
        pltpu.make_async_copy(phase_ref, phases_ref, sems.at[1]),
    ]
    copy = pltpu.make_async_copy(forcing_ref, here_ref, sems.at[2])
    for each in first_copies + [copy]:
        each.start()
    for each in first_copies:
        each.wait()
    for x in range(phase_ref.shape[0]):
        visc_ref[x] = lookup(rows_ref, phases_ref[x])
    copy.wait()


def row_plan(length, halo, shared=1):
    plan, row = [], 0
    for start in range(-halo, length + halo, shared):
        away = min(max(-x, x - length + 1, 0) for x in range(start, start + shared))
        plan.append((start, row, halo - away))
        row += halo - away
    return plan, row


def place(plane, first, inner, halo, own, low, high):
    count = low.shape[0] if low is not None else 0
    plane(first + halo, own)
    if count:
        plane(first + halo - count, low)
        plane(first + halo + inner, high)
    if count < halo:
        empty = jnp.zeros((halo - count, own.shape[1]), jnp.float32)
        plane(first, empty)
        plane(first + halo + inner + count, empty)


def writer(ref, *at):
    def store(row, value):
        ref[at + (pl.ds(row, value.shape[0]), slice(None))] = value

    return store


def message_reader(cross_ref, same_ref):
    odd = is_odd("gy")

    def low_and_high(row, count):
        if count == 0:
            return None, None
        same, cross = same_ref[pl.ds(row, count), :], cross_ref[pl.ds(row, count), :]
        return jnp.where(odd, same, cross), jnp.where(odd, cross, same)

    return low_and_high


def message_writer(cross_ref, same_ref):
    odd = is_odd("gy")

    def put(row, count, ref, at, ref_high=None, at_high=None):
        if count == 0:
            return
        ref_high, at_high = (ref, at) if ref_high is None else (ref_high, at_high)
        length = ref_high.shape[-2]
        low = ref[at + (pl.ds(0, count), slice(None))]
        high = ref_high[at_high + (pl.ds(length - count, count), slice(None))]
        same_ref[pl.ds(row, count), :] = jnp.where(odd, low, high)
        cross_ref[pl.ds(row, count), :] = jnp.where(odd, high, low)

    return put


def pack_y_kernel(forcing_ref, visc_ref, left_ref, right_ref, cross_ref, same_ref):
    parts, nx = forcing_ref.shape[:2]
    put = message_writer(cross_ref, same_ref)
    plan, total = row_plan(nx, HALO)
    for c in range(parts):
        for x, row, count in plan:
            if x < 0:
                put(c * total + row, count, left_ref, (c * HALO + x + HALO,))
            elif x < nx:
                put(c * total + row, count, forcing_ref, (c, x))
            else:
                put(c * total + row, count, right_ref, (c * HALO + x - nx,))
    for x, row, count in row_plan(nx, VISC_HALO)[0]:
        if x < 0:
            put(parts * total + row, count, left_ref, (parts * HALO + x + VISC_HALO,))
        elif x < nx:
            put(parts * total + row, count, visc_ref, (x,))
        else:
            put(parts * total + row, count, right_ref, (parts * HALO + x - nx,))


def fine_steps(weight_ref, base_ref, residual_ref, d_refs, constants, width, finish):
    first_scale, carried, scaled = constants
    parts, rows = residual_ref.shape[0], residual_ref.shape[2]
    for number in range(CHEB):
        old = base_ref if number == 0 else d_refs[number % 2]
        new = d_refs[(number + 1) % 2]
        last = number + 1 == CHEB
        for x in range(number + 1, width - 1 - number):
            outermost = x in (number + 1, width - 2 - number)
            skip, count = (HALO, rows - 2 * HALO) if last or outermost else (0, rows)
            inner = pl.ds(skip, count)
            weights = [weight_ref[f, x, inner, :] for f in range(6)]
            for c in range(parts):
                own = old[c, x, pl.ds(ROW0 + skip, count), :]
                beside = weights[0] * old[c, x - 1, pl.ds(ROW0 + skip, count), :]
                beside = beside + weights[1] * old[c, x + 1, pl.ds(ROW0 + skip, count), :]
                beside = beside + weights[2] * old[c, x, pl.ds(ROW0 + skip - 1, count), :]
                beside = beside + weights[3] * old[c, x, pl.ds(ROW0 + skip + 1, count), :]
                beside = beside + weights[4] * below(own) + weights[5] * above(own)
                if number == 0:
                    fresh = own - first_scale * (own - beside)
                    own = first_scale * own
                else:
                    fresh = residual_ref[c, x, inner, :] - own + beside
                if last:
                    finish(c, x, fresh)
                else:
                    residual_ref[c, x, inner, :] = fresh
                    new[c, x, pl.ds(ROW0 + skip, count), :] = carried[number] * own + scaled[number] * fresh


def masked(inside, has_low, has_high, own, low, high):
    if inside is not None:
        own = jnp.where(inside, own, 0.0)
        has_low, has_high = jnp.logical_and(has_low, inside), jnp.logical_and(has_high, inside)
    if low is not None:
        low, high = jnp.where(has_low, low, 0.0), jnp.where(has_high, high, 0.0)
    return own, low, high


def pre_kernel(
    shape_x,
    shape_y,
    forcing_ref, own_visc_ref, lower_ref, upper_ref, left_ref, right_ref, cross_ref, same_ref,
    weight_ref, diagonal_ref, smoothed_ref, coarse_ref, low_ref, high_ref, fine_low_ref, fine_high_ref,
    visc_ref, inverse_ref, residual_ref, base_ref, d0_ref, d1_ref, pair_ref, row_ref,
):
    parts, nx, ny, depth = forcing_ref.shape
    width, rows = nx + 2 * HALO, ny + 2 * HALO
    at_x, at_y = lax.axis_index("gx"), lax.axis_index("gy")
    has_left, has_right = at_x > 0, at_x < shape_x - 1
    has_low, has_high = at_y > 0, at_y < shape_y - 1
    low_and_high = message_reader(cross_ref, same_ref)
    fine_plan, fine_total = row_plan(nx, HALO)

    for x, row, count in row_plan(nx, VISC_HALO)[0]:
        if x < 0:
            own = left_ref[parts * HALO + x + VISC_HALO]
            inside = has_left
        elif x < nx:
            own = own_visc_ref[x]
            inside = None
        else:
            own = right_ref[parts * HALO + x - nx]
            inside = has_right
        low, high = low_and_high(parts * fine_total + row, count)
        own, low, high = masked(inside, has_low, has_high, own, low, high)
        place(writer(visc_ref, x + VISC_HALO), 0, ny, VISC_HALO, own, low, high)

    lane = lanes(rows, depth)

    for x in range(width):
        centre = visc_ref[x + 1, pl.ds(1, rows), :]
        halved = 0.5 * centre
        z_below = jnp.where(lane == 0, 0.0, below(halved))
        z_above = jnp.where(lane == depth - 1, 0.0, above(halved))
        faces = [
            halved + 0.5 * visc_ref[x, pl.ds(1, rows), :],
            halved + 0.5 * visc_ref[x + 2, pl.ds(1, rows), :],
            halved + 0.5 * visc_ref[x + 1, pl.ds(0, rows), :],
            halved + 0.5 * visc_ref[x + 1, pl.ds(2, rows), :],
            halved + z_below,
            halved + z_above,
        ]
        diagonal = faces[0] + faces[1] + faces[2] + faces[3] + faces[4] + faces[5]
        inside = centre > 0.0
        inverse = jnp.where(inside, 1.0 / jnp.where(inside, diagonal, 1.0), 0.0)
        for f in range(4):
            weight_ref[f, x] = faces[f] * inverse
        weight_ref[4, x] = jnp.where(lane == 0, 0.0, faces[4] * inverse)
        weight_ref[5, x] = jnp.where(lane == depth - 1, 0.0, faces[5] * inverse)
        inverse_ref[x] = inverse
        if HALO <= x < HALO + nx:
            pair_ref[...] = diagonal
            diagonal_ref[x - HALO] = pair_ref[pl.ds(HALO, ny), :]

    for c in range(parts):
        for x, row, count in fine_plan:
            i = x + HALO
            if x < 0:
                own = left_ref[c * HALO + i]
            elif x < nx:
                own = forcing_ref[c, x]
            else:
                own = right_ref[c * HALO + x - nx]
            low, high = low_and_high(c * fine_total + row, count)
            own = own * inverse_ref[i, pl.ds(HALO, ny), :]
            if count:
                low = low * inverse_ref[i, pl.ds(HALO - count, count), :]
                high = high * inverse_ref[i, pl.ds(HALO + ny, count), :]
            place(writer(base_ref, c, i), ROW0, ny, HALO, own, low, high)

    def finish(c, x, value):
        smoothed_ref[c, x - HALO] = value

    constants = constants_of(lower_ref, upper_ref)
    fine_steps(weight_ref, base_ref, residual_ref, (d0_ref, d1_ref), constants, width, finish)

    half = ny // 2
    even_own = lanes(ny, depth) % 2 == 0
    even_wide = lanes(ny + 2, depth) % 2 == 0
    even = lanes(half, depth) % 2 == 0
    lane_half = lanes(half, depth)

    def z_pair(value, even_mask):
        return value + jnp.where(even_mask, above(value), below(value))

    def y_sum(value, slot):
        row_ref[slot, pl.ds(0, value.shape[0]), :] = value
        return row_ref[slot, pl.ds(0, half, 2), :] + row_ref[slot, pl.ds(1, half, 2), :]

    def visc_own(x):
        return visc_ref[x + VISC_HALO, pl.ds(VISC_HALO, ny), :]

    inverses = []
    for i in range(nx // 2):
        faces_x = []
        for x in (2 * i - 1, 2 * i, 2 * i + 1, 2 * i + 2):
            faces_x.append(y_sum(z_pair(visc_own(x), even_own), 0))
        lower_x = faces_x[0] + faces_x[1]
        upper_x = faces_x[2] + faces_x[3]
        wide = pl.ds(VISC_HALO - 1, ny + 2)
        both = visc_ref[2 * i + VISC_HALO, wide, :] + visc_ref[2 * i + 1 + VISC_HALO, wide, :]
        row_ref[1, pl.ds(0, ny + 2), :] = z_pair(both, even_wide)
        picks = [row_ref[1, pl.ds(start, half, 2), :] for start in range(4)]
        lower_y = picks[0] + picks[1]
        upper_y = picks[2] + picks[3]
        column = y_sum(both[1 : ny + 1], 2)
        lower_z = column + jnp.where(lane_half == 0, 0.0, below(column))
        lower_z = jnp.where(even, lower_z, below(lower_z))
        upper_z = column + jnp.where(lane_half == depth - 1, 0.0, above(column))
        upper_z = jnp.where(even, above(upper_z), upper_z)
        inverse = 1.0 / (lower_x + upper_x + lower_y + upper_y + lower_z + upper_z)
        inverses.append(32.0 * inverse)
        sources = []
        for c in range(parts):
            total = 0.0
            for x in (2 * i, 2 * i + 1):
                total = total + smoothed_ref[c, x] * diagonal_ref[x]
            sources.append(y_sum(z_pair(total, even_own), 3 + c) * (4.0 * inverse))
        faces = [upper_x * (1.0 / 32.0), upper_y * (1.0 / 32.0), upper_z * (1.0 / 32.0)]
        coarse_ref[0, i] = jnp.where(even, sources[0], sources[1])
        coarse_ref[1, i] = jnp.where(even, sources[2], faces[0])
        coarse_ref[2, i] = jnp.where(even, faces[1], faces[2])
        if i % 2 == 1:
            coarse_ref[3, i // 2] = jnp.where(even, inverses[i - 1], inverses[i])

    at = 0
    ncx = nx // 2
    for f in range(4):
        shared = 2 if f == 3 else 1
        count = COARSE_HALO // shared
        for i in range(count):
            low_ref[at] = coarse_ref[f, i]
            high_ref[at] = coarse_ref[f, ncx // shared - count + i]
            at += 1
    for c in range(parts):
        for i in range(HALO):
            fine_low_ref[c * HALO + i] = smoothed_ref[c, i]
            fine_high_ref[c * HALO + i] = smoothed_ref[c, nx - HALO + i]


def coarse_spot(f, i, ncx):
    shared = 2 if f == 3 else 1
    count, own = COARSE_HALO // shared, ncx // shared
    base = f * COARSE_HALO
    if i < count:
        return "left", base + i
    if i < count + own:
        return "own", i - count
    return "right", base + i - count - own


def pack_coarse_kernel(coarse_ref, left_ref, right_ref, cross_ref, same_ref):
    ncx = coarse_ref.shape[1]
    sides = {"left": left_ref, "right": right_ref}
    put = message_writer(cross_ref, same_ref)
    base = 0
    for f in range(4):
        plan, total = row_plan(ncx, COARSE_HALO, 2 if f == 3 else 1)
        for i, (_, row, count) in enumerate(plan):
            side, at = coarse_spot(f, i, ncx)
            if side == "own":
                put(base + row, count, coarse_ref, (f, at))
            else:
                put(base + row, count, sides[side], (at,))
        base += total


def pack_fine_kernel(smoothed_ref, left_ref, right_ref, after_ref, cross_ref, same_ref):
    parts, nx = smoothed_ref.shape[:2]
    put = message_writer(cross_ref, same_ref)
    plan, total = row_plan(nx, HALO)
    for c in range(parts):
        for x, row, count in plan:
            if x < 0:
                put(c * total + row, count, left_ref, (c * HALO + x + HALO,))
            elif x < nx:
                put(c * total + row, count, smoothed_ref, (c, x))
            else:
                put(c * total + row, count, right_ref, (c * HALO + x - nx,))


def coarse_kernel(
    shape_x,
    shape_y,
    weight_ref, coarse_ref, lower_ref, upper_ref, left_ref, right_ref, cross_ref, same_ref,
    change_ref,
    field_ref, cweight_ref, source_ref, cd0_ref, cd1_ref, correction_ref, prolonged_ref,
):
    parts = change_ref.shape[0]
    width, rows = weight_ref.shape[1:3]
    ncx, half, depth = coarse_ref.shape[1:]
    cwidth, crows = ncx + 2 * COARSE_HALO, half + 2 * COARSE_HALO
    srows = source_ref.shape[2]
    at_x, at_y = lax.axis_index("gx"), lax.axis_index("gy")
    has_left, has_right = at_x > 0, at_x < shape_x - 1
    has_low, has_high = at_y > 0, at_y < shape_y - 1
    sides = {"left": left_ref, "right": right_ref}
    insides = {"left": has_left, "own": None, "right": has_right}
    low_and_high = message_reader(cross_ref, same_ref)
    constants = constants_of(lower_ref, upper_ref)
    first_scale, carried, scaled = constants

    base = 0
    tail = field_ref.shape[2] - ROW0 - crows
    for f in range(4):
        shared = 2 if f == 3 else 1
        plan, total = row_plan(ncx, COARSE_HALO, shared)
        for i, (_, row, count) in enumerate(plan):
            side, at = coarse_spot(f, i, ncx)
            own = coarse_ref[f, at] if side == "own" else sides[side][at]
            low, high = low_and_high(base + row, count)
            own, low, high = masked(insides[side], has_low, has_high, own, low, high)
            place(writer(field_ref, f, i), ROW0, half, COARSE_HALO, own, low, high)
            field_ref[f, i, pl.ds(0, ROW0), :] = jnp.zeros((ROW0, depth), jnp.float32)
            field_ref[f, i, pl.ds(ROW0 + crows, tail), :] = jnp.zeros((tail, depth), jnp.float32)
        base += total
    mid = pl.ds(ROW0, srows)
    lane = lanes(srows, depth)
    even = lane % 2 == 0

    def first_of(value):
        return jnp.where(even, value, below(value))

    def second_of(value):
        return jnp.where(even, above(value), value)

    before_x = None
    for i in range(cwidth):
        pair, faces_x = field_ref[0, i, mid, :], field_ref[1, i, mid, :]
        single, upper_x = first_of(faces_x), second_of(faces_x)
        source_ref[0, i] = pair
        source_ref[1, i] = single
        cd0_ref[0, i, mid, :] = first_scale * pair
        cd0_ref[1, i, mid, :] = first_scale * single
        if 0 < i < cwidth - 1:
            packed = field_ref[3, i // 2, mid, :]
            inverse = first_of(packed) if i % 2 == 0 else second_of(packed)
            faces_y = field_ref[2, i, mid, :]
            upper_z = second_of(faces_y)
            cweight_ref[0, i] = before_x * inverse
            cweight_ref[1, i] = upper_x * inverse
            cweight_ref[2, i] = first_of(field_ref[2, i, pl.ds(ROW0 - 1, srows), :]) * inverse
            cweight_ref[3, i] = first_of(faces_y) * inverse
            cweight_ref[4, i] = jnp.where(lane < 2, 0.0, below(upper_z, 2) * inverse)
            cweight_ref[5, i] = jnp.where(lane >= depth - 2, 0.0, upper_z * inverse)
        before_x = upper_x

    for number in range(COARSE_STEPS - 1):
        old, new = ((cd0_ref, cd1_ref), (cd1_ref, cd0_ref))[number % 2]
        last = number + 2 == COARSE_STEPS
        skip = 0 if number == 0 else 2
        count = srows if number == 0 else crows - 2 * skip
        inner, here = pl.ds(skip, count), pl.ds(ROW0 + skip, count)
        for i in range(number + 1, cwidth - 1 - number):
            weights = [cweight_ref[f, i, inner, :] for f in range(6)]
            for s in range(2):
                own = old[s, i, here, :]
                beside = weights[0] * old[s, i - 1, here, :] + weights[1] * old[s, i + 1, here, :]
                beside = beside + weights[2] * old[s, i, pl.ds(ROW0 + skip - 1, count), :]
                beside = beside + weights[3] * old[s, i, pl.ds(ROW0 + skip + 1, count), :]
                beside = beside + weights[4] * below(own, 2) + weights[5] * above(own, 2)
                fresh = source_ref[s, i, inner, :] - own + beside
                direction = carried[number] * own + scaled[number] * fresh
                if not last:
                    source_ref[s, i, inner, :] = fresh
                    new[s, i, here, :] = direction
                before = own if number == 0 else correction_ref[s, i, inner, :]
                correction_ref[s, i, inner, :] = before + direction

    edge = COARSE_HALO - COARSE_REACH
    pwidth, prows = ncx + 2 * COARSE_REACH, half + 2 * COARSE_REACH
    prow0 = ROW0 - (2 * COARSE_REACH - HALO)
    even_p = lanes(prows, depth) % 2 == 0
    for i in range(pwidth):
        pair = correction_ref[0, i + edge, pl.ds(edge, prows), :]
        single = correction_ref[1, i + edge, pl.ds(edge, prows), :]
        values = [
            jnp.where(even_p, pair, below(pair)),
            jnp.where(even_p, above(pair), pair),
            single,
        ]
        for c in range(parts):
            prolonged_ref[c, i, pl.ds(prow0, prows, 2), :] = values[c]
            prolonged_ref[c, i, pl.ds(prow0 + 1, prows, 2), :] = values[c]

    fine = pl.ds(ROW0, rows)
    shift = 2 * COARSE_REACH - HALO
    for i in range(width):
        weights = [weight_ref[f, i] for f in range(6)]
        at, before, after = (i + shift) // 2, (i + shift - 1) // 2, (i + shift + 1) // 2
        for c in range(parts):
            own = prolonged_ref[c, at, fine, :]
            beside = weights[0] * prolonged_ref[c, before, fine, :] + weights[1] * prolonged_ref[c, after, fine, :]
            beside = beside + weights[2] * prolonged_ref[c, at, pl.ds(ROW0 - 1, rows), :]
            beside = beside + weights[3] * prolonged_ref[c, at, pl.ds(ROW0 + 1, rows), :]
            beside = beside + weights[4] * below(own) + weights[5] * above(own)
            change_ref[c, i] = beside - own


def post_kernel(
    shape_x,
    shape_y,
    weight_ref, diagonal_ref, smoothed_ref, change_ref, lower_ref, upper_ref, left_ref, right_ref, cross_ref, same_ref,
    out_ref,
    done_ref, sems, residual_ref, base_ref, d0_ref, d1_ref,
):
    parts, nx, ny = smoothed_ref.shape[:3]
    width = nx + 2 * HALO
    at_x, at_y = lax.axis_index("gx"), lax.axis_index("gy")
    has_left, has_right = at_x > 0, at_x < shape_x - 1
    has_low, has_high = at_y > 0, at_y < shape_y - 1
    low_and_high = message_reader(cross_ref, same_ref)
    plan, total = row_plan(nx, HALO)
    for c in range(parts):
        for i, (x, row, count) in enumerate(plan):
            inside = None
            if x < 0:
                own, inside = left_ref[c * HALO + i], has_left
            elif x < nx:
                own = smoothed_ref[c, x]
            else:
                own, inside = right_ref[c * HALO + x - nx], has_right
            low, high = low_and_high(c * total + row, count)
            own, low, high = masked(inside, has_low, has_high, own, low, high)
            own = own + change_ref[c, i, pl.ds(HALO, ny), :]
            if count:
                low = low + change_ref[c, i, pl.ds(HALO - count, count), :]
                high = high + change_ref[c, i, pl.ds(HALO + ny, count), :]
            place(writer(base_ref, c, i), ROW0, ny, HALO, own, low, high)

    piece = nx // OUT_PIECES
    copies = []

    def finish(c, x, value):
        at = x - HALO
        done_ref[c, at] = value * diagonal_ref[at]
        if c == parts - 1 and at % piece == piece - 1:
            here = pl.ds(at + 1 - piece, piece)
            copies.append(pltpu.make_async_copy(done_ref.at[:, here], out_ref.at[:, here], sems.at[len(copies)]))
            copies[-1].start()

    constants = constants_of(lower_ref, upper_ref)
    fine_steps(weight_ref, base_ref, residual_ref, (d0_ref, d1_ref), constants, width, finish)
    for copy in copies:
        copy.wait()


def call(kernel, outs, scratch, specs, out_space=pltpu.VMEM):
    return pl.pallas_call(
        kernel,
        out_shape=[jax.ShapeDtypeStruct(shape, jnp.float32) for shape in outs],
        in_specs=[pl.BlockSpec(memory_space=space) for space in specs],
        out_specs=[pl.BlockSpec(memory_space=out_space) for _ in outs],
        scratch_shapes=[pltpu.VMEM(shape, jnp.float32) if isinstance(shape, tuple) else shape for shape in scratch],
        compiler_params=pltpu.CompilerParams(vmem_limit_bytes=VMEM_LIMIT),
    )


def ring_x(low, high):
    devices = lax.axis_size("gx")
    up = [(i, (i + 1) % devices) for i in range(devices)]
    down = [(j, i) for i, j in up]
    return lax.ppermute(high, "gx", up), lax.ppermute(low, "gx", down)


def swap_y(cross, same):
    devices = lax.axis_size("gy")
    pairs = [(i, i ^ 1) for i in range(devices)]
    others = [(0, 0), (devices - 1, devices - 1)]
    others = others + [(i, ((i + 1) ^ 1) - 1) for i in range(1, devices - 1)]
    return lax.ppermute(cross, "gy", others), lax.ppermute(same, "gy", pairs)


def in_hbm(value):
    return pltpu.with_memory_space_constraint(value, pltpu.HBM)


def up_to(value, unit):
    return -(-value // unit) * unit


def local(forcing, phase_index, visc_table, lower_bound, upper_bound):
    vmem, smem = pltpu.VMEM, pltpu.SMEM
    parts, nx, ny, depth = forcing.shape
    shape_x, shape_y = lax.axis_size("gx"), lax.axis_size("gy")
    width, rows = nx + 2 * HALO, ny + 2 * HALO
    ncx, half = nx // 2, ny // 2
    cwidth, crows = ncx + 2 * COARSE_HALO, half + 2 * COARSE_HALO
    srows = up_to(crows, 8)

    slab = (parts * HALO + VISC_HALO, ny, depth)
    semaphores = pltpu.SemaphoreType.DMA
    table_rows = pltpu.SMEM(visc_table.shape, jnp.float32)
    scratch = [pltpu.VMEM((2, VISC_HALO, ny, depth), jnp.int32), table_rows, semaphores((3, parts + 1))]
    low, high = call(pack_x_kernel, [slab, slab], scratch, [pltpu.HBM] * 3)(
        in_hbm(forcing), in_hbm(phase_index), in_hbm(visc_table)
    )
    left, right = ring_x(low, high)
    scratch = [pltpu.VMEM((nx, ny, depth), jnp.int32), table_rows, semaphores((3,))]
    forcing, viscosity = call(stage_kernel, [forcing.shape, (nx, ny, depth)], scratch, [pltpu.HBM] * 3)(
        in_hbm(forcing), in_hbm(phase_index), in_hbm(visc_table)
    )

    slab = (up_to(parts * row_plan(nx, HALO)[1] + row_plan(nx, VISC_HALO)[1], 8), depth)
    cross, same = call(pack_y_kernel, [slab, slab], [], [vmem] * 4)(forcing, viscosity, left, right)
    cross, same = swap_y(cross, same)

    slab = (3 * COARSE_HALO + COARSE_HALO // 2, half, depth)
    fine_slab = (parts * HALO, ny, depth)
    fine_d = (parts, width, rows + 2 * ROW0, depth)
    weight, diagonal, smoothed, coarse, low, high, fine_low, fine_high = call(
        functools.partial(pre_kernel, shape_x, shape_y),
        [(6, width, rows, depth), (nx, ny, depth), (parts, nx, ny, depth), (4, ncx, half, depth)]
        + [slab, slab, fine_slab, fine_slab],
        [
            (nx + 2 * VISC_HALO, up_to(ny + 2 * VISC_HALO, 8), depth),
            (width, rows, depth),
            (parts, width, rows, depth),
            fine_d,
            fine_d,
            fine_d,
            (rows, depth),
            (6, up_to(ny + 2, 8), depth),
        ],
        [vmem, vmem, smem, smem, vmem, vmem, vmem, vmem],
    )(forcing, viscosity, lower_bound, upper_bound, left, right, cross, same)
    left, right = ring_x(low, high)
    fine_left, fine_right = ring_x(fine_low, fine_high)

    count = 3 * row_plan(ncx, COARSE_HALO)[1] + row_plan(ncx, COARSE_HALO, 2)[1]
    slab = (up_to(count, 8), depth)
    packed, same = call(pack_coarse_kernel, [slab, slab], [], [vmem] * 3)(coarse, left, right)
    cross, same = swap_y(packed, same)
    slab = (up_to(parts * row_plan(nx, HALO)[1], 8), depth)
    fine_cross, fine_same = call(pack_fine_kernel, [slab, slab], [], [vmem] * 4)(
        smoothed, fine_left, fine_right, packed
    )
    fine_cross, fine_same = swap_y(fine_cross, fine_same)

    coarse_d = (2, cwidth, srows + 2 * ROW0, depth)
    (change,) = call(
        functools.partial(coarse_kernel, shape_x, shape_y),
        [(parts, width, rows, depth)],
        [
            (4, cwidth, up_to(ROW0 + crows + 1, 8), depth),
            (6, cwidth, srows, depth),
            (2, cwidth, srows, depth),
            coarse_d,
            coarse_d,
            (2, cwidth, srows, depth),
            (parts, ncx + 2 * COARSE_REACH, rows + 2 * ROW0, depth),
        ],
        [vmem, vmem, smem, smem, vmem, vmem, vmem, vmem],
    )(weight, coarse, lower_bound, upper_bound, left, right, cross, same)

    (out,) = call(
        functools.partial(post_kernel, shape_x, shape_y),
        [(parts, nx, ny, depth)],
        [(parts, nx, ny, depth), pltpu.SemaphoreType.DMA((OUT_PIECES,)), (parts, width, rows, depth), fine_d, fine_d, fine_d],
        [vmem, vmem, vmem, vmem, smem, smem, vmem, vmem, vmem, vmem],
        pltpu.HBM,
    )(weight, diagonal, smoothed, change, lower_bound, upper_bound, fine_left, fine_right, fine_cross, fine_same)
    return out


def solution(mesh):
    in_specs = (P(None, "gx", "gy", None), P("gx", "gy", None), P(), P(), P())
    out_specs = P(None, "gx", "gy", None)
    return jax.shard_map(local, mesh=mesh, in_specs=in_specs, out_specs=out_specs, check_vma=False)
```

```python
import functools

import jax
import jax.numpy as jnp
from jax import lax
from jax.experimental import pallas as pl
from jax.experimental.pallas import tpu as pltpu
from jax.sharding import PartitionSpec as P

CHEB = 4
COARSE_STEPS = 4
OUT_PIECES = 4
HALO = CHEB
VISC_HALO = HALO + 1
COARSE_REACH = (HALO + 2) // 2
COARSE_HALO = COARSE_REACH + COARSE_STEPS - 1
ROW0 = 8
VMEM_LIMIT = 48 * 1024 * 1024


def chebyshev_constants(lower_value, upper_value, count):
    centre = 0.5 * (upper_value + lower_value)
    radius = 0.5 * (upper_value - lower_value)
    spread = centre / radius
    damping = 1.0 / spread
    carried = []
    scaled = []
    for number in range(count - 1):
        renewed = 1.0 / (2.0 * spread - damping)
        carried.append(renewed * damping)
        scaled.append(2.0 * renewed / radius)
        damping = renewed
    return (1.0 / centre, carried, scaled)


def constants_of(lower_ref, upper_ref):
    lower_value = jnp.full((1, 128), lower_ref[0], jnp.float32)
    upper_value = jnp.full((1, 128), upper_ref[0], jnp.float32)
    return chebyshev_constants(lower_value, upper_value, max(CHEB, COARSE_STEPS))


def lookup(table_ref, phases):
    viscosity = jnp.full(phases.shape, table_ref[0], jnp.float32)
    for table_row in range(1, table_ref.shape[0]):
        viscosity = jnp.where(phases == table_row, table_ref[table_row], viscosity)
    return viscosity


def lanes(rows, depth):
    return lax.broadcasted_iota(jnp.int32, (rows, depth), 1)


def below(value, by=1):
    return pltpu.roll(value, by, 1)


def above(value, by=1):
    return pltpu.roll(value, value.shape[1] - by, 1)


def is_odd(axis):
    return lax.rem(lax.axis_index(axis), 2) == 1


def pack_x_kernel(forcing_ref, phase_ref, table_ref, low_ref, high_ref, phases_ref, rows_ref, sems):
    parts, nx = forcing_ref.shape[:2]
    base = parts * HALO
    sides = ((low_ref, 0, 0), (high_ref, nx - HALO, nx - VISC_HALO))
    first_copies, copies = [pltpu.make_async_copy(table_ref, rows_ref, sems.at[2, 0])], []
    for s, (ref, x, visc_x) in enumerate(sides):
        source = phase_ref.at[pl.ds(visc_x, VISC_HALO)]
        first_copies.append(pltpu.make_async_copy(source, phases_ref.at[s], sems.at[s, parts]))
        for c in range(parts):
            source, target = forcing_ref.at[c, pl.ds(x, HALO)], ref.at[pl.ds(c * HALO, HALO)]
            copies.append(pltpu.make_async_copy(source, target, sems.at[s, c]))
    for copy in first_copies + copies:
        copy.start()
    for copy in first_copies:
        copy.wait()
    for s, (ref, _, _) in enumerate(sides):
        for i in range(VISC_HALO):
            ref[base + i] = lookup(rows_ref, phases_ref[s, i])
    for copy in copies:
        copy.wait()


def stage_kernel(forcing_ref, phase_ref, table_ref, here_ref, visc_ref, phases_ref, rows_ref, sems):
    first_copies = [
        pltpu.make_async_copy(table_ref, rows_ref, sems.at[0]),
        pltpu.make_async_copy(phase_ref, phases_ref, sems.at[1]),
    ]
    copy = pltpu.make_async_copy(forcing_ref, here_ref, sems.at[2])
    for each in first_copies + [copy]:
        each.start()
    for each in first_copies:
        each.wait()
    for x in range(phase_ref.shape[0]):
        visc_ref[x] = lookup(rows_ref, phases_ref[x])
    copy.wait()


def row_plan(length, halo, shared=1):
    plan, row = [], 0
    for start in range(-halo, length + halo, shared):
        away = min(max(-x, x - length + 1, 0) for x in range(start, start + shared))
        plan.append((start, row, halo - away))
        row += halo - away
    return plan, row


def place(plane, first, inner, halo, own, low, high):
    count = low.shape[0] if low is not None else 0
    plane(first + halo, own)
    if count:
        plane(first + halo - count, low)
        plane(first + halo + inner, high)
    if count < halo:
        empty = jnp.zeros((halo - count, own.shape[1]), jnp.float32)
        plane(first, empty)
        plane(first + halo + inner + count, empty)


def writer(ref, *at):
    def store(row, value):
        ref[at + (pl.ds(row, value.shape[0]), slice(None))] = value

    return store


def message_reader(cross_ref, same_ref):
    odd = is_odd("gy")

    def low_and_high(row, count):
        if count == 0:
            return None, None
        same, cross = same_ref[pl.ds(row, count), :], cross_ref[pl.ds(row, count), :]
        return jnp.where(odd, same, cross), jnp.where(odd, cross, same)

    return low_and_high


def message_writer(cross_ref, same_ref):
    odd = is_odd("gy")

    def put(row, count, ref, at, ref_high=None, at_high=None):
        if count == 0:
            return
        ref_high, at_high = (ref, at) if ref_high is None else (ref_high, at_high)
        length = ref_high.shape[-2]
        low = ref[at + (pl.ds(0, count), slice(None))]
        high = ref_high[at_high + (pl.ds(length - count, count), slice(None))]
        same_ref[pl.ds(row, count), :] = jnp.where(odd, low, high)
        cross_ref[pl.ds(row, count), :] = jnp.where(odd, high, low)

    return put


def pack_y_kernel(forcing_ref, visc_ref, left_ref, right_ref, cross_ref, same_ref):
    parts, nx = forcing_ref.shape[:2]
    put = message_writer(cross_ref, same_ref)
    plan, total = row_plan(nx, HALO)
    for c in range(parts):
        for x, row, count in plan:
            if x < 0:
                put(c * total + row, count, left_ref, (c * HALO + x + HALO,))
            elif x < nx:
                put(c * total + row, count, forcing_ref, (c, x))
            else:
                put(c * total + row, count, right_ref, (c * HALO + x - nx,))
    for x, row, count in row_plan(nx, VISC_HALO)[0]:
        if x < 0:
            put(parts * total + row, count, left_ref, (parts * HALO + x + VISC_HALO,))
        elif x < nx:
            put(parts * total + row, count, visc_ref, (x,))
        else:
            put(parts * total + row, count, right_ref, (parts * HALO + x - nx,))


def fine_steps(weight_ref, base_ref, residual_ref, d_refs, constants, width, finish):
    first_scale, carried, scaled = constants
    parts, rows = residual_ref.shape[0], residual_ref.shape[2]
    for number in range(CHEB):
        old = base_ref if number == 0 else d_refs[number % 2]
        new = d_refs[(number + 1) % 2]
        last = number + 1 == CHEB
        for x in range(number + 1, width - 1 - number):
            outermost = x in (number + 1, width - 2 - number)
            skip, count = (HALO, rows - 2 * HALO) if last or outermost else (0, rows)
            inner = pl.ds(skip, count)
            weights = [weight_ref[f, x, inner, :] for f in range(6)]
            for c in range(parts):
                own = old[c, x, pl.ds(ROW0 + skip, count), :]
                beside = weights[0] * old[c, x - 1, pl.ds(ROW0 + skip, count), :]
                beside = beside + weights[1] * old[c, x + 1, pl.ds(ROW0 + skip, count), :]
                beside = beside + weights[2] * old[c, x, pl.ds(ROW0 + skip - 1, count), :]
                beside = beside + weights[3] * old[c, x, pl.ds(ROW0 + skip + 1, count), :]
                beside = beside + weights[4] * below(own) + weights[5] * above(own)
                if number == 0:
                    fresh = own - first_scale * (own - beside)
                    own = first_scale * own
                else:
                    fresh = residual_ref[c, x, inner, :] - own + beside
                if last:
                    finish(c, x, fresh)
                else:
                    residual_ref[c, x, inner, :] = fresh
                    new[c, x, pl.ds(ROW0 + skip, count), :] = carried[number] * own + scaled[number] * fresh


def masked(inside, has_low, has_high, own, low, high):
    if inside is not None:
        own = jnp.where(inside, own, 0.0)
        has_low, has_high = jnp.logical_and(has_low, inside), jnp.logical_and(has_high, inside)
    if low is not None:
        low, high = jnp.where(has_low, low, 0.0), jnp.where(has_high, high, 0.0)
    return own, low, high


def pre_kernel(
    shape_x,
    shape_y,
    forcing_ref, own_visc_ref, lower_ref, upper_ref, left_ref, right_ref, cross_ref, same_ref,
    weight_ref, diagonal_ref, smoothed_ref, coarse_ref, low_ref, high_ref, fine_low_ref, fine_high_ref,
    visc_ref, inverse_ref, residual_ref, base_ref, d0_ref, d1_ref, pair_ref, row_ref,
):
    parts, nx, ny, depth = forcing_ref.shape
    width, rows = nx + 2 * HALO, ny + 2 * HALO
    at_x, at_y = lax.axis_index("gx"), lax.axis_index("gy")
    has_left, has_right = at_x > 0, at_x < shape_x - 1
    has_low, has_high = at_y > 0, at_y < shape_y - 1
    low_and_high = message_reader(cross_ref, same_ref)
    fine_plan, fine_total = row_plan(nx, HALO)

    for x, row, count in row_plan(nx, VISC_HALO)[0]:
        if x < 0:
            own = left_ref[parts * HALO + x + VISC_HALO]
            inside = has_left
        elif x < nx:
            own = own_visc_ref[x]
            inside = None
        else:
            own = right_ref[parts * HALO + x - nx]
            inside = has_right
        low, high = low_and_high(parts * fine_total + row, count)
        own, low, high = masked(inside, has_low, has_high, own, low, high)
        place(writer(visc_ref, x + VISC_HALO), 0, ny, VISC_HALO, own, low, high)

    lane = lanes(rows, depth)

    for x in range(width):
        centre = visc_ref[x + 1, pl.ds(1, rows), :]
        halved = 0.5 * centre
        z_below = jnp.where(lane == 0, 0.0, below(halved))
        z_above = jnp.where(lane == depth - 1, 0.0, above(halved))
        faces = [
            halved + 0.5 * visc_ref[x, pl.ds(1, rows), :],
            halved + 0.5 * visc_ref[x + 2, pl.ds(1, rows), :],
            halved + 0.5 * visc_ref[x + 1, pl.ds(0, rows), :],
            halved + 0.5 * visc_ref[x + 1, pl.ds(2, rows), :],
            halved + z_below,
            halved + z_above,
        ]
        diagonal = faces[0] + faces[1] + faces[2] + faces[3] + faces[4] + faces[5]
        inside = centre > 0.0
        inverse = jnp.where(inside, 1.0 / jnp.where(inside, diagonal, 1.0), 0.0)
        for f in range(4):
            weight_ref[f, x] = faces[f] * inverse
        weight_ref[4, x] = jnp.where(lane == 0, 0.0, faces[4] * inverse)
        weight_ref[5, x] = jnp.where(lane == depth - 1, 0.0, faces[5] * inverse)
        inverse_ref[x] = inverse
        if HALO <= x < HALO + nx:
            pair_ref[...] = diagonal
            diagonal_ref[x - HALO] = pair_ref[pl.ds(HALO, ny), :]

    for c in range(parts):
        for x, row, count in fine_plan:
            i = x + HALO
            if x < 0:
                own = left_ref[c * HALO + i]
            elif x < nx:
                own = forcing_ref[c, x]
            else:
                own = right_ref[c * HALO + x - nx]
            low, high = low_and_high(c * fine_total + row, count)
            own = own * inverse_ref[i, pl.ds(HALO, ny), :]
            if count:
                low = low * inverse_ref[i, pl.ds(HALO - count, count), :]
                high = high * inverse_ref[i, pl.ds(HALO + ny, count), :]
            place(writer(base_ref, c, i), ROW0, ny, HALO, own, low, high)

    def finish(c, x, value):
        smoothed_ref[c, x - HALO] = value

    constants = constants_of(lower_ref, upper_ref)
    fine_steps(weight_ref, base_ref, residual_ref, (d0_ref, d1_ref), constants, width, finish)

    half = ny // 2
    even_own = lanes(ny, depth) % 2 == 0
    even_wide = lanes(ny + 2, depth) % 2 == 0
    even = lanes(half, depth) % 2 == 0
    lane_half = lanes(half, depth)

    def z_pair(value, even_mask):
        return value + jnp.where(even_mask, above(value), below(value))

    def y_sum(value, slot):
        row_ref[slot, pl.ds(0, value.shape[0]), :] = value
        return row_ref[slot, pl.ds(0, half, 2), :] + row_ref[slot, pl.ds(1, half, 2), :]

    def visc_own(x):
        return visc_ref[x + VISC_HALO, pl.ds(VISC_HALO, ny), :]

    inverses = []
    for i in range(nx // 2):
        faces_x = []
        for x in (2 * i - 1, 2 * i, 2 * i + 1, 2 * i + 2):
            faces_x.append(y_sum(z_pair(visc_own(x), even_own), 0))
        lower_x = faces_x[0] + faces_x[1]
        upper_x = faces_x[2] + faces_x[3]
        wide = pl.ds(VISC_HALO - 1, ny + 2)
        both = visc_ref[2 * i + VISC_HALO, wide, :] + visc_ref[2 * i + 1 + VISC_HALO, wide, :]
        row_ref[1, pl.ds(0, ny + 2), :] = z_pair(both, even_wide)
        picks = [row_ref[1, pl.ds(start, half, 2), :] for start in range(4)]
        lower_y = picks[0] + picks[1]
        upper_y = picks[2] + picks[3]
        column = y_sum(both[1 : ny + 1], 2)
        lower_z = column + jnp.where(lane_half == 0, 0.0, below(column))
        lower_z = jnp.where(even, lower_z, below(lower_z))
        upper_z = column + jnp.where(lane_half == depth - 1, 0.0, above(column))
        upper_z = jnp.where(even, above(upper_z), upper_z)
        inverse = 1.0 / (lower_x + upper_x + lower_y + upper_y + lower_z + upper_z)
        inverses.append(32.0 * inverse)
        sources = []
        for c in range(parts):
            total = 0.0
            for x in (2 * i, 2 * i + 1):
                total = total + smoothed_ref[c, x] * diagonal_ref[x]
            sources.append(y_sum(z_pair(total, even_own), 3 + c) * (4.0 * inverse))
        faces = [upper_x * (1.0 / 32.0), upper_y * (1.0 / 32.0), upper_z * (1.0 / 32.0)]
        coarse_ref[0, i] = jnp.where(even, sources[0], sources[1])
        coarse_ref[1, i] = jnp.where(even, sources[2], faces[0])
        coarse_ref[2, i] = jnp.where(even, faces[1], faces[2])
        if i % 2 == 1:
            coarse_ref[3, i // 2] = jnp.where(even, inverses[i - 1], inverses[i])

    at = 0
    ncx = nx // 2
    for f in range(4):
        shared = 2 if f == 3 else 1
        count = COARSE_HALO // shared
        for i in range(count):
            low_ref[at] = coarse_ref[f, i]
            high_ref[at] = coarse_ref[f, ncx // shared - count + i]
            at += 1
    for c in range(parts):
        for i in range(HALO):
            fine_low_ref[c * HALO + i] = smoothed_ref[c, i]
            fine_high_ref[c * HALO + i] = smoothed_ref[c, nx - HALO + i]


def coarse_spot(f, i, ncx):
    shared = 2 if f == 3 else 1
    count, own = COARSE_HALO // shared, ncx // shared
    base = f * COARSE_HALO
    if i < count:
        return "left", base + i
    if i < count + own:
        return "own", i - count
    return "right", base + i - count - own


def pack_coarse_kernel(coarse_ref, left_ref, right_ref, cross_ref, same_ref):
    ncx = coarse_ref.shape[1]
    sides = {"left": left_ref, "right": right_ref}
    put = message_writer(cross_ref, same_ref)
    base = 0
    for f in range(4):
        plan, total = row_plan(ncx, COARSE_HALO, 2 if f == 3 else 1)
        for i, (_, row, count) in enumerate(plan):
            side, at = coarse_spot(f, i, ncx)
            if side == "own":
                put(base + row, count, coarse_ref, (f, at))
            else:
                put(base + row, count, sides[side], (at,))
        base += total


def pack_fine_kernel(smoothed_ref, left_ref, right_ref, after_ref, cross_ref, same_ref):
    parts, nx = smoothed_ref.shape[:2]
    put = message_writer(cross_ref, same_ref)
    plan, total = row_plan(nx, HALO)
    for c in range(parts):
        for x, row, count in plan:
            if x < 0:
                put(c * total + row, count, left_ref, (c * HALO + x + HALO,))
            elif x < nx:
                put(c * total + row, count, smoothed_ref, (c, x))
            else:
                put(c * total + row, count, right_ref, (c * HALO + x - nx,))


def coarse_kernel(
    shape_x,
    shape_y,
    weight_ref, coarse_ref, lower_ref, upper_ref, left_ref, right_ref, cross_ref, same_ref,
    change_ref,
    field_ref, cweight_ref, source_ref, cd0_ref, cd1_ref, correction_ref, prolonged_ref,
):
    parts = change_ref.shape[0]
    width, rows = weight_ref.shape[1:3]
    ncx, half, depth = coarse_ref.shape[1:]
    cwidth, crows = ncx + 2 * COARSE_HALO, half + 2 * COARSE_HALO
    srows = source_ref.shape[2]
    at_x, at_y = lax.axis_index("gx"), lax.axis_index("gy")
    has_left, has_right = at_x > 0, at_x < shape_x - 1
    has_low, has_high = at_y > 0, at_y < shape_y - 1
    sides = {"left": left_ref, "right": right_ref}
    insides = {"left": has_left, "own": None, "right": has_right}
    low_and_high = message_reader(cross_ref, same_ref)
    constants = constants_of(lower_ref, upper_ref)
    first_scale, carried, scaled = constants

    base = 0
    tail = field_ref.shape[2] - ROW0 - crows
    for f in range(4):
        shared = 2 if f == 3 else 1
        plan, total = row_plan(ncx, COARSE_HALO, shared)
        for i, (_, row, count) in enumerate(plan):
            side, at = coarse_spot(f, i, ncx)
            own = coarse_ref[f, at] if side == "own" else sides[side][at]
            low, high = low_and_high(base + row, count)
            own, low, high = masked(insides[side], has_low, has_high, own, low, high)
            place(writer(field_ref, f, i), ROW0, half, COARSE_HALO, own, low, high)
            field_ref[f, i, pl.ds(0, ROW0), :] = jnp.zeros((ROW0, depth), jnp.float32)
            field_ref[f, i, pl.ds(ROW0 + crows, tail), :] = jnp.zeros((tail, depth), jnp.float32)
        base += total
    mid = pl.ds(ROW0, srows)
    lane = lanes(srows, depth)
    even = lane % 2 == 0

    def first_of(value):
        return jnp.where(even, value, below(value))

    def second_of(value):
        return jnp.where(even, above(value), value)

    before_x = None
    for i in range(cwidth):
        pair, faces_x = field_ref[0, i, mid, :], field_ref[1, i, mid, :]
        single, upper_x = first_of(faces_x), second_of(faces_x)
        source_ref[0, i] = pair
        source_ref[1, i] = single
        cd0_ref[0, i, mid, :] = first_scale * pair
        cd0_ref[1, i, mid, :] = first_scale * single
        if 0 < i < cwidth - 1:
            packed = field_ref[3, i // 2, mid, :]
            inverse = first_of(packed) if i % 2 == 0 else second_of(packed)
            faces_y = field_ref[2, i, mid, :]
            upper_z = second_of(faces_y)
            cweight_ref[0, i] = before_x * inverse
            cweight_ref[1, i] = upper_x * inverse
            cweight_ref[2, i] = first_of(field_ref[2, i, pl.ds(ROW0 - 1, srows), :]) * inverse
            cweight_ref[3, i] = first_of(faces_y) * inverse
            cweight_ref[4, i] = jnp.where(lane < 2, 0.0, below(upper_z, 2) * inverse)
            cweight_ref[5, i] = jnp.where(lane >= depth - 2, 0.0, upper_z * inverse)
        before_x = upper_x

    for number in range(COARSE_STEPS - 1):
        old, new = ((cd0_ref, cd1_ref), (cd1_ref, cd0_ref))[number % 2]
        last = number + 2 == COARSE_STEPS
        for i in range(number + 1, cwidth - 1 - number):
            outermost = i in (number + 1, cwidth - 2 - number)
            skip = COARSE_HALO if outermost else 0 if number == 0 else 2
            count = srows if skip == 0 else crows - 2 * skip
            inner, here = pl.ds(skip, count), pl.ds(ROW0 + skip, count)
            weights = [cweight_ref[f, i, inner, :] for f in range(6)]
            for s in range(2):
                own = old[s, i, here, :]
                beside = weights[0] * old[s, i - 1, here, :] + weights[1] * old[s, i + 1, here, :]
                beside = beside + weights[2] * old[s, i, pl.ds(ROW0 + skip - 1, count), :]
                beside = beside + weights[3] * old[s, i, pl.ds(ROW0 + skip + 1, count), :]
                beside = beside + weights[4] * below(own, 2) + weights[5] * above(own, 2)
                fresh = source_ref[s, i, inner, :] - own + beside
                direction = carried[number] * own + scaled[number] * fresh
                if not last:
                    source_ref[s, i, inner, :] = fresh
                    new[s, i, here, :] = direction
                before = own if number == 0 else correction_ref[s, i, inner, :]
                correction_ref[s, i, inner, :] = before + direction

    edge = COARSE_HALO - COARSE_REACH
    pwidth, prows = ncx + 2 * COARSE_REACH, half + 2 * COARSE_REACH
    prow0 = ROW0 - (2 * COARSE_REACH - HALO)
    even_p = lanes(prows, depth) % 2 == 0
    for i in range(pwidth):
        pair = correction_ref[0, i + edge, pl.ds(edge, prows), :]
        single = correction_ref[1, i + edge, pl.ds(edge, prows), :]
        values = [
            jnp.where(even_p, pair, below(pair)),
            jnp.where(even_p, above(pair), pair),
            single,
        ]
        for c in range(parts):
            prolonged_ref[c, i, pl.ds(prow0, prows, 2), :] = values[c]
            prolonged_ref[c, i, pl.ds(prow0 + 1, prows, 2), :] = values[c]

    fine = pl.ds(ROW0, rows)
    shift = 2 * COARSE_REACH - HALO
    for i in range(width):
        weights = [weight_ref[f, i] for f in range(6)]
        at, before, after = (i + shift) // 2, (i + shift - 1) // 2, (i + shift + 1) // 2
        for c in range(parts):
            own = prolonged_ref[c, at, fine, :]
            beside = weights[0] * prolonged_ref[c, before, fine, :] + weights[1] * prolonged_ref[c, after, fine, :]
            beside = beside + weights[2] * prolonged_ref[c, at, pl.ds(ROW0 - 1, rows), :]
            beside = beside + weights[3] * prolonged_ref[c, at, pl.ds(ROW0 + 1, rows), :]
            beside = beside + weights[4] * below(own) + weights[5] * above(own)
            change_ref[c, i] = beside - own


def post_kernel(
    shape_x,
    shape_y,
    weight_ref, diagonal_ref, smoothed_ref, change_ref, lower_ref, upper_ref, left_ref, right_ref, cross_ref, same_ref,
    out_ref,
    done_ref, sems, residual_ref, base_ref, d0_ref, d1_ref,
):
    parts, nx, ny = smoothed_ref.shape[:3]
    width = nx + 2 * HALO
    at_x, at_y = lax.axis_index("gx"), lax.axis_index("gy")
    has_left, has_right = at_x > 0, at_x < shape_x - 1
    has_low, has_high = at_y > 0, at_y < shape_y - 1
    low_and_high = message_reader(cross_ref, same_ref)
    plan, total = row_plan(nx, HALO)
    for c in range(parts):
        for i, (x, row, count) in enumerate(plan):
            inside = None
            if x < 0:
                own, inside = left_ref[c * HALO + i], has_left
            elif x < nx:
                own = smoothed_ref[c, x]
            else:
                own, inside = right_ref[c * HALO + x - nx], has_right
            low, high = low_and_high(c * total + row, count)
            own, low, high = masked(inside, has_low, has_high, own, low, high)
            own = own + change_ref[c, i, pl.ds(HALO, ny), :]
            if count:
                low = low + change_ref[c, i, pl.ds(HALO - count, count), :]
                high = high + change_ref[c, i, pl.ds(HALO + ny, count), :]
            place(writer(base_ref, c, i), ROW0, ny, HALO, own, low, high)

    piece = nx // OUT_PIECES
    copies = []

    def finish(c, x, value):
        at = x - HALO
        done_ref[c, at] = value * diagonal_ref[at]
        if c == parts - 1 and at % piece == piece - 1:
            here = pl.ds(at + 1 - piece, piece)
            copies.append(pltpu.make_async_copy(done_ref.at[:, here], out_ref.at[:, here], sems.at[len(copies)]))
            copies[-1].start()

    constants = constants_of(lower_ref, upper_ref)
    fine_steps(weight_ref, base_ref, residual_ref, (d0_ref, d1_ref), constants, width, finish)
    for copy in copies:
        copy.wait()


def call(kernel, outs, scratch, specs, out_space=pltpu.VMEM):
    return pl.pallas_call(
        kernel,
        out_shape=[jax.ShapeDtypeStruct(shape, jnp.float32) for shape in outs],
        in_specs=[pl.BlockSpec(memory_space=space) for space in specs],
        out_specs=[pl.BlockSpec(memory_space=out_space) for _ in outs],
        scratch_shapes=[pltpu.VMEM(shape, jnp.float32) if isinstance(shape, tuple) else shape for shape in scratch],
        compiler_params=pltpu.CompilerParams(vmem_limit_bytes=VMEM_LIMIT),
    )


def ring_x(low, high):
    devices = lax.axis_size("gx")
    up = [(i, (i + 1) % devices) for i in range(devices)]
    down = [(j, i) for i, j in up]
    return lax.ppermute(high, "gx", up), lax.ppermute(low, "gx", down)


def swap_y(cross, same):
    devices = lax.axis_size("gy")
    pairs = [(i, i ^ 1) for i in range(devices)]
    others = [(0, 0), (devices - 1, devices - 1)]
    others = others + [(i, ((i + 1) ^ 1) - 1) for i in range(1, devices - 1)]
    return lax.ppermute(cross, "gy", others), lax.ppermute(same, "gy", pairs)


def in_hbm(value):
    return pltpu.with_memory_space_constraint(value, pltpu.HBM)


def up_to(value, unit):
    return -(-value // unit) * unit


def local(forcing, phase_index, visc_table, lower_bound, upper_bound):
    vmem, smem = pltpu.VMEM, pltpu.SMEM
    parts, nx, ny, depth = forcing.shape
    shape_x, shape_y = lax.axis_size("gx"), lax.axis_size("gy")
    width, rows = nx + 2 * HALO, ny + 2 * HALO
    ncx, half = nx // 2, ny // 2
    cwidth, crows = ncx + 2 * COARSE_HALO, half + 2 * COARSE_HALO
    srows = up_to(crows, 8)

    slab = (parts * HALO + VISC_HALO, ny, depth)
    semaphores = pltpu.SemaphoreType.DMA
    table_rows = pltpu.SMEM(visc_table.shape, jnp.float32)
    scratch = [pltpu.VMEM((2, VISC_HALO, ny, depth), jnp.int32), table_rows, semaphores((3, parts + 1))]
    low, high = call(pack_x_kernel, [slab, slab], scratch, [pltpu.HBM] * 3)(
        in_hbm(forcing), in_hbm(phase_index), in_hbm(visc_table)
    )
    left, right = ring_x(low, high)
    scratch = [pltpu.VMEM((nx, ny, depth), jnp.int32), table_rows, semaphores((3,))]
    forcing, viscosity = call(stage_kernel, [forcing.shape, (nx, ny, depth)], scratch, [pltpu.HBM] * 3)(
        in_hbm(forcing), in_hbm(phase_index), in_hbm(visc_table)
    )

    slab = (up_to(parts * row_plan(nx, HALO)[1] + row_plan(nx, VISC_HALO)[1], 8), depth)
    cross, same = call(pack_y_kernel, [slab, slab], [], [vmem] * 4)(forcing, viscosity, left, right)
    cross, same = swap_y(cross, same)

    slab = (3 * COARSE_HALO + COARSE_HALO // 2, half, depth)
    fine_slab = (parts * HALO, ny, depth)
    fine_d = (parts, width, rows + 2 * ROW0, depth)
    weight, diagonal, smoothed, coarse, low, high, fine_low, fine_high = call(
        functools.partial(pre_kernel, shape_x, shape_y),
        [(6, width, rows, depth), (nx, ny, depth), (parts, nx, ny, depth), (4, ncx, half, depth)]
        + [slab, slab, fine_slab, fine_slab],
        [
            (nx + 2 * VISC_HALO, up_to(ny + 2 * VISC_HALO, 8), depth),
            (width, rows, depth),
            (parts, width, rows, depth),
            fine_d,
            fine_d,
            fine_d,
            (rows, depth),
            (6, up_to(ny + 2, 8), depth),
        ],
        [vmem, vmem, smem, smem, vmem, vmem, vmem, vmem],
    )(forcing, viscosity, lower_bound, upper_bound, left, right, cross, same)
    left, right = ring_x(low, high)
    fine_left, fine_right = ring_x(fine_low, fine_high)

    count = 3 * row_plan(ncx, COARSE_HALO)[1] + row_plan(ncx, COARSE_HALO, 2)[1]
    slab = (up_to(count, 8), depth)
    packed, same = call(pack_coarse_kernel, [slab, slab], [], [vmem] * 3)(coarse, left, right)
    cross, same = swap_y(packed, same)
    slab = (up_to(parts * row_plan(nx, HALO)[1], 8), depth)
    fine_cross, fine_same = call(pack_fine_kernel, [slab, slab], [], [vmem] * 4)(
        smoothed, fine_left, fine_right, packed
    )
    fine_cross, fine_same = swap_y(fine_cross, fine_same)

    coarse_d = (2, cwidth, srows + 2 * ROW0, depth)
    (change,) = call(
        functools.partial(coarse_kernel, shape_x, shape_y),
        [(parts, width, rows, depth)],
        [
            (4, cwidth, up_to(ROW0 + crows + 1, 8), depth),
            (6, cwidth, srows, depth),
            (2, cwidth, srows, depth),
            coarse_d,
            coarse_d,
            (2, cwidth, srows, depth),
            (parts, ncx + 2 * COARSE_REACH, rows + 2 * ROW0, depth),
        ],
        [vmem, vmem, smem, smem, vmem, vmem, vmem, vmem],
    )(weight, coarse, lower_bound, upper_bound, left, right, cross, same)

    (out,) = call(
        functools.partial(post_kernel, shape_x, shape_y),
        [(parts, nx, ny, depth)],
        [(parts, nx, ny, depth), pltpu.SemaphoreType.DMA((OUT_PIECES,)), (parts, width, rows, depth), fine_d, fine_d, fine_d],
        [vmem, vmem, vmem, vmem, smem, smem, vmem, vmem, vmem, vmem],
        pltpu.HBM,
    )(weight, diagonal, smoothed, change, lower_bound, upper_bound, fine_left, fine_right, fine_cross, fine_same)
    return out


def solution(mesh):
    in_specs = (P(None, "gx", "gy", None), P("gx", "gy", None), P(), P(), P())
    out_specs = P(None, "gx", "gy", None)
    return jax.shard_map(local, mesh=mesh, in_specs=in_specs, out_specs=out_specs, check_vma=False)
```
